128 devices in a mesh: energy: 16 (over y, x_hi, core), layer: 8 (over x_lo, z).
Axes of the slice: x: 4 (x_hi: 2, x_lo: 2; x = x_hi * 2 + x_lo), y: 4, z: 4, core: 2. Of those that a mesh axis runs over, the one named last changes fastest.
Arguments:
- green_blocks: bfloat16 [64, 8, 2, 384, 384], P('energy', 'layer'), may hold values from -6 to 6
- offsets: int32 [4], replicated, may hold values from -4 to 4, as said below
- occupation: float32 [4], replicated, may hold values from 0.1 to 2
- coupling: int32 [8, 4], P('layer'), may hold values from 0 to 3
- vertex: bfloat16 [4, 2, 384, 384], replicated, may hold values from -0.15625 to 0.15625
- magnon_free: bfloat16 [4, 2, 384, 384], replicated, may hold values from -0.0034179688 to 0.0034179688
Outputs:
- sigma: bfloat16 [64, 8, 2, 384, 384], P('energy', 'layer')
The draws below stay inside these ranges and needn't reach their ends.
Inputs may be any that keep to these rules, and one draw needn't show every extreme that they name: `offsets`: each offset is a nonzero whole number; one equals 4 and one equals -4.
All inputs are finite; a program needn't handle non-finite values.
Results may differ from the reference program's by a relative error of at most 0.0056.
Values may be sent and summed in bfloat16 or wider, within the bound.
No kernel may reach another device: no remote copies, remote signals or barrier semaphores. Data moves between devices by JAX's collectives and lax.ppermute only.
A program may use at most 192 MiB of HBM per device.

```python
import math
import jax
import jax.numpy as jnp
from jax import lax

NB = 384
NOFF = 4
NV = 4
E_DEV = 4
NE = 64
GROUPS = 8


def draw_offsets(key, part):
    first_key, second_key = jax.random.split(jax.random.fold_in(key, 11))
    raw = jax.random.randint(first_key, (NOFF - 2,), 0, 2 * E_DEV, dtype=jnp.int32)
    others = jnp.where(raw < E_DEV, raw - E_DEV, raw - E_DEV + 1).astype(jnp.int32)
    values = jnp.concatenate([jnp.array([E_DEV, -E_DEV], jnp.int32), others])
    order = jax.random.permutation(second_key, NOFF)
    return values[order].astype(jnp.int32)


def set_ends(result, own_key, low, high):
    shape = result.shape
    spot = [jax.random.randint(jax.random.fold_in(own_key, axis), (), 0, shape[axis]) for axis in range(len(shape))]
    result = result.at[tuple(spot)].set(low)
    longest = shape.index(max(shape))
    spot[longest] = (spot[longest] + 1) % shape[longest]
    return result.at[tuple(spot)].set(high)


def shard_levels(key, shape, cuts, low, top_value):
    gain = 1.0
    for axis_at, blocks in cuts:
        heights = jax.random.uniform(jax.random.fold_in(jax.random.fold_in(key, 6), axis_at), (blocks,), jnp.float32, low / len(cuts), top_value / len(cuts))
        gain = gain * jnp.repeat(jnp.exp(heights), shape[axis_at] // blocks).reshape((-1,) + (1,) * (len(shape) - 1 - axis_at))
    return gain


def normal_values(stream_key, extent, width, reach, shards=(), kind=jnp.bfloat16):
    drawn = jax.random.normal(stream_key, extent, jnp.float32) * width
    if len(shards) > 0:
        drawn = shard_levels(stream_key, extent, shards, -0.22, 0.18) * drawn
    return jnp.clip(drawn, min=-reach, max=reach).astype(kind)


def setup_inputs(seed: int = 0) -> dict:
    seeds = jax.random.split(jax.random.key(seed), 7)
    green_blocks = normal_values(seeds[0], (NE, GROUPS, 2, NB, NB), 1.0, 6.0, ((0, 16), (1, 8)))
    offsets = draw_offsets(jax.random.fold_in(seeds[6], 71), 0)
    occupation = jnp.clip(jnp.exp(jax.random.uniform(seeds[2], (NOFF,), jnp.float32, math.log(0.1), math.log(2.0))), 0.1, 2.0)
    coupling = set_ends(jax.random.randint(seeds[3], (GROUPS, NOFF), 0, NV), jax.random.fold_in(seeds[3], 1), 0, NV - 1).astype(jnp.int32)
    vertex = normal_values(seeds[4], (NV, 2, NB, NB), (4 * NB) ** -0.5, 0.15625)
    magnon_free = normal_values(seeds[5], (NOFF, 2, NB, NB), (16 * NB * NE * GROUPS) ** -0.5, 0.0034179688)
    return dict(green_blocks=green_blocks, offsets=offsets, occupation=occupation, coupling=coupling, vertex=vertex, magnon_free=magnon_free)


def complex_product(pattern, left_real, left_imag, right_real, right_imag):
    def product(first, second):
        return jnp.einsum(pattern, first.astype(jnp.float32), second.astype(jnp.float32))
    return (product(left_real, right_real) - product(left_imag, right_imag),
            product(left_real, right_imag) + product(left_imag, right_real))


def reference(green_blocks, offsets, occupation, coupling, vertex, magnon_free):
    margin = jnp.zeros((E_DEV,) + green_blocks.shape[1:], green_blocks.dtype)
    padded = jnp.concatenate([margin, green_blocks, margin], axis=0)
    chosen = vertex[coupling]
    weights = occupation[:, None, None, None, None]

    def partners(energy):
        below = jnp.take(padded, energy + E_DEV - offsets, axis=0)
        above = jnp.take(padded, energy + E_DEV + offsets, axis=0)
        return below.astype(jnp.float32), above.astype(jnp.float32)

    def accumulate(carry, energy):
        below, above = partners(energy)
        own = green_blocks[energy].astype(jnp.float32)
        flipped = jnp.swapaxes(above, -1, -2)
        real_part = jnp.sum(own[None, :, 0] * flipped[:, :, 0] - own[None, :, 1] * flipped[:, :, 1], axis=1)
        imag_part = jnp.sum(own[None, :, 0] * flipped[:, :, 1] + own[None, :, 1] * flipped[:, :, 0], axis=1)
        return carry + jnp.stack([real_part, imag_part], axis=1), None

    energies = jnp.arange(NE, dtype=jnp.int32)
    start = jnp.zeros((NOFF, 2, NB, NB), jnp.float32)
    polar, _ = lax.scan(accumulate, start, energies)
    polar = lax.optimization_barrier(polar.astype(jnp.bfloat16))
    magnon_real, magnon_imag = complex_product("kab,kbc->kac", polar[:, 0], polar[:, 1],
                                               magnon_free[:, 0], magnon_free[:, 1])
    magnon = lax.optimization_barrier(jnp.stack([magnon_real, magnon_imag], axis=1).astype(jnp.bfloat16))
    magnon = magnon.astype(jnp.float32)

    def sigma_at(energy):
        below, above = partners(energy)
        mixed = (weights * below + (weights + 1.0) * above).astype(jnp.bfloat16)
        mixed = lax.optimization_barrier(mixed)
        half_real, half_imag = complex_product("gkab,kgbc->kgac", chosen[:, :, 0], chosen[:, :, 1],
                                               mixed[:, :, 0], mixed[:, :, 1])
        half_real = lax.optimization_barrier(half_real.astype(jnp.bfloat16))
        half_imag = lax.optimization_barrier(half_imag.astype(jnp.bfloat16))
        born_real, born_imag = complex_product("kgab,gkcb->gac", half_real, half_imag,
                                               chosen[:, :, 0], -chosen[:, :, 1])
        summed = below + above
        hadamard_real = jnp.sum(magnon[:, 0][:, None] * summed[:, :, 0] - magnon[:, 1][:, None] * summed[:, :, 1], axis=0)
        hadamard_imag = jnp.sum(magnon[:, 0][:, None] * summed[:, :, 1] + magnon[:, 1][:, None] * summed[:, :, 0], axis=0)
        return jnp.stack([born_real + hadamard_real, born_imag + hadamard_imag], axis=1).astype(jnp.bfloat16)

    return lax.map(sigma_at, energies)
```

```python
import jax
import jax.numpy as jnp
from jax import lax
from jax.experimental import pallas as pl
from jax.experimental.pallas import tpu as pltpu
from jax.sharding import Mesh
from jax.sharding import PartitionSpec as P


NB = 384
HALF = NB // 2
BANDS = 64
ROWS = 56
FLAT = BANDS * ROWS
F32 = jnp.float32
BF16 = jnp.bfloat16
SWAP = [(0, 1), (1, 0)]
OTHERS = ("y", "xh", "xl", "z")
ENERGY = ("y", "xh", "core")
LAYER = ("xl", "z")
ANY = pl.BlockSpec(memory_space=pl.ANY)
SMEM = pl.BlockSpec(memory_space=pltpu.SMEM)


def first_index(offsets, value):
    return jnp.where(
        offsets[0] == value, 0, jnp.where(offsets[1] == value, 1, jnp.where(offsets[2] == value, 2, 3))
    )


def offset_roles(offsets):
    top = first_index(offsets, 4)
    bottom = first_index(offsets, -4)
    low = jnp.minimum(top, bottom)
    high = jnp.maximum(top, bottom)
    first = jnp.where(low != 0, 0, jnp.where(high != 1, 1, 2))
    last = jnp.where(high != 3, 3, jnp.where(low != 2, 2, 1))
    return top, bottom, first, last


def spans(offsets, first, last):
    return (jnp.int32(4), jnp.abs(offsets[first]), jnp.abs(offsets[last]))


def polar_body(place, offsets, own, mate, near, send, keep, slots, turned, sems):
    core = place[0]
    copies = [
        pltpu.make_async_copy(own, slots.at[pl.ds(2, 4)], sems.at[0]),
        pltpu.make_async_copy(
            mate.at[pl.ds(2 * core, 2)], slots.at[pl.ds(6 - 6 * core, 2)], sems.at[1]
        ),
        pltpu.make_async_copy(near, slots.at[pl.ds(6 * core, 2)], sems.at[2]),
    ]
    for copy in copies:
        copy.start()
    for copy in copies:
        copy.wait()

    @pl.loop(0, 10)
    def _(step):
        slot = step // 2
        part = step % 2
        turned[slot, part] = slots[slot + 3, part].astype(F32).T

    _, _, first, last = offset_roles(offsets)
    for index, span in enumerate(spans(offsets, first, last)):
        base = jnp.clip(4 - span, 0, 2)
        for target, half in ((send, 1 - core), (keep, core)):

            @pl.loop(0, HALF // 16)
            def _(block):
                rows = pl.ds(pl.multiple_of(half * HALF + block * 16, 16), 16)
                real = jnp.zeros((16, NB), F32)
                imag = jnp.zeros((16, NB), F32)
                for step in range(4):
                    left = base + step
                    right = left + span - 3
                    ar = slots[left, 0, rows, :].astype(F32)
                    ai = slots[left, 1, rows, :].astype(F32)
                    br = turned[right, 0, rows, :]
                    bi = turned[right, 1, rows, :]
                    real += ar * br - ai * bi
                    imag += ar * bi + ai * br
                for part, value in enumerate((real, imag)):
                    for panel in range(3):
                        start = ((index * 2 + part) * 3 + panel) * HALF
                        target[pl.ds(pl.multiple_of(start + block * 16, 16), 16), :] = value[
                            :, panel * 128 : (panel + 1) * 128
                        ].astype(target.dtype)

    tail = pl.ds(18 * HALF, FLAT - 18 * HALF)
    send[tail, :] = jnp.zeros((FLAT - 18 * HALF, 128), BF16)
    keep[tail, :] = jnp.zeros((FLAT - 18 * HALF, 128), F32)


def polar_call(place, offsets, own, mate, near):
    return pl.pallas_call(
        polar_body,
        out_shape=(
            jax.ShapeDtypeStruct((FLAT, 128), BF16),
            jax.ShapeDtypeStruct((FLAT, 128), F32),
        ),
        in_specs=[SMEM, SMEM, ANY, ANY, ANY],
        out_specs=(
            pl.BlockSpec(memory_space=pltpu.VMEM),
            pl.BlockSpec(memory_space=pltpu.VMEM),
        ),
        scratch_shapes=[
            pltpu.VMEM((8, 2, NB, NB), BF16),
            pltpu.VMEM((5, 2, NB, NB), F32),
            pltpu.SemaphoreType.DMA((3,)),
        ],
        compiler_params=pltpu.CompilerParams(vmem_limit_bytes=24 << 20),
        cost_estimate=pl.CostEstimate(flops=20_000_000, bytes_accessed=9_000_000, transcendentals=0),
        name="polar",
    )(place, offsets, own, mate, near)


def window_copies(core, own, mate, near, far, slots, sems):
    copies = [
        pltpu.make_async_copy(own, slots.at[pl.ds(4, 4)], sems.at[0]),
        pltpu.make_async_copy(mate, slots.at[pl.ds(8 - 8 * core, 4)], sems.at[1]),
        pltpu.make_async_copy(near, slots.at[pl.ds(2 + 6 * core, 2)], sems.at[2]),
    ]
    if far is not None:
        copies.append(pltpu.make_async_copy(far, slots.at[pl.ds(10 * core, 2)], sems.at[3]))
    return copies


def born_body(early, *refs):
    if early:
        (place, offsets, occupation, coupling, own, mate, near, vertex, out, *rest) = refs
        far = None
    else:
        (place, offsets, occupation, coupling, own, mate, near, far, vertex, out, *rest) = refs
    slots, mixed, wide, stack, side, total, sems = rest
    core = place[0]
    copies = window_copies(core, own, mate, near, far, slots, sems)
    for copy in copies:
        copy.start()
    for copy in copies:
        copy.wait()
    energy = 2 * (1 - core) if early else 2 * core

    @pl.loop(0, 4)
    def _(k):
        which = coupling[0, k]
        vr = vertex[which, 0]
        vi = vertex[which, 1]
        wide[:NB, :NB] = vr
        wide[:NB, NB:] = -vi
        wide[NB:, :NB] = vi
        wide[NB:, NB:] = vr
        side[:NB, :NB] = vr
        side[:NB, NB:] = vi
        side[NB:, :NB] = -vi
        side[NB:, NB:] = vr
        span = offsets[k]
        weight = occupation[k]
        for item in range(2):
            at = energy + 4 + item
            for part in range(2):
                low = slots[at - span, part].astype(F32)
                high = slots[at + span, part].astype(F32)
                value = weight * low + (weight + 1.0) * high
                mixed[part * NB : (part + 1) * NB, item * NB : (item + 1) * NB] = value.astype(BF16)
        half = jnp.dot(wide[...], mixed[...], preferred_element_type=F32).astype(BF16)
        for item in range(2):
            for part in range(2):
                stack[item * NB : (item + 1) * NB, part * NB : (part + 1) * NB] = half[
                    part * NB : (part + 1) * NB, item * NB : (item + 1) * NB
                ]
        term = lax.dot_general(
            stack[...], side[...], (((1,), (1,)), ((), ())), preferred_element_type=F32
        )

        @pl.when(k == 0)
        def _():
            total[...] = term

        @pl.when(k > 0)
        def _():
            total[...] += term

    out[...] = total[...]


def born_call(early, place, offsets, occupation, coupling, arrays, vertex):
    size = 2 * NB
    return pl.pallas_call(
        lambda *refs: born_body(early, *refs),
        out_shape=jax.ShapeDtypeStruct((size, size), F32),
        in_specs=[SMEM] * 4 + [ANY] * len(arrays) + [pl.BlockSpec(memory_space=pltpu.VMEM)],
        out_specs=pl.BlockSpec(memory_space=pltpu.VMEM),
        scratch_shapes=[
            pltpu.VMEM((12, 2, NB, NB), BF16),
            pltpu.VMEM((size, size), BF16),
            pltpu.VMEM((size, size), BF16),
            pltpu.VMEM((size, size), BF16),
            pltpu.VMEM((size, size), BF16),
            pltpu.VMEM((size, size), F32),
            pltpu.SemaphoreType.DMA((4,)),
        ],
        compiler_params=pltpu.CompilerParams(vmem_limit_bytes=32 << 20),
        cost_estimate=pl.CostEstimate(
            flops=16 * size**3, bytes_accessed=12_000_000, transcendentals=0
        ),
        name="born_early" if early else "born_late",
    )(place, offsets, occupation, coupling, *arrays, vertex)


def final_body(
    place, offsets, mine, other, free, own, mate, near, far, early, late, out,
    slots, joined, flipped, table, magnon, sems,
):
    core = place[0]
    copies = window_copies(core, own, mate, near, far, slots, sems)
    for copy in copies:
        copy.start()
    for source, half in ((mine, core), (other, 1 - core)):
        rows = pl.ds(pl.multiple_of(half * HALF, HALF), HALF)
        for index in range(3):
            for part in range(2):
                for panel in range(3):
                    start = ((index * 2 + part) * 3 + panel) * HALF
                    joined[index, rows, part * NB + panel * 128 : part * NB + (panel + 1) * 128] = source[
                        start : start + HALF, :
                    ]

    def turn(index, target):
        for part in range(2):
            columns = slice(part * NB, (part + 1) * NB)
            target[:, columns] = joined[index, :, columns].astype(F32).T.astype(BF16)

    def product(left, k):
        fr = free[k, 0]
        fi = free[k, 1]
        table[:NB, :NB] = fr
        table[:NB, NB:] = fi
        table[NB:, :NB] = -fi
        table[NB:, NB:] = fr
        value = jnp.dot(left[...], table[...], preferred_element_type=F32)
        return value.astype(BF16).astype(F32)

    top, bottom, first, last = offset_roles(offsets)
    turn(0, flipped)
    magnon[0] = product(joined.at[0], top)
    magnon[0] += product(flipped, bottom)
    for index, k in ((1, first), (2, last)):

        @pl.when(offsets[k] < 0)
        def _():
            turn(index, flipped)

        @pl.when(offsets[k] > 0)
        def _():
            flipped[...] = joined[index]

        magnon[index] = product(flipped, k)

    for copy in copies:
        copy.wait()
    reach = spans(offsets, first, last)
    for source, energy in ((early, 2 * (1 - core)), (late, 2 * core)):
        for item in range(2):

            @pl.loop(0, NB // 16)
            def _(block):
                rows = pl.ds(pl.multiple_of(block * 16, 16), 16)
                begin = pl.ds(pl.multiple_of(item * NB + block * 16, 16), 16)
                real = source[begin, :NB]
                imag = source[begin, NB:]
                at = energy + 4 + item
                for index in range(3):
                    down = at - reach[index]
                    up = at + reach[index]
                    sr = slots[down, 0, rows, :].astype(F32) + slots[up, 0, rows, :].astype(F32)
                    si = slots[down, 1, rows, :].astype(F32) + slots[up, 1, rows, :].astype(F32)
                    mr = magnon[index, rows, :NB]
                    mi = magnon[index, rows, NB:]
                    real += mr * sr - mi * si
                    imag += mr * si + mi * sr
                out[energy + item, 0, 0, rows, :] = real.astype(BF16)
                out[energy + item, 0, 1, rows, :] = imag.astype(BF16)


def final_call(place, offsets, mine, other, free, own, mate, near, far, early, late):
    vmem = pl.BlockSpec(memory_space=pltpu.VMEM)
    return pl.pallas_call(
        final_body,
        out_shape=jax.ShapeDtypeStruct((4, 1, 2, NB, NB), BF16),
        in_specs=[SMEM, SMEM, vmem, vmem, vmem, ANY, ANY, ANY, ANY, vmem, vmem],
        out_specs=vmem,
        scratch_shapes=[
            pltpu.VMEM((12, 2, NB, NB), BF16),
            pltpu.VMEM((3, NB, 2 * NB), BF16),
            pltpu.VMEM((NB, 2 * NB), BF16),
            pltpu.VMEM((2 * NB, 2 * NB), BF16),
            pltpu.VMEM((3, NB, 2 * NB), F32),
            pltpu.SemaphoreType.DMA((4,)),
        ],
        compiler_params=pltpu.CompilerParams(vmem_limit_bytes=40 << 20),
        cost_estimate=pl.CostEstimate(
            flops=2_000_000_000, bytes_accessed=18_000_000, transcendentals=0
        ),
        name="final",
    )(place, offsets, mine, other, free, own, mate, near, far, early, late)


def per_device(green_blocks, offsets, occupation, coupling, vertex, magnon_free):
    count = lax.axis_size(ENERGY)
    core = lax.axis_index("core").astype(jnp.int32)
    place = core[None]
    own = green_blocks.reshape(4, 2, NB, NB)
    across = [(i, i + 1) for i in range(1, count - 1, 2)]
    across += [(target, source) for source, target in across]
    near = lax.ppermute(lax.dynamic_slice_in_dim(own, 2 * core, 2, 0), ENERGY, across)
    mate = lax.ppermute(own, "core", SWAP)
    far = lax.ppermute(lax.dynamic_slice_in_dim(own, 2 - 2 * core, 2, 0), ENERGY, across)
    send, keep = polar_call(place, offsets, own, mate, near)
    pair = keep + lax.ppermute(send, "core", SWAP).astype(F32)
    bands = lax.all_to_all(pair.astype(BF16).reshape(BANDS, ROWS, 128), OTHERS, 0, 0, tiled=True)
    polar = jnp.sum(bands.astype(F32), axis=0).astype(BF16)
    early = born_call(True, place, offsets, occupation, coupling, (own, mate, near), vertex)
    mine = lax.all_to_all(
        jnp.broadcast_to(polar[None], (BANDS, ROWS, 128)), OTHERS, 0, 0, tiled=True
    ).reshape(FLAT, 128)
    late = born_call(False, place, offsets, occupation, coupling, (own, mate, near, far), vertex)
    other = lax.ppermute(mine, "core", SWAP)
    return final_call(place, offsets, mine, other, magnon_free, own, mate, near, far, early, late)


def solution(mesh):
    fine = Mesh(mesh.devices.reshape(4, 2, 2, 2, 4), ("y", "xh", "core", "xl", "z"))
    blocks = P(ENERGY, LAYER, None, None, None)
    placed = (blocks, P(), P(), P(LAYER, None), P(), P())
    return jax.shard_map(
        per_device, mesh=fine, in_specs=placed, out_specs=blocks, check_vma=False
    )
```

```python
import jax
import jax.numpy as jnp
from jax import lax
from jax.experimental import pallas as pl
from jax.experimental.pallas import tpu as pltpu
from jax.sharding import Mesh
from jax.sharding import PartitionSpec as P


NB = 384
HALF = NB // 2
BANDS = 64
ROWS = 56
FLAT = BANDS * ROWS
FULL = 60 << 20
F32 = jnp.float32
BF16 = jnp.bfloat16
SWAP = [(0, 1), (1, 0)]
OTHERS = ("y", "xh", "xl", "z")
ENERGY = ("y", "xh", "core")
LAYER = ("xl", "z")
ANY = pl.BlockSpec(memory_space=pl.ANY)
SMEM = pl.BlockSpec(memory_space=pltpu.SMEM)
VMEM = pl.BlockSpec(memory_space=pltpu.VMEM)


def first_index(offsets, value):
    return jnp.where(
        offsets[0] == value, 0, jnp.where(offsets[1] == value, 1, jnp.where(offsets[2] == value, 2, 3))
    )


def offset_roles(offsets):
    top = first_index(offsets, 4)
    bottom = first_index(offsets, -4)
    low = jnp.minimum(top, bottom)
    high = jnp.maximum(top, bottom)
    first = jnp.where(low != 0, 0, jnp.where(high != 1, 1, 2))
    last = jnp.where(high != 3, 3, jnp.where(low != 2, 2, 1))
    return top, bottom, first, last


def spans(offsets, first, last):
    return (jnp.int32(4), jnp.abs(offsets[first]), jnp.abs(offsets[last]))


def cut_body(place, base, sign, own, out, sem):
    copy = pltpu.make_async_copy(own.at[pl.ds(base + sign * place[0], 2)], out, sem)
    copy.start()
    copy.wait()


def cut_call(place, own, base, sign):
    return pl.pallas_call(
        lambda place, own, out, sem: cut_body(place, base, sign, own, out, sem),
        out_shape=jax.ShapeDtypeStruct((2, 2, NB, NB), BF16),
        in_specs=[SMEM, ANY],
        out_specs=VMEM,
        scratch_shapes=[pltpu.SemaphoreType.DMA],
        compiler_params=pltpu.CompilerParams(vmem_limit_bytes=4 << 20),
        cost_estimate=pl.CostEstimate(flops=0, bytes_accessed=2_400_000, transcendentals=0),
    )(place, own)


def polar_pairs(core, near, slots, turned, offsets, each):
    _, _, first, last = offset_roles(offsets)
    for index, span in enumerate(spans(offsets, first, last)):
        base = jnp.clip(4 - span, 0, 2)
        split = jnp.where(core == 0, jnp.maximum(base, 2), jnp.maximum(base, 6 - span))
        outer = (core == 0) == near
        begin = jnp.where(outer, base, split)
        end = jnp.where(outer, split, base + 4)
        if index == 0:
            back = jnp.bool_(False)
        else:
            back = offsets[first if index == 1 else last] < 0
        plain = jnp.where(back, span, 0)
        cross = jnp.where(back, 0, span)

        def block_sum(rows, real, imag):
            def step(s, carry):
                real, imag = carry
                ar = slots[s + plain + 2, 0, rows, :].astype(F32)
                ai = slots[s + plain + 2, 1, rows, :].astype(F32)
                br = turned[s + cross, 0, rows, :]
                bi = turned[s + cross, 1, rows, :]
                return real + (ar * br - ai * bi), imag + (ar * bi + ai * br)

            return lax.fori_loop(begin, end, step, (real, imag))

        each(index, block_sum)


def prepare_body(place, offsets, own, mate, slots, turned, partial, sems):
    core = place[0]
    copies = [
        pltpu.make_async_copy(own, slots.at[pl.ds(4, 4)], sems.at[0]),
        pltpu.make_async_copy(mate, slots.at[pl.ds(8 - 8 * core, 4)], sems.at[1]),
    ]
    for copy in copies:
        copy.start()
    for copy in copies:
        copy.wait()

    @pl.loop(0, 12)
    def _(step):
        slot = step // 2 + 2 - 2 * core
        part = step % 2
        turned[slot, part] = slots[slot + 2, part].astype(F32).T

    def each(index, block_sum):
        @pl.loop(0, NB // 16)
        def _(block):
            rows = pl.ds(pl.multiple_of(block * 16, 16), 16)
            zero = jnp.zeros((16, NB), F32)
            real, imag = block_sum(rows, zero, zero)
            partial[index, 0, rows, :] = real
            partial[index, 1, rows, :] = imag

    polar_pairs(core, False, slots, turned, offsets, each)


def prepare_call(place, offsets, own, mate):
    return pl.pallas_call(
        prepare_body,
        out_shape=(
            jax.ShapeDtypeStruct((12, 2, NB, NB), BF16),
            jax.ShapeDtypeStruct((8, 2, NB, NB), F32),
            jax.ShapeDtypeStruct((3, 2, NB, NB), F32),
        ),
        in_specs=[SMEM, SMEM, ANY, ANY],
        out_specs=(VMEM, VMEM, VMEM),
        scratch_shapes=[pltpu.SemaphoreType.DMA((2,))],
        compiler_params=pltpu.CompilerParams(vmem_limit_bytes=4 << 20),
        cost_estimate=pl.CostEstimate(flops=20_000_000, bytes_accessed=9_000_000, transcendentals=0),
        name="prepare",
    )(place, offsets, own, mate)


def polar_body(place, offsets, near, slots_in, turned_in, partial, slots, turned, send, keep, sem):
    core = place[0]
    copy = pltpu.make_async_copy(near, slots.at[pl.ds(2 + 6 * core, 2)], sem)
    copy.start()
    copy.wait()
    for item in range(2):
        slot = 6 * core + item
        for part in range(2):
            turned[slot, part] = slots[slot + 2, part].astype(F32).T

    def each(index, block_sum):
        for target, half in ((send, 1 - core), (keep, core)):

            @pl.loop(0, HALF // 16)
            def _(block):
                rows = pl.ds(pl.multiple_of(half * HALF + block * 16, 16), 16)
                pair = block_sum(rows, partial[index, 0, rows, :], partial[index, 1, rows, :])
                for part, value in enumerate(pair):
                    for panel in range(3):
                        start = ((index * 2 + part) * 3 + panel) * HALF
                        target[pl.ds(pl.multiple_of(start + block * 16, 16), 16), :] = value[
                            :, panel * 128 : (panel + 1) * 128
                        ].astype(target.dtype)

    polar_pairs(core, True, slots, turned, offsets, each)
    tail = pl.ds(18 * HALF, FLAT - 18 * HALF)
    send[tail, :] = jnp.zeros((FLAT - 18 * HALF, 128), BF16)
    keep[tail, :] = jnp.zeros((FLAT - 18 * HALF, 128), F32)


def polar_call(place, offsets, near, slots, turned, partial):
    return pl.pallas_call(
        polar_body,
        out_shape=(
            jax.ShapeDtypeStruct(slots.shape, BF16),
            jax.ShapeDtypeStruct(turned.shape, F32),
            jax.ShapeDtypeStruct((FLAT, 128), BF16),
            jax.ShapeDtypeStruct((FLAT, 128), F32),
        ),
        in_specs=[SMEM, SMEM, ANY, VMEM, VMEM, VMEM],
        out_specs=(VMEM, VMEM, VMEM, VMEM),
        input_output_aliases={3: 0, 4: 1},
        scratch_shapes=[pltpu.SemaphoreType.DMA],
        compiler_params=pltpu.CompilerParams(vmem_limit_bytes=4 << 20),
        cost_estimate=pl.CostEstimate(flops=20_000_000, bytes_accessed=9_000_000, transcendentals=0),
        name="polar",
    )(place, offsets, near, slots, turned, partial)


def tables_body(free, out):
    for k in range(4):
        fr = free[k, 0]
        fi = free[k, 1]
        out[k, :NB, :NB] = fr
        out[k, :NB, NB:] = fi
        out[k, NB:, :NB] = -fi
        out[k, NB:, NB:] = fr


def tables_call(free):
    return pl.pallas_call(
        tables_body,
        out_shape=jax.ShapeDtypeStruct((4, 2 * NB, 2 * NB), BF16),
        in_specs=[VMEM],
        out_specs=VMEM,
        compiler_params=pltpu.CompilerParams(vmem_limit_bytes=4 << 20),
        cost_estimate=pl.CostEstimate(flops=0, bytes_accessed=7_000_000, transcendentals=0),
        name="tables",
    )(free)


def window_copies(core, own, mate, near, far, slots, sems):
    copies = [
        pltpu.make_async_copy(own, slots.at[pl.ds(4, 4)], sems.at[0]),
        pltpu.make_async_copy(mate, slots.at[pl.ds(8 - 8 * core, 4)], sems.at[1]),
        pltpu.make_async_copy(near, slots.at[pl.ds(2 + 6 * core, 2)], sems.at[2]),
    ]
    if far is not None:
        copies.append(pltpu.make_async_copy(far, slots.at[pl.ds(10 * core, 2)], sems.at[3]))
    return copies


def born_body(early, *refs):
    if early:
        (place, offsets, occupation, coupling, own, mate, near, vertex, out, *rest) = refs
        far = None
    else:
        (place, offsets, occupation, coupling, own, mate, near, far, vertex, out, *rest) = refs
    slots, chosen, mixed, wide, stack, side, total, sems = rest
    core = place[0]
    loads = [
        pltpu.make_async_copy(vertex.at[coupling[0, k]], chosen.at[k], sems.at[4 + k])
        for k in range(4)
    ]
    loads += window_copies(core, own, mate, near, far, slots, sems)
    for load in loads:
        load.start()
    for load in loads:
        load.wait()
    energy = 2 * (1 - core) if early else 2 * core

    @pl.loop(0, 4)
    def _(k):
        vr = chosen[k, 0]
        vi = chosen[k, 1]
        wide[:NB, :NB] = vr
        wide[:NB, NB:] = -vi
        wide[NB:, :NB] = vi
        wide[NB:, NB:] = vr
        side[:NB, :NB] = vr
        side[:NB, NB:] = vi
        side[NB:, :NB] = -vi
        side[NB:, NB:] = vr
        span = offsets[k]
        weight = occupation[k]
        for item in range(2):
            at = energy + 4 + item
            for part in range(2):
                low = slots[at - span, part].astype(F32)
                high = slots[at + span, part].astype(F32)
                value = weight * low + (weight + 1.0) * high
                mixed[part * NB : (part + 1) * NB, item * NB : (item + 1) * NB] = value.astype(BF16)
        half = jnp.dot(wide[...], mixed[...], preferred_element_type=F32).astype(BF16)
        for item in range(2):
            for part in range(2):
                stack[item * NB : (item + 1) * NB, part * NB : (part + 1) * NB] = half[
                    part * NB : (part + 1) * NB, item * NB : (item + 1) * NB
                ]
        term = lax.dot_general(
            stack[...], side[...], (((1,), (1,)), ((), ())), preferred_element_type=F32
        )

        @pl.when(k == 0)
        def _():
            total[...] = term

        @pl.when(k > 0)
        def _():
            total[...] += term

    store = pltpu.make_async_copy(total, out, sems.at[0])
    store.start()
    store.wait()


def born_call(place, offsets, occupation, coupling, arrays, vertex):
    early = len(arrays) == 3
    size = 2 * NB
    return pl.pallas_call(
        lambda *refs: born_body(early, *refs),
        out_shape=jax.ShapeDtypeStruct((size, size), F32),
        in_specs=[SMEM] * 4 + [ANY] * (len(arrays) + 1),
        out_specs=ANY,
        scratch_shapes=[
            pltpu.VMEM((12, 2, NB, NB), BF16),
            pltpu.VMEM((4, 2, NB, NB), BF16),
            pltpu.VMEM((size, size), BF16),
            pltpu.VMEM((size, size), BF16),
            pltpu.VMEM((size, size), BF16),
            pltpu.VMEM((size, size), BF16),
            pltpu.VMEM((size, size), F32),
            pltpu.SemaphoreType.DMA((8,)),
        ],
        compiler_params=pltpu.CompilerParams(vmem_limit_bytes=FULL),
        cost_estimate=pl.CostEstimate(
            flops=16 * size**3, bytes_accessed=12_000_000, transcendentals=0
        ),
        name="born_early" if early else "born_late",
    )(place, offsets, occupation, coupling, *arrays, vertex)


def sum_body(bands, out, buffer, copies, sems):
    loads = [
        pltpu.make_async_copy(bands.at[pl.ds(16 * i, 16)], buffer.at[pl.ds(16 * i, 16)], sems.at[i])
        for i in range(4)
    ]
    for load in loads:
        load.start()
    total = jnp.zeros((ROWS, 128), F32)
    for i, load in enumerate(loads):
        load.wait()
        total = lax.fori_loop(
            16 * i, 16 * i + 16, lambda at, value: value + buffer[at].astype(F32), total
        )
    value = total.astype(BF16)
    for i in range(16):
        copies[i] = value
    stores = [
        pltpu.make_async_copy(copies, out.at[pl.ds(16 * i, 16)], sems.at[i]) for i in range(4)
    ]
    for store in stores:
        store.start()
    for store in stores:
        store.wait()


def sum_call(bands):
    return pl.pallas_call(
        sum_body,
        out_shape=jax.ShapeDtypeStruct(bands.shape, BF16),
        in_specs=[ANY],
        out_specs=ANY,
        scratch_shapes=[
            pltpu.VMEM(bands.shape, BF16),
            pltpu.VMEM((16, ROWS, 128), BF16),
            pltpu.SemaphoreType.DMA((4,)),
        ],
        compiler_params=pltpu.CompilerParams(vmem_limit_bytes=4 << 20),
        cost_estimate=pl.CostEstimate(flops=500_000, bytes_accessed=1_900_000, transcendentals=0),
        name="band_sum",
    )(bands)


def final_body(
    place, offsets, mine, other, tables, own, mate, near, far, early, late, out,
    slots, halves, joined, flipped, table, magnon, born, sems,
):
    core = place[0]
    polar = [
        pltpu.make_async_copy(mine, halves.at[0], sems.at[10]),
        pltpu.make_async_copy(other, halves.at[1], sems.at[11]),
    ]
    free = [pltpu.make_async_copy(tables.at[k], table.at[k], sems.at[k + 6]) for k in range(4)]
    loads = window_copies(core, own, mate, near, far, slots, sems) + [
        pltpu.make_async_copy(early, born.at[0], sems.at[4]),
        pltpu.make_async_copy(late, born.at[1], sems.at[5]),
    ]
    for load in polar + free + loads:
        load.start()
    for load in polar:
        load.wait()
    for item, half in ((0, core), (1, 1 - core)):
        rows = pl.ds(pl.multiple_of(half * HALF, HALF), HALF)
        for index in range(3):
            for part in range(2):
                for panel in range(3):
                    start = ((index * 2 + part) * 3 + panel) * HALF
                    joined[index, rows, part * NB + panel * 128 : part * NB + (panel + 1) * 128] = halves[
                        item, start : start + HALF, :
                    ]

    def product(left, k):
        value = jnp.dot(left[...], table[k], preferred_element_type=F32)
        return value.astype(BF16).astype(F32)

    top, bottom, first, last = offset_roles(offsets)
    for part in range(2):
        columns = slice(part * NB, (part + 1) * NB)
        flipped[:, columns] = joined[0, :, columns].astype(F32).T.astype(BF16)
    for load in free:
        load.wait()
    magnon[1] = product(joined.at[1], first)
    magnon[2] = product(joined.at[2], last)
    magnon[0] = product(joined.at[0], top)
    magnon[0] += product(flipped, bottom)
    for load in loads:
        load.wait()
    reach = spans(offsets, first, last)
    for source, energy in ((0, 2 * (1 - core)), (1, 2 * core)):
        for item in range(2):

            @pl.loop(0, NB // 16)
            def _(block):
                rows = pl.ds(pl.multiple_of(block * 16, 16), 16)
                begin = pl.ds(pl.multiple_of(item * NB + block * 16, 16), 16)
                real = born[source, begin, :NB]
                imag = born[source, begin, NB:]
                at = energy + 4 + item
                for index in range(3):
                    down = at - reach[index]
                    up = at + reach[index]
                    sr = slots[down, 0, rows, :].astype(F32) + slots[up, 0, rows, :].astype(F32)
                    si = slots[down, 1, rows, :].astype(F32) + slots[up, 1, rows, :].astype(F32)
                    mr = magnon[index, rows, :NB]
                    mi = magnon[index, rows, NB:]
                    real += mr * sr - mi * si
                    imag += mr * si + mi * sr
                out[energy + item, 0, 0, rows, :] = real.astype(BF16)
                out[energy + item, 0, 1, rows, :] = imag.astype(BF16)


def final_call(place, offsets, mine, other, tables, own, mate, near, far, early, late):
    return pl.pallas_call(
        final_body,
        out_shape=jax.ShapeDtypeStruct((4, 1, 2, NB, NB), BF16),
        in_specs=[SMEM, SMEM] + [ANY] * 9,
        out_specs=VMEM,
        scratch_shapes=[
            pltpu.VMEM((12, 2, NB, NB), BF16),
            pltpu.VMEM((2, FLAT, 128), BF16),
            pltpu.VMEM((3, NB, 2 * NB), BF16),
            pltpu.VMEM((NB, 2 * NB), BF16),
            pltpu.VMEM((4, 2 * NB, 2 * NB), BF16),
            pltpu.VMEM((3, NB, 2 * NB), F32),
            pltpu.VMEM((2, 2 * NB, 2 * NB), F32),
            pltpu.SemaphoreType.DMA((12,)),
        ],
        compiler_params=pltpu.CompilerParams(vmem_limit_bytes=FULL),
        cost_estimate=pl.CostEstimate(
            flops=2_000_000_000, bytes_accessed=18_000_000, transcendentals=0
        ),
        name="final",
    )(place, offsets, mine, other, tables, own, mate, near, far, early, late)


def per_device(green_blocks, offsets, occupation, coupling, vertex, magnon_free):
    count = lax.axis_size(ENERGY)
    core = lax.axis_index("core").astype(jnp.int32)
    place = core[None]
    own = green_blocks.reshape(4, 2, NB, NB)
    across = [(i, i + 1) for i in range(1, count - 1, 2)]
    across += [(target, source) for source, target in across]
    outer = cut_call(place, own, 0, 2)
    near = lax.ppermute(outer, ENERGY, across)
    mate = lax.ppermute(own, "core", SWAP)
    inner = cut_call(place, own, 2, -2)
    far = lax.ppermute(inner, ENERGY, across)
    slots, turned, partial = prepare_call(place, offsets, own, mate)
    tables = tables_call(magnon_free)
    _, _, send, keep = polar_call(place, offsets, near, slots, turned, partial)
    pair = keep + lax.ppermute(send, "core", SWAP).astype(F32)
    bands = lax.all_to_all(pair.astype(BF16).reshape(BANDS, ROWS, 128), OTHERS, 0, 0, tiled=True)
    early = born_call(place, offsets, occupation, coupling, (own, mate, near), vertex)
    copies = sum_call(bands)
    mine = lax.all_to_all(copies, OTHERS, 0, 0, tiled=True).reshape(FLAT, 128)
    late = born_call(
        place, offsets, occupation, coupling, (own, mate, near, far), vertex
    )
    other = lax.ppermute(mine, "core", SWAP)
    return final_call(place, offsets, mine, other, tables, own, mate, near, far, early, late)


def solution(mesh):
    fine = Mesh(mesh.devices.reshape(4, 2, 2, 2, 4), ("y", "xh", "core", "xl", "z"))
    blocks = P(ENERGY, LAYER, None, None, None)
    placed = (blocks, P(), P(), P(LAYER, None), P(), P())
    return jax.shard_map(
        per_device, mesh=fine, in_specs=placed, out_specs=blocks, check_vma=False
    )
```

```python
import jax
import jax.numpy as jnp
from jax import lax
from jax.experimental import pallas as pl
from jax.experimental.pallas import tpu as pltpu
from jax.sharding import Mesh
from jax.sharding import PartitionSpec as P


NB = 384
HALF = NB // 2
BANDS = 64
ROWS = 56
FLAT = BANDS * ROWS
FULL = 60 << 20
F32 = jnp.float32
BF16 = jnp.bfloat16
SWAP = [(0, 1), (1, 0)]
OTHERS = ("y", "xh", "xl", "z")
ENERGY = ("y", "xh", "core")
LAYER = ("xl", "z")
ANY = pl.BlockSpec(memory_space=pl.ANY)
SMEM = pl.BlockSpec(memory_space=pltpu.SMEM)
VMEM = pl.BlockSpec(memory_space=pltpu.VMEM)


def in_hbm(array):
    return pltpu.with_memory_space_constraint(array, pltpu.HBM)


def first_index(offsets, value):
    return jnp.where(
        offsets[0] == value, 0, jnp.where(offsets[1] == value, 1, jnp.where(offsets[2] == value, 2, 3))
    )


def offset_roles(offsets):
    top = first_index(offsets, 4)
    bottom = first_index(offsets, -4)
    low = jnp.minimum(top, bottom)
    high = jnp.maximum(top, bottom)
    first = jnp.where(low != 0, 0, jnp.where(high != 1, 1, 2))
    last = jnp.where(high != 3, 3, jnp.where(low != 2, 2, 1))
    return top, bottom, first, last


def spans(offsets, first, last):
    return (jnp.int32(4), jnp.abs(offsets[first]), jnp.abs(offsets[last]))


def cut_body(place, base, sign, own, out, sem):
    copy = pltpu.make_async_copy(own.at[pl.ds(base + sign * place[0], 2)], out, sem)
    copy.start()
    copy.wait()


def cut_call(place, own, base, sign):
    return pl.pallas_call(
        lambda place, own, out, sem: cut_body(place, base, sign, own, out, sem),
        out_shape=jax.ShapeDtypeStruct((2, 2, NB, NB), BF16),
        in_specs=[SMEM, ANY],
        out_specs=VMEM,
        scratch_shapes=[pltpu.SemaphoreType.DMA],
        compiler_params=pltpu.CompilerParams(vmem_limit_bytes=4 << 20),
        cost_estimate=pl.CostEstimate(flops=0, bytes_accessed=2_400_000, transcendentals=0),
    )(place, own)


def polar_pairs(core, near, slots, turned, offsets, each):
    _, _, first, last = offset_roles(offsets)
    for index, span in enumerate(spans(offsets, first, last)):
        base = jnp.clip(4 - span, 0, 2)
        split = jnp.where(core == 0, jnp.maximum(base, 2), jnp.maximum(base, 6 - span))
        outer = (core == 0) == near
        begin = jnp.where(outer, base, split)
        end = jnp.where(outer, split, base + 4)
        if index == 0:
            back = jnp.bool_(False)
        else:
            back = offsets[first if index == 1 else last] < 0
        plain = jnp.where(back, span, 0)
        cross = jnp.where(back, 0, span)

        def block_sum(rows, real, imag):
            def step(s, carry):
                real, imag = carry
                ar = slots[s + plain + 2, 0, rows, :].astype(F32)
                ai = slots[s + plain + 2, 1, rows, :].astype(F32)
                br = turned[s + cross, 0, rows, :]
                bi = turned[s + cross, 1, rows, :]
                return real + (ar * br - ai * bi), imag + (ar * bi + ai * br)

            return lax.fori_loop(begin, end, step, (real, imag))

        each(index, block_sum)


def prepare_body(place, offsets, own, mate, slots, turned, partial, sems):
    core = place[0]
    copies = [
        pltpu.make_async_copy(own, slots.at[pl.ds(4, 4)], sems.at[0]),
        pltpu.make_async_copy(mate, slots.at[pl.ds(8 - 8 * core, 4)], sems.at[1]),
    ]
    for copy in copies:
        copy.start()
    for copy in copies:
        copy.wait()

    @pl.loop(0, 12)
    def _(step):
        slot = step // 2 + 2 - 2 * core
        part = step % 2
        turned[slot, part] = slots[slot + 2, part].astype(F32).T

    def each(index, block_sum):
        @pl.loop(0, NB // 16)
        def _(block):
            rows = pl.ds(pl.multiple_of(block * 16, 16), 16)
            zero = jnp.zeros((16, NB), F32)
            real, imag = block_sum(rows, zero, zero)
            partial[index, 0, rows, :] = real
            partial[index, 1, rows, :] = imag

    polar_pairs(core, False, slots, turned, offsets, each)


def prepare_call(place, offsets, own, mate):
    return pl.pallas_call(
        prepare_body,
        out_shape=(
            jax.ShapeDtypeStruct((12, 2, NB, NB), BF16),
            jax.ShapeDtypeStruct((8, 2, NB, NB), F32),
            jax.ShapeDtypeStruct((3, 2, NB, NB), F32),
        ),
        in_specs=[SMEM, SMEM, ANY, ANY],
        out_specs=(VMEM, VMEM, VMEM),
        scratch_shapes=[pltpu.SemaphoreType.DMA((2,))],
        compiler_params=pltpu.CompilerParams(vmem_limit_bytes=4 << 20),
        cost_estimate=pl.CostEstimate(flops=20_000_000, bytes_accessed=9_000_000, transcendentals=0),
        name="prepare",
    )(place, offsets, own, mate)


def polar_half(core, half, offsets, slots, turned, partial, target):
    def each(index, block_sum):
        @pl.loop(0, HALF // 16)
        def _(block):
            rows = pl.ds(pl.multiple_of(half * HALF + block * 16, 16), 16)
            pair = block_sum(rows, partial[index, 0, rows, :], partial[index, 1, rows, :])
            for part, value in enumerate(pair):
                for panel in range(3):
                    start = ((index * 2 + part) * 3 + panel) * HALF
                    target[pl.ds(pl.multiple_of(start + block * 16, 16), 16), :] = value[
                        :, panel * 128 : (panel + 1) * 128
                    ].astype(target.dtype)

    polar_pairs(core, True, slots, turned, offsets, each)
    tail = pl.ds(18 * HALF, FLAT - 18 * HALF)
    target[tail, :] = jnp.zeros((FLAT - 18 * HALF, 128), target.dtype)


def polar_send_body(place, offsets, near, slots_in, turned_in, partial, slots, turned, send, sem):
    core = place[0]
    copy = pltpu.make_async_copy(near, slots.at[pl.ds(2 + 6 * core, 2)], sem)
    copy.start()
    copy.wait()
    for item in range(2):
        slot = 6 * core + item
        for part in range(2):
            turned[slot, part] = slots[slot + 2, part].astype(F32).T
    polar_half(core, 1 - core, offsets, slots, turned, partial, send)


def polar_keep_body(place, offsets, slots, turned, partial, keep):
    core = place[0]
    polar_half(core, core, offsets, slots, turned, partial, keep)


def polar_send_call(place, offsets, near, slots, turned, partial):
    return pl.pallas_call(
        polar_send_body,
        out_shape=(
            jax.ShapeDtypeStruct(slots.shape, BF16),
            jax.ShapeDtypeStruct(turned.shape, F32),
            jax.ShapeDtypeStruct((FLAT, 128), BF16),
        ),
        in_specs=[SMEM, SMEM, ANY, VMEM, VMEM, VMEM],
        out_specs=(VMEM, VMEM, VMEM),
        input_output_aliases={3: 0, 4: 1},
        scratch_shapes=[pltpu.SemaphoreType.DMA],
        compiler_params=pltpu.CompilerParams(vmem_limit_bytes=4 << 20),
        cost_estimate=pl.CostEstimate(flops=20_000_000, bytes_accessed=9_000_000, transcendentals=0),
        name="polar_send",
    )(place, offsets, near, slots, turned, partial)


def polar_keep_call(place, offsets, slots, turned, partial):
    return pl.pallas_call(
        polar_keep_body,
        out_shape=jax.ShapeDtypeStruct((FLAT, 128), F32),
        in_specs=[SMEM, SMEM, VMEM, VMEM, VMEM],
        out_specs=VMEM,
        compiler_params=pltpu.CompilerParams(vmem_limit_bytes=4 << 20),
        cost_estimate=pl.CostEstimate(flops=20_000_000, bytes_accessed=9_000_000, transcendentals=0),
        name="polar_keep",
    )(place, offsets, slots, turned, partial)


def tables_body(free, out):
    for k in range(4):
        fr = free[k, 0]
        fi = free[k, 1]
        out[k, :NB, :NB] = fr
        out[k, :NB, NB:] = fi
        out[k, NB:, :NB] = -fi
        out[k, NB:, NB:] = fr


def tables_call(free):
    return pl.pallas_call(
        tables_body,
        out_shape=jax.ShapeDtypeStruct((4, 2 * NB, 2 * NB), BF16),
        in_specs=[VMEM],
        out_specs=VMEM,
        compiler_params=pltpu.CompilerParams(vmem_limit_bytes=4 << 20),
        cost_estimate=pl.CostEstimate(flops=0, bytes_accessed=7_000_000, transcendentals=0),
        name="tables",
    )(free)


def window_copies(core, own, mate, near, far, slots, sems):
    copies = [
        pltpu.make_async_copy(own, slots.at[pl.ds(4, 4)], sems.at[0]),
        pltpu.make_async_copy(mate, slots.at[pl.ds(8 - 8 * core, 4)], sems.at[1]),
        pltpu.make_async_copy(near, slots.at[pl.ds(2 + 6 * core, 2)], sems.at[2]),
    ]
    if far is not None:
        copies.append(pltpu.make_async_copy(far, slots.at[pl.ds(10 * core, 2)], sems.at[3]))
    return copies


def born_body(early, *refs):
    if early:
        (place, offsets, occupation, coupling, own, mate, near, vertex, out, *rest) = refs
        far = None
    else:
        (place, offsets, occupation, coupling, own, mate, near, far, vertex, out, *rest) = refs
    chosen, lows, highs, mixed, wide, stack, side, total, sems = rest
    core = place[0]
    energy = 2 * (1 - core) if early else 2 * core

    def fetch(slot, target, sem):
        sources = [(own, 4, 4), (mate, 8 - 8 * core, 4), (near, 2 + 6 * core, 2)]
        if far is not None:
            sources.append((far, 10 * core, 2))
        for source, low, size in sources:

            @pl.when((slot >= low) & (slot < low + size))
            def _():
                pltpu.make_async_copy(source.at[slot - low], target, sem).start()

    for k in range(4):
        pltpu.make_async_copy(vertex.at[coupling[0, k]], chosen.at[k], sems.at[k, 4]).start()
        for item in range(2):
            at = energy + 4 + item
            fetch(at - offsets[k], lows.at[k, item], sems.at[k, 2 * item])
            fetch(at + offsets[k], highs.at[k, item], sems.at[k, 2 * item + 1])

    @pl.loop(0, 4)
    def _(k):
        pltpu.make_async_copy(vertex.at[0], chosen.at[k], sems.at[k, 4]).wait()
        vr = chosen[k, 0]
        vi = chosen[k, 1]
        wide[:NB, :NB] = vr
        wide[:NB, NB:] = -vi
        wide[NB:, :NB] = vi
        wide[NB:, NB:] = vr
        side[:NB, :NB] = vr
        side[:NB, NB:] = vi
        side[NB:, :NB] = -vi
        side[NB:, NB:] = vr
        weight = occupation[k]
        for item in range(2):
            pltpu.make_async_copy(own.at[0], lows.at[k, item], sems.at[k, 2 * item]).wait()
            pltpu.make_async_copy(own.at[0], highs.at[k, item], sems.at[k, 2 * item + 1]).wait()
        for item in range(2):
            for part in range(2):
                low = lows[k, item, part].astype(F32)
                high = highs[k, item, part].astype(F32)
                value = weight * low + (weight + 1.0) * high
                mixed[part * NB : (part + 1) * NB, item * NB : (item + 1) * NB] = value.astype(BF16)
        half = jnp.dot(wide[...], mixed[...], preferred_element_type=F32).astype(BF16)
        for item in range(2):
            for part in range(2):
                stack[item * NB : (item + 1) * NB, part * NB : (part + 1) * NB] = half[
                    part * NB : (part + 1) * NB, item * NB : (item + 1) * NB
                ]
        term = lax.dot_general(
            stack[...], side[...], (((1,), (1,)), ((), ())), preferred_element_type=F32
        )

        @pl.when(k == 0)
        def _():
            total[...] = term

        @pl.when(k > 0)
        def _():
            total[...] += term

    store = pltpu.make_async_copy(total, out, sems.at[0, 0])
    store.start()
    store.wait()


def born_call(place, offsets, occupation, coupling, arrays, vertex):
    early = len(arrays) == 3
    size = 2 * NB
    return pl.pallas_call(
        lambda *refs: born_body(early, *refs),
        out_shape=jax.ShapeDtypeStruct((size, size), F32),
        in_specs=[SMEM] * 4 + [ANY] * (len(arrays) + 1),
        out_specs=ANY,
        scratch_shapes=[
            pltpu.VMEM((4, 2, NB, NB), BF16),
            pltpu.VMEM((4, 2, 2, NB, NB), BF16),
            pltpu.VMEM((4, 2, 2, NB, NB), BF16),
            pltpu.VMEM((size, size), BF16),
            pltpu.VMEM((size, size), BF16),
            pltpu.VMEM((size, size), BF16),
            pltpu.VMEM((size, size), BF16),
            pltpu.VMEM((size, size), F32),
            pltpu.SemaphoreType.DMA((4, 5)),
        ],
        compiler_params=pltpu.CompilerParams(vmem_limit_bytes=FULL),
        cost_estimate=pl.CostEstimate(
            flops=16 * size**3, bytes_accessed=12_000_000, transcendentals=0
        ),
        name="born_early" if early else "born_late",
    )(place, offsets, occupation, coupling, *arrays, vertex)


def sum_body(bands, out, buffer, copies, sems):
    loads = [
        pltpu.make_async_copy(bands.at[pl.ds(16 * i, 16)], buffer.at[pl.ds(16 * i, 16)], sems.at[i])
        for i in range(4)
    ]
    for load in loads:
        load.start()
    total = jnp.zeros((ROWS, 128), F32)
    for i, load in enumerate(loads):
        load.wait()
        total = lax.fori_loop(
            16 * i, 16 * i + 16, lambda at, value: value + buffer[at].astype(F32), total
        )
    value = total.astype(BF16)
    for i in range(16):
        copies[i] = value
    stores = [
        pltpu.make_async_copy(copies, out.at[pl.ds(16 * i, 16)], sems.at[i]) for i in range(4)
    ]
    for store in stores:
        store.start()
    for store in stores:
        store.wait()


def sum_call(bands):
    return pl.pallas_call(
        sum_body,
        out_shape=jax.ShapeDtypeStruct(bands.shape, BF16),
        in_specs=[ANY],
        out_specs=ANY,
        scratch_shapes=[
            pltpu.VMEM(bands.shape, BF16),
            pltpu.VMEM((16, ROWS, 128), BF16),
            pltpu.SemaphoreType.DMA((4,)),
        ],
        compiler_params=pltpu.CompilerParams(vmem_limit_bytes=4 << 20),
        cost_estimate=pl.CostEstimate(flops=500_000, bytes_accessed=1_900_000, transcendentals=0),
        name="band_sum",
    )(bands)


def half_products(offsets, half, source, joined, table, magnon, bottom_sum):
    for index in range(3):
        for part in range(2):
            for panel in range(3):
                start = ((index * 2 + part) * 3 + panel) * HALF
                joined[index, :, part * NB + panel * 128 : part * NB + (panel + 1) * 128] = source[
                    start : start + HALF, :
                ]
    top, bottom, first, last = offset_roles(offsets)
    rows = pl.ds(pl.multiple_of(half * HALF, HALF), HALF)
    for index, k in enumerate((top, first, last)):
        value = jnp.dot(joined[index], table[k], preferred_element_type=F32)
        magnon[index, rows, :] = value.astype(BF16).astype(F32)
    for part in range(2):
        turned = joined[0, :, part * NB : (part + 1) * NB].astype(F32).T.astype(BF16)
        begin = pl.ds(pl.multiple_of(part * NB + half * HALF, HALF), HALF)
        bottom_sum[...] += jnp.dot(turned, table[bottom, begin, :], preferred_element_type=F32)


def start_body(
    place, offsets, mine, tables, own, mate, near, far, early, late,
    slots, table, born, magnon, bottom_sum, source, joined, sems,
):
    core = place[0]
    ready = pltpu.make_async_copy(mine, source, sems.at[10])
    free = [pltpu.make_async_copy(tables.at[k], table.at[k], sems.at[k + 6]) for k in range(4)]
    loads = window_copies(core, own, mate, near, far, slots, sems) + [
        pltpu.make_async_copy(early, born.at[0], sems.at[4]),
        pltpu.make_async_copy(late, born.at[1], sems.at[5]),
    ]
    for load in [ready] + free + loads:
        load.start()
    bottom_sum[...] = jnp.zeros_like(bottom_sum)
    for load in [ready] + free:
        load.wait()
    half_products(offsets, core, source, joined, table, magnon, bottom_sum)
    for load in loads:
        load.wait()


def start_call(place, offsets, mine, tables, own, mate, near, far, early, late):
    size = 2 * NB
    return pl.pallas_call(
        start_body,
        out_shape=(
            jax.ShapeDtypeStruct((12, 2, NB, NB), BF16),
            jax.ShapeDtypeStruct((4, size, size), BF16),
            jax.ShapeDtypeStruct((2, size, size), F32),
            jax.ShapeDtypeStruct((3, NB, size), F32),
            jax.ShapeDtypeStruct((NB, size), F32),
        ),
        in_specs=[SMEM, SMEM] + [ANY] * 8,
        out_specs=(VMEM,) * 5,
        scratch_shapes=[
            pltpu.VMEM((FLAT, 128), BF16),
            pltpu.VMEM((3, HALF, size), BF16),
            pltpu.SemaphoreType.DMA((11,)),
        ],
        compiler_params=pltpu.CompilerParams(vmem_limit_bytes=8 << 20),
        cost_estimate=pl.CostEstimate(
            flops=1_000_000_000, bytes_accessed=18_000_000, transcendentals=0
        ),
        name="final_start",
    )(place, offsets, mine, *(in_hbm(x) for x in (tables, own, mate, near, far, early, late)))


def final_body(
    place, offsets, other, slots, table, born, magnon_in, sum_in, out, magnon, bottom_sum,
    source, joined, result, sems,
):
    core = place[0]
    ready = pltpu.make_async_copy(other, source, sems.at[4])
    ready.start()
    ready.wait()
    half_products(offsets, 1 - core, source, joined, table, magnon, bottom_sum)
    magnon[0] += bottom_sum[...].astype(BF16).astype(F32)
    _, _, first, last = offset_roles(offsets)
    reach = spans(offsets, first, last)
    stores = []
    for item, energy in enumerate((2 - 2 * core, 3 - 2 * core, 2 * core, 2 * core + 1)):

        @pl.loop(0, NB // 16)
        def _(block):
            rows = pl.ds(pl.multiple_of(block * 16, 16), 16)
            begin = pl.ds(pl.multiple_of((item % 2) * NB + block * 16, 16), 16)
            real = born[item // 2, begin, :NB]
            imag = born[item // 2, begin, NB:]
            for index in range(3):
                down = energy + 4 - reach[index]
                up = energy + 4 + reach[index]
                sr = slots[down, 0, rows, :].astype(F32) + slots[up, 0, rows, :].astype(F32)
                si = slots[down, 1, rows, :].astype(F32) + slots[up, 1, rows, :].astype(F32)
                mr = magnon[index, rows, :NB]
                mi = magnon[index, rows, NB:]
                real += mr * sr - mi * si
                imag += mr * si + mi * sr
            result[item, 0, rows, :] = real.astype(BF16)
            result[item, 1, rows, :] = imag.astype(BF16)

        store = pltpu.make_async_copy(result.at[item], out.at[energy, 0], sems.at[item])
        store.start()
        stores.append(store)
    for store in stores:
        store.wait()


def final_call(place, offsets, other, slots, table, born, magnon, bottom_sum):
    size = 2 * NB
    return pl.pallas_call(
        final_body,
        out_shape=(
            jax.ShapeDtypeStruct((4, 1, 2, NB, NB), BF16),
            jax.ShapeDtypeStruct(magnon.shape, F32),
            jax.ShapeDtypeStruct(bottom_sum.shape, F32),
        ),
        in_specs=[SMEM, SMEM, ANY] + [VMEM] * 5,
        out_specs=(ANY, VMEM, VMEM),
        input_output_aliases={6: 1, 7: 2},
        scratch_shapes=[
            pltpu.VMEM((FLAT, 128), BF16),
            pltpu.VMEM((3, HALF, size), BF16),
            pltpu.VMEM((4, 2, NB, NB), BF16),
            pltpu.SemaphoreType.DMA((5,)),
        ],
        compiler_params=pltpu.CompilerParams(vmem_limit_bytes=12 << 20),
        cost_estimate=pl.CostEstimate(
            flops=1_000_000_000, bytes_accessed=18_000_000, transcendentals=0
        ),
        name="final",
    )(place, offsets, other, slots, table, born, magnon, bottom_sum)[0]


def per_device(green_blocks, offsets, occupation, coupling, vertex, magnon_free):
    count = lax.axis_size(ENERGY)
    core = lax.axis_index("core").astype(jnp.int32)
    place = core[None]
    own = green_blocks.reshape(4, 2, NB, NB)
    across = [(i, i + 1) for i in range(1, count - 1, 2)]
    across += [(target, source) for source, target in across]
    outer = cut_call(place, own, 0, 2)
    near = lax.ppermute(outer, ENERGY, across)
    mate = lax.ppermute(own, "core", SWAP)
    inner = cut_call(place, own, 2, -2)
    far = lax.ppermute(inner, ENERGY, across)
    slots, turned, partial = prepare_call(place, offsets, own, mate)
    tables = tables_call(magnon_free)
    slots, turned, send = polar_send_call(place, offsets, near, slots, turned, partial)
    sent = lax.ppermute(send, "core", SWAP)
    pair = polar_keep_call(place, offsets, slots, turned, partial) + sent.astype(F32)
    bands = lax.all_to_all(pair.astype(BF16).reshape(BANDS, ROWS, 128), OTHERS, 0, 0, tiled=True)
    early = born_call(place, offsets, occupation, coupling, (own, mate, near), vertex)
    copies = sum_call(bands)
    mine = lax.all_to_all(copies, OTHERS, 0, 0, tiled=True).reshape(FLAT, 128)
    late = born_call(
        place, offsets, occupation, coupling, (own, mate, near, far), vertex
    )
    other = lax.ppermute(mine, "core", SWAP)
    held = start_call(place, offsets, mine, tables, own, mate, near, far, early, late)
    return final_call(place, offsets, other, *held)


def solution(mesh):
    fine = Mesh(mesh.devices.reshape(4, 2, 2, 2, 4), ("y", "xh", "core", "xl", "z"))
    blocks = P(ENERGY, LAYER, None, None, None)
    placed = (blocks, P(), P(), P(LAYER, None), P(), P())
    return jax.shard_map(
        per_device, mesh=fine, in_specs=placed, out_specs=blocks, check_vma=False
    )
```

```python
import jax
import jax.numpy as jnp
from jax import lax
from jax.experimental import pallas as pl
from jax.experimental.pallas import tpu as pltpu
from jax.sharding import Mesh
from jax.sharding import PartitionSpec as P


NB = 384
HALF = NB // 2
BANDS = 64
ROWS = 56
FLAT = BANDS * ROWS
FULL = 60 << 20
F32 = jnp.float32
BF16 = jnp.bfloat16
SWAP = [(0, 1), (1, 0)]
OTHERS = ("y", "xh", "xl", "z")
ENERGY = ("y", "xh", "core")
LAYER = ("xl", "z")
ANY = pl.BlockSpec(memory_space=pl.ANY)
SMEM = pl.BlockSpec(memory_space=pltpu.SMEM)
VMEM = pl.BlockSpec(memory_space=pltpu.VMEM)


def in_hbm(array):
    return pltpu.with_memory_space_constraint(array, pltpu.HBM)


def first_index(offsets, value):
    return jnp.where(
        offsets[0] == value, 0, jnp.where(offsets[1] == value, 1, jnp.where(offsets[2] == value, 2, 3))
    )


def offset_roles(offsets):
    top = first_index(offsets, 4)
    bottom = first_index(offsets, -4)
    low = jnp.minimum(top, bottom)
    high = jnp.maximum(top, bottom)
    first = jnp.where(low != 0, 0, jnp.where(high != 1, 1, 2))
    last = jnp.where(high != 3, 3, jnp.where(low != 2, 2, 1))
    return top, bottom, first, last


def spans(offsets, first, last):
    return (jnp.int32(4), jnp.abs(offsets[first]), jnp.abs(offsets[last]))


def cut_body(place, base, sign, own, out, sem):
    copy = pltpu.make_async_copy(own.at[pl.ds(base + sign * place[0], 2)], out, sem)
    copy.start()
    copy.wait()


def cut_call(place, own, base, sign):
    return pl.pallas_call(
        lambda place, own, out, sem: cut_body(place, base, sign, own, out, sem),
        out_shape=jax.ShapeDtypeStruct((2, 2, NB, NB), BF16),
        in_specs=[SMEM, ANY],
        out_specs=VMEM,
        scratch_shapes=[pltpu.SemaphoreType.DMA],
        compiler_params=pltpu.CompilerParams(vmem_limit_bytes=4 << 20),
        cost_estimate=pl.CostEstimate(flops=0, bytes_accessed=2_400_000, transcendentals=0),
    )(place, own)


def polar_pairs(core, near, slots, turned, offsets, each):
    _, _, first, last = offset_roles(offsets)
    for index, span in enumerate(spans(offsets, first, last)):
        base = jnp.clip(4 - span, 0, 2)
        split = jnp.where(core == 0, jnp.maximum(base, 2), jnp.maximum(base, 6 - span))
        outer = (core == 0) == near
        begin = jnp.where(outer, base, split)
        end = jnp.where(outer, split, base + 4)
        if index == 0:
            back = jnp.bool_(False)
        else:
            back = offsets[first if index == 1 else last] < 0
        plain = jnp.where(back, span, 0)
        cross = jnp.where(back, 0, span)

        def block_sum(rows, real, imag):
            def step(s, carry):
                real, imag = carry
                ar = slots[s + plain + 2, 0, rows, :].astype(F32)
                ai = slots[s + plain + 2, 1, rows, :].astype(F32)
                br = turned[s + cross, 0, rows, :]
                bi = turned[s + cross, 1, rows, :]
                return real + (ar * br - ai * bi), imag + (ar * bi + ai * br)

            return lax.fori_loop(begin, end, step, (real, imag))

        each(index, block_sum)


def prepare_body(place, offsets, own, mate, slots, turned, partial, sems):
    core = place[0]
    copies = [
        pltpu.make_async_copy(own, slots.at[pl.ds(4, 4)], sems.at[0]),
        pltpu.make_async_copy(mate, slots.at[pl.ds(8 - 8 * core, 4)], sems.at[1]),
    ]
    for copy in copies:
        copy.start()
    for copy in copies:
        copy.wait()

    @pl.loop(0, 12)
    def _(step):
        slot = step // 2 + 2 - 2 * core
        part = step % 2
        turned[slot, part] = slots[slot + 2, part].astype(F32).T

    def each(index, block_sum):
        @pl.loop(0, NB // 16)
        def _(block):
            rows = pl.ds(pl.multiple_of(block * 16, 16), 16)
            zero = jnp.zeros((16, NB), F32)
            real, imag = block_sum(rows, zero, zero)
            partial[index, 0, rows, :] = real
            partial[index, 1, rows, :] = imag

    polar_pairs(core, False, slots, turned, offsets, each)


def prepare_call(place, offsets, own, mate):
    return pl.pallas_call(
        prepare_body,
        out_shape=(
            jax.ShapeDtypeStruct((12, 2, NB, NB), BF16),
            jax.ShapeDtypeStruct((8, 2, NB, NB), F32),
            jax.ShapeDtypeStruct((3, 2, NB, NB), F32),
        ),
        in_specs=[SMEM, SMEM, ANY, ANY],
        out_specs=(VMEM, VMEM, VMEM),
        scratch_shapes=[pltpu.SemaphoreType.DMA((2,))],
        compiler_params=pltpu.CompilerParams(vmem_limit_bytes=4 << 20),
        cost_estimate=pl.CostEstimate(flops=20_000_000, bytes_accessed=9_000_000, transcendentals=0),
        name="prepare",
    )(place, offsets, own, mate)


def polar_half(core, half, offsets, slots, turned, partial, target):
    def each(index, block_sum):
        @pl.loop(0, HALF // 32)
        def _(block):
            rows = pl.ds(pl.multiple_of(half * HALF + block * 32, 32), 32)
            pair = block_sum(rows, partial[index, 0, rows, :], partial[index, 1, rows, :])
            for part, value in enumerate(pair):
                for panel in range(3):
                    start = ((index * 2 + part) * 3 + panel) * HALF
                    target[pl.ds(pl.multiple_of(start + block * 32, 32), 32), :] = value[
                        :, panel * 128 : (panel + 1) * 128
                    ].astype(target.dtype)

    polar_pairs(core, True, slots, turned, offsets, each)
    tail = pl.ds(18 * HALF, FLAT - 18 * HALF)
    target[tail, :] = jnp.zeros((FLAT - 18 * HALF, 128), target.dtype)


def polar_send_body(place, offsets, near, slots_in, turned_in, partial, slots, turned, send, sem):
    core = place[0]
    copy = pltpu.make_async_copy(near, slots.at[pl.ds(2 + 6 * core, 2)], sem)
    copy.start()
    copy.wait()
    for item in range(2):
        slot = 6 * core + item
        for part in range(2):
            turned[slot, part] = slots[slot + 2, part].astype(F32).T
    polar_half(core, 1 - core, offsets, slots, turned, partial, send)


def polar_keep_body(place, offsets, slots, turned, partial, keep):
    core = place[0]
    polar_half(core, core, offsets, slots, turned, partial, keep)


def polar_send_call(place, offsets, near, slots, turned, partial):
    return pl.pallas_call(
        polar_send_body,
        out_shape=(
            jax.ShapeDtypeStruct(slots.shape, BF16),
            jax.ShapeDtypeStruct(turned.shape, F32),
            jax.ShapeDtypeStruct((FLAT, 128), BF16),
        ),
        in_specs=[SMEM, SMEM, ANY, VMEM, VMEM, VMEM],
        out_specs=(VMEM, VMEM, VMEM),
        input_output_aliases={3: 0, 4: 1},
        scratch_shapes=[pltpu.SemaphoreType.DMA],
        compiler_params=pltpu.CompilerParams(vmem_limit_bytes=4 << 20),
        cost_estimate=pl.CostEstimate(flops=20_000_000, bytes_accessed=9_000_000, transcendentals=0),
        name="polar_send",
    )(place, offsets, near, slots, turned, partial)


def polar_keep_call(place, offsets, slots, turned, partial):
    return pl.pallas_call(
        polar_keep_body,
        out_shape=jax.ShapeDtypeStruct((FLAT, 128), F32),
        in_specs=[SMEM, SMEM, VMEM, VMEM, VMEM],
        out_specs=VMEM,
        compiler_params=pltpu.CompilerParams(vmem_limit_bytes=4 << 20),
        cost_estimate=pl.CostEstimate(flops=20_000_000, bytes_accessed=9_000_000, transcendentals=0),
        name="polar_keep",
    )(place, offsets, slots, turned, partial)


def add_body(kept, sent, out, total, sems):
    third = FLAT // 4
    stores = []
    for i in range(4):
        rows = pl.ds(i * third, third)
        total[rows, :] = (kept[rows, :] + sent[rows, :].astype(F32)).astype(BF16)
        store = pltpu.make_async_copy(total.at[rows], out.at[rows], sems.at[i])
        store.start()
        stores.append(store)
    for store in stores:
        store.wait()


def add_call(kept, sent):
    return pl.pallas_call(
        add_body,
        out_shape=jax.ShapeDtypeStruct((FLAT, 128), BF16),
        in_specs=[VMEM, VMEM],
        out_specs=ANY,
        scratch_shapes=[pltpu.VMEM((FLAT, 128), BF16), pltpu.SemaphoreType.DMA((4,))],
        compiler_params=pltpu.CompilerParams(vmem_limit_bytes=3 << 20),
        cost_estimate=pl.CostEstimate(flops=500_000, bytes_accessed=3_000_000, transcendentals=0),
        name="pair_add",
    )(kept, sent)


def window_copies(core, own, mate, near, far, slots, sems):
    copies = [
        pltpu.make_async_copy(own, slots.at[pl.ds(4, 4)], sems.at[0]),
        pltpu.make_async_copy(mate, slots.at[pl.ds(8 - 8 * core, 4)], sems.at[1]),
        pltpu.make_async_copy(near, slots.at[pl.ds(2 + 6 * core, 2)], sems.at[2]),
    ]
    if far is not None:
        copies.append(pltpu.make_async_copy(far, slots.at[pl.ds(10 * core, 2)], sems.at[3]))
    return copies


def born_body(early, *refs):
    if early:
        (place, offsets, occupation, coupling, own, mate, near, vertex, out, *rest) = refs
        far = None
    else:
        (place, offsets, occupation, coupling, own, mate, near, far, vertex, out, *rest) = refs
    chosen, lows, highs, mixed, wide, stack, side, total, sems = rest
    core = place[0]
    energy = 2 * (1 - core) if early else 2 * core

    def fetch(slot, target, sem):
        sources = [(own, 4, 4), (mate, 8 - 8 * core, 4), (near, 2 + 6 * core, 2)]
        if far is not None:
            sources.append((far, 10 * core, 2))
        for source, low, size in sources:

            @pl.when((slot >= low) & (slot < low + size))
            def _():
                pltpu.make_async_copy(source.at[slot - low], target, sem).start()

    for k in range(4):
        pltpu.make_async_copy(vertex.at[coupling[0, k]], chosen.at[k], sems.at[k, 4]).start()
        for item in range(2):
            at = energy + 4 + item
            fetch(at - offsets[k], lows.at[k, item], sems.at[k, 2 * item])
            fetch(at + offsets[k], highs.at[k, item], sems.at[k, 2 * item + 1])

    @pl.loop(0, 4)
    def _(k):
        pltpu.make_async_copy(vertex.at[0], chosen.at[k], sems.at[k, 4]).wait()
        vr = chosen[k, 0]
        vi = chosen[k, 1]
        wide[:NB, :NB] = vr
        wide[:NB, NB:] = -vi
        wide[NB:, :NB] = vi
        wide[NB:, NB:] = vr
        side[:NB, :NB] = vr
        side[:NB, NB:] = vi
        side[NB:, :NB] = -vi
        side[NB:, NB:] = vr
        weight = occupation[k]
        for item in range(2):
            pltpu.make_async_copy(own.at[0], lows.at[k, item], sems.at[k, 2 * item]).wait()
            pltpu.make_async_copy(own.at[0], highs.at[k, item], sems.at[k, 2 * item + 1]).wait()
        for item in range(2):
            for part in range(2):
                low = lows[k, item, part].astype(F32)
                high = highs[k, item, part].astype(F32)
                value = weight * low + (weight + 1.0) * high
                mixed[part * NB : (part + 1) * NB, item * NB : (item + 1) * NB] = value.astype(BF16)
        half = jnp.dot(wide[...], mixed[...], preferred_element_type=F32).astype(BF16)
        for item in range(2):
            for part in range(2):
                stack[item * NB : (item + 1) * NB, part * NB : (part + 1) * NB] = half[
                    part * NB : (part + 1) * NB, item * NB : (item + 1) * NB
                ]
        term = lax.dot_general(
            stack[...], side[...], (((1,), (1,)), ((), ())), preferred_element_type=F32
        )

        @pl.when(k == 0)
        def _():
            total[...] = term

        @pl.when(k > 0)
        def _():
            total[...] += term

    out[...] = total[...].astype(BF16)


def born_call(place, offsets, occupation, coupling, arrays, vertex):
    early = len(arrays) == 3
    size = 2 * NB
    return pl.pallas_call(
        lambda *refs: born_body(early, *refs),
        out_shape=jax.ShapeDtypeStruct((size, size), BF16),
        in_specs=[SMEM] * 4 + [ANY] * (len(arrays) + 1),
        out_specs=VMEM,
        scratch_shapes=[
            pltpu.VMEM((4, 2, NB, NB), BF16),
            pltpu.VMEM((4, 2, 2, NB, NB), BF16),
            pltpu.VMEM((4, 2, 2, NB, NB), BF16),
            pltpu.VMEM((size, size), BF16),
            pltpu.VMEM((size, size), BF16),
            pltpu.VMEM((size, size), BF16),
            pltpu.VMEM((size, size), BF16),
            pltpu.VMEM((size, size), F32),
            pltpu.SemaphoreType.DMA((4, 5)),
        ],
        compiler_params=pltpu.CompilerParams(vmem_limit_bytes=FULL),
        cost_estimate=pl.CostEstimate(
            flops=16 * size**3, bytes_accessed=12_000_000, transcendentals=0
        ),
        name="born_early" if early else "born_late",
    )(place, offsets, occupation, coupling, *arrays, vertex)


def sum_body(bands, out, buffer, copies, sems):
    loads = [
        pltpu.make_async_copy(bands.at[pl.ds(16 * i, 16)], buffer.at[pl.ds(16 * i, 16)], sems.at[i])
        for i in range(4)
    ]
    for load in loads:
        load.start()
    total = jnp.zeros((ROWS, 128), F32)
    for i, load in enumerate(loads):
        load.wait()
        for at in range(16 * i, 16 * i + 16):
            total += buffer[at].astype(F32)
    value = total.astype(BF16)
    for i in range(16):
        copies[i] = value
    stores = [
        pltpu.make_async_copy(copies, out.at[pl.ds(16 * i, 16)], sems.at[i]) for i in range(4)
    ]
    for store in stores:
        store.start()
    for store in stores:
        store.wait()


def sum_call(bands):
    return pl.pallas_call(
        sum_body,
        out_shape=jax.ShapeDtypeStruct(bands.shape, BF16),
        in_specs=[ANY],
        out_specs=ANY,
        scratch_shapes=[
            pltpu.VMEM(bands.shape, BF16),
            pltpu.VMEM((16, ROWS, 128), BF16),
            pltpu.SemaphoreType.DMA((4,)),
        ],
        compiler_params=pltpu.CompilerParams(vmem_limit_bytes=4 << 20),
        cost_estimate=pl.CostEstimate(flops=500_000, bytes_accessed=1_900_000, transcendentals=0),
        name="band_sum",
    )(bands)


def half_products(offsets, half, source, joined, table, magnon, bottom_sum):
    for index in range(3):
        for part in range(2):
            for panel in range(3):
                start = ((index * 2 + part) * 3 + panel) * HALF
                joined[index, :, part * NB + panel * 128 : part * NB + (panel + 1) * 128] = source[
                    start : start + HALF, :
                ]
    top, bottom, first, last = offset_roles(offsets)
    rows = pl.ds(pl.multiple_of(half * HALF, HALF), HALF)
    for index, k in enumerate((top, first, last)):
        value = jnp.dot(joined[index], table[k], preferred_element_type=F32)
        magnon[index, rows, :] = value.astype(BF16).astype(F32)
    for part in range(2):
        turned = joined[0, :, part * NB : (part + 1) * NB].astype(F32).T.astype(BF16)
        begin = pl.ds(pl.multiple_of(part * NB + half * HALF, HALF), HALF)
        bottom_sum[...] += jnp.dot(turned, table[bottom, begin, :], preferred_element_type=F32)


def start_body(
    place, offsets, mine, free, own, mate, near, far,
    slots, magnon, bottom_sum, table, source, plain, joined, sems,
):
    core = place[0]
    ready = [
        pltpu.make_async_copy(mine, source, sems.at[4]),
        pltpu.make_async_copy(free, plain, sems.at[5]),
    ]
    loads = window_copies(core, own, mate, near, far, slots, sems)
    for load in ready + loads:
        load.start()
    bottom_sum[...] = jnp.zeros_like(bottom_sum)
    for load in ready:
        load.wait()
    for k in range(4):
        fr = plain[k, 0]
        fi = plain[k, 1]
        table[k, :NB, :NB] = fr
        table[k, :NB, NB:] = fi
        table[k, NB:, :NB] = -fi
        table[k, NB:, NB:] = fr
    half_products(offsets, core, source, joined, table, magnon, bottom_sum)
    for load in loads:
        load.wait()


def start_call(place, offsets, mine, free, own, mate, near, far):
    size = 2 * NB
    return pl.pallas_call(
        start_body,
        out_shape=(
            jax.ShapeDtypeStruct((12, 2, NB, NB), BF16),
            jax.ShapeDtypeStruct((3, NB, size), F32),
            jax.ShapeDtypeStruct((NB, size), F32),
            jax.ShapeDtypeStruct((4, size, size), BF16),
        ),
        in_specs=[SMEM, SMEM] + [ANY] * 6,
        out_specs=(VMEM,) * 4,
        scratch_shapes=[
            pltpu.VMEM((FLAT, 128), BF16),
            pltpu.VMEM((4, 2, NB, NB), BF16),
            pltpu.VMEM((3, HALF, size), BF16),
            pltpu.SemaphoreType.DMA((6,)),
        ],
        compiler_params=pltpu.CompilerParams(vmem_limit_bytes=10 << 20),
        cost_estimate=pl.CostEstimate(
            flops=1_000_000_000, bytes_accessed=10_000_000, transcendentals=0
        ),
        name="final_start",
    )(place, offsets, mine, *(in_hbm(x) for x in (free, own, mate, near, far)))


def final_body(
    place, offsets, other, early, late, slots, magnon_in, sum_in, table, out, magnon, bottom_sum,
    source, joined, result, sems,
):
    core = place[0]
    ready = pltpu.make_async_copy(other, source, sems.at[4])
    ready.start()
    ready.wait()
    half_products(offsets, 1 - core, source, joined, table, magnon, bottom_sum)
    magnon[0] += bottom_sum[...].astype(BF16).astype(F32)
    _, _, first, last = offset_roles(offsets)
    reach = spans(offsets, first, last)
    stores = []
    for item, energy in enumerate((2 - 2 * core, 3 - 2 * core, 2 * core, 2 * core + 1)):
        born = early if item < 2 else late

        @pl.loop(0, NB // 16)
        def _(block):
            rows = pl.ds(pl.multiple_of(block * 16, 16), 16)
            begin = pl.ds(pl.multiple_of((item % 2) * NB + block * 16, 16), 16)
            real = born[begin, :NB].astype(F32)
            imag = born[begin, NB:].astype(F32)
            for index in range(3):
                down = energy + 4 - reach[index]
                up = energy + 4 + reach[index]
                sr = slots[down, 0, rows, :].astype(F32) + slots[up, 0, rows, :].astype(F32)
                si = slots[down, 1, rows, :].astype(F32) + slots[up, 1, rows, :].astype(F32)
                mr = magnon[index, rows, :NB]
                mi = magnon[index, rows, NB:]
                real += mr * sr - mi * si
                imag += mr * si + mi * sr
            result[item, 0, rows, :] = real.astype(BF16)
            result[item, 1, rows, :] = imag.astype(BF16)

        store = pltpu.make_async_copy(result.at[item], out.at[energy, 0], sems.at[item])
        store.start()
        stores.append(store)
    for store in stores:
        store.wait()


def final_call(place, offsets, other, early, late, slots, magnon, bottom_sum, table):
    size = 2 * NB
    return pl.pallas_call(
        final_body,
        out_shape=(
            jax.ShapeDtypeStruct((4, 1, 2, NB, NB), BF16),
            jax.ShapeDtypeStruct(magnon.shape, F32),
            jax.ShapeDtypeStruct(bottom_sum.shape, F32),
        ),
        in_specs=[SMEM, SMEM, ANY] + [VMEM] * 6,
        out_specs=(ANY, VMEM, VMEM),
        input_output_aliases={6: 1, 7: 2},
        scratch_shapes=[
            pltpu.VMEM((FLAT, 128), BF16),
            pltpu.VMEM((3, HALF, size), BF16),
            pltpu.VMEM((4, 2, NB, NB), BF16),
            pltpu.SemaphoreType.DMA((5,)),
        ],
        compiler_params=pltpu.CompilerParams(vmem_limit_bytes=12 << 20),
        cost_estimate=pl.CostEstimate(
            flops=1_000_000_000, bytes_accessed=18_000_000, transcendentals=0
        ),
        name="final",
    )(place, offsets, other, early, late, slots, magnon, bottom_sum, table)[0]


def per_device(green_blocks, offsets, occupation, coupling, vertex, magnon_free):
    count = lax.axis_size(ENERGY)
    core = lax.axis_index("core").astype(jnp.int32)
    place = core[None]
    own = green_blocks.reshape(4, 2, NB, NB)
    across = [(i, i + 1) for i in range(1, count - 1, 2)]
    across += [(target, source) for source, target in across]
    outer = cut_call(place, own, 0, 2)
    near = lax.ppermute(outer, ENERGY, across)
    mate = lax.ppermute(own, "core", SWAP)
    inner = cut_call(place, own, 2, -2)
    far = lax.ppermute(inner, ENERGY, across)
    slots, turned, partial = prepare_call(place, offsets, own, mate)
    slots, turned, send = polar_send_call(place, offsets, near, slots, turned, partial)
    sent = lax.ppermute(send, "core", SWAP)
    kept = polar_keep_call(place, offsets, slots, turned, partial)
    pair = add_call(kept, sent)
    bands = lax.all_to_all(
        pair.reshape(BANDS, ROWS, 128), OTHERS, 0, 0, tiled=True
    )
    early = born_call(place, offsets, occupation, coupling, (own, mate, near), vertex)
    copies = sum_call(bands)
    mine = lax.all_to_all(copies, OTHERS, 0, 0, tiled=True).reshape(FLAT, 128)
    late = born_call(
        place, offsets, occupation, coupling, (own, mate, near, far), vertex
    )
    other = lax.ppermute(mine, "core", SWAP)
    held = start_call(place, offsets, mine, magnon_free, own, mate, near, far)
    return final_call(place, offsets, other, early, late, *held)


def solution(mesh):
    fine = Mesh(mesh.devices.reshape(4, 2, 2, 2, 4), ("y", "xh", "core", "xl", "z"))
    blocks = P(ENERGY, LAYER, None, None, None)
    placed = (blocks, P(), P(), P(LAYER, None), P(), P())
    return jax.shard_map(
        per_device, mesh=fine, in_specs=placed, out_specs=blocks, check_vma=False
    )
```

```python
import jax
import jax.numpy as jnp
from jax import lax
from jax.experimental import pallas as pl
from jax.experimental.pallas import tpu as pltpu
from jax.sharding import Mesh
from jax.sharding import PartitionSpec as P


NB = 384
HALF = NB // 2
BANDS = 16
ROWS = 18 * HALF // BANDS
FLAT = BANDS * ROWS
FULL = 60 << 20
F32 = jnp.float32
BF16 = jnp.bfloat16
SWAP = [(0, 1), (1, 0)]
PLANE = ("y", "z")
ROW = ("xh", "xl")
ENERGY = ("y", "xh", "core")
LAYER = ("xl", "z")
ANY = pl.BlockSpec(memory_space=pl.ANY)
SMEM = pl.BlockSpec(memory_space=pltpu.SMEM)
VMEM = pl.BlockSpec(memory_space=pltpu.VMEM)


def in_hbm(array):
    return pltpu.with_memory_space_constraint(array, pltpu.HBM)


def first_index(offsets, value):
    return jnp.where(
        offsets[0] == value, 0, jnp.where(offsets[1] == value, 1, jnp.where(offsets[2] == value, 2, 3))
    )


def offset_roles(offsets):
    top = first_index(offsets, 4)
    bottom = first_index(offsets, -4)
    low = jnp.minimum(top, bottom)
    high = jnp.maximum(top, bottom)
    first = jnp.where(low != 0, 0, jnp.where(high != 1, 1, 2))
    last = jnp.where(high != 3, 3, jnp.where(low != 2, 2, 1))
    return top, bottom, first, last


def spans(offsets, first, last):
    return (jnp.int32(4), jnp.abs(offsets[first]), jnp.abs(offsets[last]))


def cut_body(place, base, sign, own, out, sem):
    copy = pltpu.make_async_copy(own.at[pl.ds(base + sign * place[0], 2)], out, sem)
    copy.start()
    copy.wait()


def cut_call(place, own, base, sign):
    return pl.pallas_call(
        lambda place, own, out, sem: cut_body(place, base, sign, own, out, sem),
        out_shape=jax.ShapeDtypeStruct((2, 2, NB, NB), BF16),
        in_specs=[SMEM, ANY],
        out_specs=VMEM,
        scratch_shapes=[pltpu.SemaphoreType.DMA],
        compiler_params=pltpu.CompilerParams(vmem_limit_bytes=4 << 20),
        cost_estimate=pl.CostEstimate(flops=0, bytes_accessed=2_400_000, transcendentals=0),
    )(place, in_hbm(own))


def polar_pairs(core, near, slots, turned, offsets, each):
    _, _, first, last = offset_roles(offsets)
    for index, span in enumerate(spans(offsets, first, last)):
        base = jnp.clip(4 - span, 0, 2)
        split = jnp.where(core == 0, jnp.maximum(base, 2), jnp.maximum(base, 6 - span))
        outer = (core == 0) == near
        begin = jnp.where(outer, base, split)
        end = jnp.where(outer, split, base + 4)
        if index == 0:
            back = jnp.bool_(False)
        else:
            back = offsets[first if index == 1 else last] < 0
        plain = jnp.where(back, span, 0)
        cross = jnp.where(back, 0, span)

        def block_sum(rows, real, imag):
            def step(s, carry):
                real, imag = carry
                ar = slots[s + plain + 2, 0, rows, :].astype(F32)
                ai = slots[s + plain + 2, 1, rows, :].astype(F32)
                br = turned[s + cross, 0, rows, :]
                bi = turned[s + cross, 1, rows, :]
                return real + (ar * br - ai * bi), imag + (ar * bi + ai * br)

            return lax.fori_loop(begin, end, step, (real, imag))

        each(index, block_sum)


def prepare_body(place, offsets, own, mate, slots, turned, partial, sems):
    core = place[0]
    copies = [
        pltpu.make_async_copy(own, slots.at[pl.ds(4, 4)], sems.at[0]),
        pltpu.make_async_copy(mate, slots.at[pl.ds(8 - 8 * core, 4)], sems.at[1]),
    ]
    for copy in copies:
        copy.start()
    for copy in copies:
        copy.wait()

    @pl.loop(0, 12)
    def _(step):
        slot = step // 2 + 2 - 2 * core
        part = step % 2
        turned[slot, part] = slots[slot + 2, part].astype(F32).T

    def each(index, block_sum):
        @pl.loop(0, NB // 16)
        def _(block):
            rows = pl.ds(pl.multiple_of(block * 16, 16), 16)
            zero = jnp.zeros((16, NB), F32)
            real, imag = block_sum(rows, zero, zero)
            partial[index, 0, rows, :] = real
            partial[index, 1, rows, :] = imag

    polar_pairs(core, False, slots, turned, offsets, each)


def prepare_call(place, offsets, own, mate):
    return pl.pallas_call(
        prepare_body,
        out_shape=(
            jax.ShapeDtypeStruct((12, 2, NB, NB), BF16),
            jax.ShapeDtypeStruct((8, 2, NB, NB), F32),
            jax.ShapeDtypeStruct((3, 2, NB, NB), F32),
        ),
        in_specs=[SMEM, SMEM, ANY, ANY],
        out_specs=(VMEM, VMEM, VMEM),
        scratch_shapes=[pltpu.SemaphoreType.DMA((2,))],
        compiler_params=pltpu.CompilerParams(vmem_limit_bytes=4 << 20),
        cost_estimate=pl.CostEstimate(flops=20_000_000, bytes_accessed=9_000_000, transcendentals=0),
        name="prepare",
    )(place, offsets, own, mate)


def polar_half(core, half, offsets, slots, turned, partial, target):
    def each(index, block_sum):
        @pl.loop(0, HALF // 32)
        def _(block):
            rows = pl.ds(pl.multiple_of(half * HALF + block * 32, 32), 32)
            pair = block_sum(rows, partial[index, 0, rows, :], partial[index, 1, rows, :])
            for part, value in enumerate(pair):
                for panel in range(3):
                    start = ((index * 2 + part) * 3 + panel) * HALF
                    target[pl.ds(pl.multiple_of(start + block * 32, 32), 32), :] = value[
                        :, panel * 128 : (panel + 1) * 128
                    ].astype(target.dtype)

    polar_pairs(core, True, slots, turned, offsets, each)


def polar_send_body(place, offsets, near, slots_in, turned_in, partial, slots, turned, send, sem):
    core = place[0]
    copy = pltpu.make_async_copy(near, slots.at[pl.ds(2 + 6 * core, 2)], sem)
    copy.start()
    copy.wait()
    for item in range(2):
        slot = 6 * core + item
        for part in range(2):
            turned[slot, part] = slots[slot + 2, part].astype(F32).T
    polar_half(core, 1 - core, offsets, slots, turned, partial, send)


def polar_keep_body(place, offsets, slots, turned, partial, keep):
    core = place[0]
    polar_half(core, core, offsets, slots, turned, partial, keep)


def polar_send_call(place, offsets, near, slots, turned, partial):
    return pl.pallas_call(
        polar_send_body,
        out_shape=(
            jax.ShapeDtypeStruct(slots.shape, BF16),
            jax.ShapeDtypeStruct(turned.shape, F32),
            jax.ShapeDtypeStruct((FLAT, 128), BF16),
        ),
        in_specs=[SMEM, SMEM, ANY, VMEM, VMEM, VMEM],
        out_specs=(VMEM, VMEM, VMEM),
        input_output_aliases={3: 0, 4: 1},
        scratch_shapes=[pltpu.SemaphoreType.DMA],
        compiler_params=pltpu.CompilerParams(vmem_limit_bytes=4 << 20),
        cost_estimate=pl.CostEstimate(flops=20_000_000, bytes_accessed=9_000_000, transcendentals=0),
        name="polar_send",
    )(place, offsets, near, slots, turned, partial)


def polar_keep_call(place, offsets, slots, turned, partial):
    return pl.pallas_call(
        polar_keep_body,
        out_shape=jax.ShapeDtypeStruct((FLAT, 128), F32),
        in_specs=[SMEM, SMEM, VMEM, VMEM, VMEM],
        out_specs=VMEM,
        compiler_params=pltpu.CompilerParams(vmem_limit_bytes=4 << 20),
        cost_estimate=pl.CostEstimate(flops=20_000_000, bytes_accessed=9_000_000, transcendentals=0),
        name="polar_keep",
    )(place, offsets, slots, turned, partial)


def add_body(kept, sent, out, total, sems):
    third = FLAT // 4
    stores = []
    for i in range(4):
        rows = pl.ds(i * third, third)
        total[rows, :] = (kept[rows, :] + sent[rows, :].astype(F32)).astype(BF16)
        store = pltpu.make_async_copy(total.at[rows], out.at[rows], sems.at[i])
        store.start()
        stores.append(store)
    for store in stores:
        store.wait()


def add_call(kept, sent):
    return pl.pallas_call(
        add_body,
        out_shape=jax.ShapeDtypeStruct((FLAT, 128), BF16),
        in_specs=[VMEM, VMEM],
        out_specs=ANY,
        scratch_shapes=[pltpu.VMEM((FLAT, 128), BF16), pltpu.SemaphoreType.DMA((4,))],
        compiler_params=pltpu.CompilerParams(vmem_limit_bytes=3 << 20),
        cost_estimate=pl.CostEstimate(flops=500_000, bytes_accessed=3_000_000, transcendentals=0),
        name="pair_add",
    )(kept, sent)


def window_copies(core, own, mate, near, far, slots, sems):
    copies = [
        pltpu.make_async_copy(own, slots.at[pl.ds(4, 4)], sems.at[0]),
        pltpu.make_async_copy(mate, slots.at[pl.ds(8 - 8 * core, 4)], sems.at[1]),
        pltpu.make_async_copy(near, slots.at[pl.ds(2 + 6 * core, 2)], sems.at[2]),
    ]
    if far is not None:
        copies.append(pltpu.make_async_copy(far, slots.at[pl.ds(10 * core, 2)], sems.at[3]))
    return copies


def born_body(early, *refs):
    if early:
        (place, offsets, occupation, coupling, own, mate, near, vertex, out, *rest) = refs
        far = None
    else:
        (place, offsets, occupation, coupling, own, mate, near, far, vertex, out, *rest) = refs
    chosen, lows, highs, mixed, wide, stack, side, total, sems = rest
    core = place[0]
    energy = 2 * (1 - core) if early else 2 * core

    def fetch(slot, target, sem):
        sources = [(own, 4, 4), (mate, 8 - 8 * core, 4), (near, 2 + 6 * core, 2)]
        if far is not None:
            sources.append((far, 10 * core, 2))
        for source, low, size in sources:

            @pl.when((slot >= low) & (slot < low + size))
            def _():
                pltpu.make_async_copy(source.at[slot - low], target, sem).start()

    for k in range(4):
        pltpu.make_async_copy(vertex.at[coupling[0, k]], chosen.at[k], sems.at[k, 4]).start()
        for item in range(2):
            at = energy + 4 + item
            fetch(at - offsets[k], lows.at[k, item], sems.at[k, 2 * item])
            fetch(at + offsets[k], highs.at[k, item], sems.at[k, 2 * item + 1])

    total[...] = jnp.zeros_like(total)

    @pl.loop(0, 4)
    def _(k):
        pltpu.make_async_copy(vertex.at[0], chosen.at[k], sems.at[k, 4]).wait()
        vr = chosen[k, 0]
        vi = chosen[k, 1]
        wide[:NB, :NB] = vr
        wide[:NB, NB:] = -vi
        wide[NB:, :NB] = vi
        wide[NB:, NB:] = vr
        side[:NB, :NB] = vr
        side[:NB, NB:] = vi
        side[NB:, :NB] = -vi
        side[NB:, NB:] = vr
        weight = occupation[k]
        for item in range(2):
            pltpu.make_async_copy(own.at[0], lows.at[k, item], sems.at[k, 2 * item]).wait()
            pltpu.make_async_copy(own.at[0], highs.at[k, item], sems.at[k, 2 * item + 1]).wait()
        for item in range(2):
            for part in range(2):
                low = lows[k, item, part].astype(F32)
                high = highs[k, item, part].astype(F32)
                value = weight * low + (weight + 1.0) * high
                mixed[part * NB : (part + 1) * NB, item * NB : (item + 1) * NB] = value.astype(BF16)
        for piece in range(2):
            begin = piece * 384
            part, row = begin // NB, begin % NB
            half = jnp.dot(
                wide[begin : begin + 384, :], mixed[...], preferred_element_type=F32
            ).astype(BF16)
            for item in range(2):
                stack[item * NB + row : item * NB + row + 384, part * NB : (part + 1) * NB] = half[
                    :, item * NB : (item + 1) * NB
                ]
        for piece in range(2):
            rows = slice(piece * 384, (piece + 1) * 384)
            term = lax.dot_general(
                stack[rows, :], side[...], (((1,), (1,)), ((), ())), preferred_element_type=F32
            )
            total[rows, :] += term

    out[...] = total[...].astype(BF16)


def born_call(place, offsets, occupation, coupling, arrays, vertex):
    early = len(arrays) == 3
    size = 2 * NB
    return pl.pallas_call(
        lambda *refs: born_body(early, *refs),
        out_shape=jax.ShapeDtypeStruct((size, size), BF16),
        in_specs=[SMEM] * 4 + [ANY] * (len(arrays) + 1),
        out_specs=VMEM,
        scratch_shapes=[
            pltpu.VMEM((4, 2, NB, NB), BF16),
            pltpu.VMEM((4, 2, 2, NB, NB), BF16),
            pltpu.VMEM((4, 2, 2, NB, NB), BF16),
            pltpu.VMEM((size, size), BF16),
            pltpu.VMEM((size, size), BF16),
            pltpu.VMEM((size, size), BF16),
            pltpu.VMEM((size, size), BF16),
            pltpu.VMEM((size, size), F32),
            pltpu.SemaphoreType.DMA((4, 5)),
        ],
        compiler_params=pltpu.CompilerParams(vmem_limit_bytes=FULL),
        cost_estimate=pl.CostEstimate(
            flops=16 * size**3, bytes_accessed=12_000_000, transcendentals=0
        ),
        name="born_early" if early else "born_late",
    )(place, offsets, occupation, coupling, *arrays, vertex)


def sum_body(count, copies, bands, out, buffer, value, *sems):
    loads = [
        pltpu.make_async_copy(bands.at[i], buffer.at[i], sems[0].at[i]) for i in range(count)
    ]
    for load in loads:
        load.start()
    for load in loads:
        load.wait()

    for begin in range(0, ROWS, 64):
        rows = slice(begin, min(begin + 64, ROWS))
        total = buffer[0, rows, :].astype(F32)
        for i in range(1, count):
            total += buffer[i, rows, :].astype(F32)
        value[rows, :] = total.astype(BF16)

    stores = [pltpu.make_async_copy(value, out.at[i], sems[1].at[i]) for i in range(copies)]
    for store in stores:
        store.start()
    for store in stores:
        store.wait()


def sum_call(bands, copies):
    count = bands.shape[0]
    return pl.pallas_call(
        lambda *refs: sum_body(count, copies, *refs),
        out_shape=jax.ShapeDtypeStruct((copies, ROWS, 128), BF16),
        in_specs=[ANY],
        out_specs=ANY,
        scratch_shapes=[
            pltpu.VMEM(bands.shape, BF16),
            pltpu.VMEM((ROWS, 128), BF16),
            pltpu.SemaphoreType.DMA((count,)),
            pltpu.SemaphoreType.DMA((copies,)),
        ],
        compiler_params=pltpu.CompilerParams(vmem_limit_bytes=4 << 20),
        cost_estimate=pl.CostEstimate(flops=500_000, bytes_accessed=1_900_000, transcendentals=0),
    )(bands)


def half_products(offsets, half, source, joined, table, magnon, bottom_sum):
    for index in range(3):
        for part in range(2):
            for panel in range(3):
                start = ((index * 2 + part) * 3 + panel) * HALF
                joined[index, :, part * NB + panel * 128 : part * NB + (panel + 1) * 128] = source[
                    start : start + HALF, :
                ]
    top, bottom, first, last = offset_roles(offsets)
    rows = pl.ds(pl.multiple_of(half * HALF, HALF), HALF)
    for index, k in enumerate((top, first, last)):
        value = jnp.dot(joined[index], table[k], preferred_element_type=F32)
        magnon[index, rows, :] = value.astype(BF16).astype(F32)
    for part in range(2):
        turned = joined[0, :, part * NB : (part + 1) * NB].astype(F32).T.astype(BF16)
        begin = pl.ds(pl.multiple_of(part * NB + half * HALF, HALF), HALF)
        bottom_sum[...] += jnp.dot(turned, table[bottom, begin, :], preferred_element_type=F32)


def start_body(
    place, offsets, mine, free, own, mate, near, far,
    slots, magnon, bottom_sum, table, source, plain, joined, sems,
):
    core = place[0]
    ready = [
        pltpu.make_async_copy(mine, source, sems.at[4]),
        pltpu.make_async_copy(free, plain, sems.at[5]),
    ]
    loads = window_copies(core, own, mate, near, far, slots, sems)
    for load in ready + loads:
        load.start()
    bottom_sum[...] = jnp.zeros_like(bottom_sum)
    for load in ready:
        load.wait()
    for k in range(4):
        fr = plain[k, 0]
        fi = plain[k, 1]
        table[k, :NB, :NB] = fr
        table[k, :NB, NB:] = fi
        table[k, NB:, :NB] = -fi
        table[k, NB:, NB:] = fr
    half_products(offsets, core, source, joined, table, magnon, bottom_sum)
    for load in loads:
        load.wait()


def start_call(place, offsets, mine, free, own, mate, near, far):
    size = 2 * NB
    return pl.pallas_call(
        start_body,
        out_shape=(
            jax.ShapeDtypeStruct((12, 2, NB, NB), BF16),
            jax.ShapeDtypeStruct((3, NB, size), F32),
            jax.ShapeDtypeStruct((NB, size), F32),
            jax.ShapeDtypeStruct((4, size, size), BF16),
        ),
        in_specs=[SMEM, SMEM] + [ANY] * 6,
        out_specs=(VMEM,) * 4,
        scratch_shapes=[
            pltpu.VMEM((FLAT, 128), BF16),
            pltpu.VMEM((4, 2, NB, NB), BF16),
            pltpu.VMEM((3, HALF, size), BF16),
            pltpu.SemaphoreType.DMA((6,)),
        ],
        compiler_params=pltpu.CompilerParams(vmem_limit_bytes=10 << 20),
        cost_estimate=pl.CostEstimate(
            flops=1_000_000_000, bytes_accessed=10_000_000, transcendentals=0
        ),
        name="final_start",
    )(place, offsets, mine, *(in_hbm(x) for x in (free, own, mate, near, far)))


def final_body(
    place, offsets, other, early, late, slots, magnon_in, sum_in, table, out, magnon, bottom_sum,
    source, joined, result, sems,
):
    core = place[0]
    ready = pltpu.make_async_copy(other, source, sems.at[4])
    ready.start()
    ready.wait()
    half_products(offsets, 1 - core, source, joined, table, magnon, bottom_sum)
    magnon[0] += bottom_sum[...].astype(BF16).astype(F32)
    _, _, first, last = offset_roles(offsets)
    reach = spans(offsets, first, last)
    stores = []
    for item, energy in enumerate((2 - 2 * core, 3 - 2 * core, 2 * core, 2 * core + 1)):
        born = early if item < 2 else late

        @pl.loop(0, NB // 16)
        def _(block):
            rows = pl.ds(pl.multiple_of(block * 16, 16), 16)
            begin = pl.ds(pl.multiple_of((item % 2) * NB + block * 16, 16), 16)
            real = born[begin, :NB].astype(F32)
            imag = born[begin, NB:].astype(F32)
            for index in range(3):
                down = energy + 4 - reach[index]
                up = energy + 4 + reach[index]
                sr = slots[down, 0, rows, :].astype(F32) + slots[up, 0, rows, :].astype(F32)
                si = slots[down, 1, rows, :].astype(F32) + slots[up, 1, rows, :].astype(F32)
                mr = magnon[index, rows, :NB]
                mi = magnon[index, rows, NB:]
                real += mr * sr - mi * si
                imag += mr * si + mi * sr
            result[item, 0, rows, :] = real.astype(BF16)
            result[item, 1, rows, :] = imag.astype(BF16)

        store = pltpu.make_async_copy(result.at[item], out.at[energy, 0], sems.at[item])
        store.start()
        stores.append(store)
    for store in stores:
        store.wait()


def final_call(place, offsets, other, early, late, slots, magnon, bottom_sum, table):
    size = 2 * NB
    return pl.pallas_call(
        final_body,
        out_shape=(
            jax.ShapeDtypeStruct((4, 1, 2, NB, NB), BF16),
            jax.ShapeDtypeStruct(magnon.shape, F32),
            jax.ShapeDtypeStruct(bottom_sum.shape, F32),
        ),
        in_specs=[SMEM, SMEM, ANY] + [VMEM] * 6,
        out_specs=(ANY, VMEM, VMEM),
        input_output_aliases={6: 1, 7: 2},
        scratch_shapes=[
            pltpu.VMEM((FLAT, 128), BF16),
            pltpu.VMEM((3, HALF, size), BF16),
            pltpu.VMEM((4, 2, NB, NB), BF16),
            pltpu.SemaphoreType.DMA((5,)),
        ],
        compiler_params=pltpu.CompilerParams(vmem_limit_bytes=12 << 20),
        cost_estimate=pl.CostEstimate(
            flops=1_000_000_000, bytes_accessed=18_000_000, transcendentals=0
        ),
        name="final",
    )(place, offsets, other, early, late, slots, magnon, bottom_sum, table)[0]


def per_device(green_blocks, offsets, occupation, coupling, vertex, magnon_free):
    count = lax.axis_size(ENERGY)
    core = lax.axis_index("core").astype(jnp.int32)
    place = core[None]
    own = green_blocks.reshape(4, 2, NB, NB)
    across = [(i, i + 1) for i in range(1, count - 1, 2)]
    across += [(target, source) for source, target in across]
    outer = cut_call(place, own, 0, 2)
    near = lax.ppermute(outer, ENERGY, across)
    mate = lax.ppermute(own, "core", SWAP)
    inner = cut_call(place, own, 2, -2)
    far = lax.ppermute(inner, ENERGY, across)
    slots, turned, partial = prepare_call(place, offsets, own, mate)
    slots, turned, send = polar_send_call(place, offsets, near, slots, turned, partial)
    sent = lax.ppermute(send, "core", SWAP)
    kept = polar_keep_call(place, offsets, slots, turned, partial)
    pair = add_call(kept, sent)
    bands = lax.all_to_all(pair.reshape(BANDS, ROWS, 128), PLANE, 0, 0, tiled=True)
    early = born_call(place, offsets, occupation, coupling, (own, mate, near), vertex)
    copies = sum_call(bands, 4)
    bands = lax.all_to_all(copies, ROW, 0, 0, tiled=True)
    copies = sum_call(bands, BANDS)
    mine = lax.all_to_all(copies, PLANE, 0, 0, tiled=True).reshape(FLAT, 128)
    late = born_call(
        place, offsets, occupation, coupling, (own, mate, near, far), vertex
    )
    other = lax.ppermute(mine, "core", SWAP)
    held = start_call(place, offsets, mine, magnon_free, own, mate, near, far)
    return final_call(place, offsets, other, early, late, *held)


def solution(mesh):
    fine = Mesh(mesh.devices.reshape(4, 2, 2, 2, 4), ("y", "xh", "core", "xl", "z"))
    blocks = P(ENERGY, LAYER, None, None, None)
    placed = (blocks, P(), P(), P(LAYER, None), P(), P())
    return jax.shard_map(
        per_device, mesh=fine, in_specs=placed, out_specs=blocks, check_vma=False
    )
```

```python
import jax
import jax.numpy as jnp
from jax import lax
from jax.experimental import pallas as pl
from jax.experimental.pallas import tpu as pltpu
from jax.sharding import Mesh
from jax.sharding import PartitionSpec as P


NB = 384
HALF = NB // 2
BANDS = 16
ROWS = 18 * HALF // BANDS
FLAT = BANDS * ROWS
F32 = jnp.float32
BF16 = jnp.bfloat16
SWAP = [(0, 1), (1, 0)]
PLANE = ("y", "z")
ROW = ("xh", "xl")
ENERGY = ("y", "xh", "core")
LAYER = ("xl", "z")
ANY = pl.BlockSpec(memory_space=pl.ANY)
SMEM = pl.BlockSpec(memory_space=pltpu.SMEM)
VMEM = pl.BlockSpec(memory_space=pltpu.VMEM)


def in_hbm(array):
    return pltpu.with_memory_space_constraint(array, pltpu.HBM)


def first_index(offsets, value):
    return jnp.where(
        offsets[0] == value, 0, jnp.where(offsets[1] == value, 1, jnp.where(offsets[2] == value, 2, 3))
    )


def offset_roles(offsets):
    top = first_index(offsets, 4)
    bottom = first_index(offsets, -4)
    low = jnp.minimum(top, bottom)
    high = jnp.maximum(top, bottom)
    first = jnp.where(low != 0, 0, jnp.where(high != 1, 1, 2))
    last = jnp.where(high != 3, 3, jnp.where(low != 2, 2, 1))
    return top, bottom, first, last


def spans(offsets, first, last):
    return (jnp.int32(4), jnp.abs(offsets[first]), jnp.abs(offsets[last]))


def cut_body(place, base, sign, own, out, sem):
    copy = pltpu.make_async_copy(own.at[pl.ds(base + sign * place[0], 2)], out, sem)
    copy.start()
    copy.wait()


def cut_call(place, own, base, sign):
    return pl.pallas_call(
        lambda place, own, out, sem: cut_body(place, base, sign, own, out, sem),
        out_shape=jax.ShapeDtypeStruct((2, 2, NB, NB), BF16),
        in_specs=[SMEM, ANY],
        out_specs=VMEM,
        scratch_shapes=[pltpu.SemaphoreType.DMA],
        compiler_params=pltpu.CompilerParams(vmem_limit_bytes=4 << 20),
        cost_estimate=pl.CostEstimate(flops=0, bytes_accessed=2_400_000, transcendentals=0),
    )(place, in_hbm(own))


def edge_body(place, own, same, cross, whole, sems):
    core = place[0]

    @pl.when(core == 1)
    def _():
        copies = [
            pltpu.make_async_copy(own.at[pl.ds(2, 2), :, pl.ds(HALF, HALF), :], same, sems.at[0]),
            pltpu.make_async_copy(own.at[pl.ds(2, 2), :, pl.ds(0, HALF), :], cross, sems.at[1]),
        ]
        for copy in copies:
            copy.start()
        for copy in copies:
            copy.wait()

    @pl.when(core == 0)
    def _():
        copy = pltpu.make_async_copy(own.at[pl.ds(0, 2)], whole, sems.at[0])
        copy.start()
        copy.wait()
        for item in range(2):
            for part in range(2):
                value = whole[item, part].astype(F32).T.astype(BF16)
                same[item, part] = value[:HALF]
                cross[item, part] = value[HALF:]


def edge_call(place, own):
    half = jax.ShapeDtypeStruct((2, 2, HALF, NB), BF16)
    return pl.pallas_call(
        edge_body,
        out_shape=(half, half),
        in_specs=[SMEM, ANY],
        out_specs=(VMEM, VMEM),
        scratch_shapes=[pltpu.VMEM((2, 2, NB, NB), BF16), pltpu.SemaphoreType.DMA((2,))],
        compiler_params=pltpu.CompilerParams(vmem_limit_bytes=6 << 20),
        cost_estimate=pl.CostEstimate(flops=0, bytes_accessed=2_400_000, transcendentals=0),
        name="edge",
    )(place, in_hbm(own))


def prepare_body(place, offsets, own, mate, chip, turned, partial, sems):
    core = place[0]
    copies = [
        pltpu.make_async_copy(own, chip.at[pl.ds(4 * core, 4)], sems.at[0]),
        pltpu.make_async_copy(mate, chip.at[pl.ds(4 - 4 * core, 4)], sems.at[1]),
    ]
    for copy in copies:
        copy.start()
    for copy in copies:
        copy.wait()

    @pl.loop(2, 16)
    def _(step):
        turned[step // 2, step % 2] = chip[step // 2, step % 2].astype(F32).T

    _, _, first, last = offset_roles(offsets)
    for index, span in enumerate(spans(offsets, first, last)):

        @pl.loop(0, HALF // 32)
        def _(block):
            rows = pl.ds(pl.multiple_of(block * 32, 32), 32)
            there = pl.ds(pl.multiple_of(core * HALF + block * 32, 32), 32)

            def step(s, carry):
                real, imag = carry
                ar = chip[s, 0, there, :].astype(F32)
                ai = chip[s, 1, there, :].astype(F32)
                br = turned[s + span, 0, there, :]
                bi = turned[s + span, 1, there, :]
                return real + (ar * br - ai * bi), imag + (ar * bi + ai * br)

            zero = jnp.zeros((32, NB), F32)
            real, imag = lax.fori_loop(0, 8 - span, step, (zero, zero))
            partial[index, 0, rows, :] = real
            partial[index, 1, rows, :] = imag


def prepare_call(place, offsets, own, mate):
    return pl.pallas_call(
        prepare_body,
        out_shape=(
            jax.ShapeDtypeStruct((8, 2, NB, NB), BF16),
            jax.ShapeDtypeStruct((8, 2, NB, NB), F32),
            jax.ShapeDtypeStruct((3, 2, HALF, NB), F32),
        ),
        in_specs=[SMEM, SMEM, ANY, ANY],
        out_specs=(VMEM, VMEM, VMEM),
        scratch_shapes=[pltpu.SemaphoreType.DMA((2,))],
        compiler_params=pltpu.CompilerParams(vmem_limit_bytes=4 << 20),
        cost_estimate=pl.CostEstimate(flops=20_000_000, bytes_accessed=9_000_000, transcendentals=0),
        name="prepare",
    )(place, offsets, own, mate)


def polar_body(place, offsets, same, cross, chip, turned, partial, out, edges, flat, sems):
    core = place[0]
    copies = [
        pltpu.make_async_copy(same, edges.at[1 - core], sems.at[0]),
        pltpu.make_async_copy(cross, edges.at[core], sems.at[1]),
    ]
    for copy in copies:
        copy.start()
    for copy in copies:
        copy.wait()
    _, _, first, last = offset_roles(offsets)
    stores = []
    for index, span in enumerate(spans(offsets, first, last)):

        @pl.loop(0, HALF // 32)
        def _(block):
            rows = pl.ds(pl.multiple_of(block * 32, 32), 32)
            there = pl.ds(pl.multiple_of(core * HALF + block * 32, 32), 32)

            def multiply(carry, ar, ai, br, bi):
                real, imag = carry
                return real + (ar * br - ai * bi), imag + (ar * bi + ai * br)

            def before(j, carry):
                return multiply(
                    carry,
                    edges[0, 1 - j, 0, rows, :].astype(F32),
                    edges[0, 1 - j, 1, rows, :].astype(F32),
                    turned[span - 1 - j, 0, there, :],
                    turned[span - 1 - j, 1, there, :],
                )

            def after(j, carry):
                return multiply(
                    carry,
                    chip[8 - span + j, 0, there, :].astype(F32),
                    chip[8 - span + j, 1, there, :].astype(F32),
                    edges[1, j, 0, rows, :].astype(F32),
                    edges[1, j, 1, rows, :].astype(F32),
                )

            pair = (partial[index, 0, rows, :], partial[index, 1, rows, :])
            pair = lax.fori_loop(0, jnp.maximum(span - 2, 0), before, pair)
            pair = lax.fori_loop(0, jnp.minimum(span, 2), after, pair)
            for part, value in enumerate(pair):
                for panel in range(3):
                    start = ((index * 2 + part) * 3 + panel) * HALF
                    flat[pl.ds(pl.multiple_of(start + block * 32, 32), 32), :] = value[
                        :, panel * 128 : (panel + 1) * 128
                    ].astype(BF16)

        done = pl.ds(index * 6 * HALF, 6 * HALF)
        store = pltpu.make_async_copy(flat.at[done], out.at[done], sems.at[2 + index])
        store.start()
        stores.append(store)
    for store in stores:
        store.wait()


def polar_call(place, offsets, same, cross, chip, turned, partial):
    return pl.pallas_call(
        polar_body,
        out_shape=jax.ShapeDtypeStruct((FLAT, 128), BF16),
        in_specs=[SMEM, SMEM, ANY, ANY, VMEM, VMEM, VMEM],
        out_specs=ANY,
        scratch_shapes=[
            pltpu.VMEM((2, 2, 2, HALF, NB), BF16),
            pltpu.VMEM((FLAT, 128), BF16),
            pltpu.SemaphoreType.DMA((5,)),
        ],
        compiler_params=pltpu.CompilerParams(vmem_limit_bytes=6 << 20),
        cost_estimate=pl.CostEstimate(flops=20_000_000, bytes_accessed=9_000_000, transcendentals=0),
        name="polar",
    )(place, offsets, same, cross, chip, turned, partial)


def near_body(place, swapped, cross, out, sems):
    core = place[0]
    copies = [
        pltpu.make_async_copy(cross, out.at[:, :, pl.ds(core * HALF, HALF), :], sems.at[0]),
        pltpu.make_async_copy(
            swapped, out.at[:, :, pl.ds(HALF - core * HALF, HALF), :], sems.at[1]
        ),
    ]
    for copy in copies:
        copy.start()
    for copy in copies:
        copy.wait()

    @pl.when(core == 1)
    def _():
        for item in range(2):
            for part in range(2):
                out[item, part] = out[item, part].astype(F32).T.astype(BF16)


def near_call(place, swapped, cross):
    return pl.pallas_call(
        near_body,
        out_shape=jax.ShapeDtypeStruct((2, 2, NB, NB), BF16),
        in_specs=[SMEM, ANY, ANY],
        out_specs=VMEM,
        scratch_shapes=[pltpu.SemaphoreType.DMA((2,))],
        compiler_params=pltpu.CompilerParams(vmem_limit_bytes=4 << 20),
        cost_estimate=pl.CostEstimate(flops=0, bytes_accessed=2_400_000, transcendentals=0),
        name="near_join",
    )(place, swapped, cross)


def born_body(early, *refs):
    if early:
        (place, offsets, occupation, coupling, own, mate, near, vertex, out, *rest) = refs
        far = None
    else:
        (place, offsets, occupation, coupling, own, mate, near, far, vertex, out, *rest) = refs
    chosen, lows, highs, mixed, wide, stack, side, total, sems = rest
    core = place[0]
    energy = 2 * (1 - core) if early else 2 * core

    def fetch(slot, target, sem):
        sources = [(own, 4, 4), (mate, 8 - 8 * core, 4), (near, 2 + 6 * core, 2)]
        if far is not None:
            sources.append((far, 10 * core, 2))
        for source, low, size in sources:

            @pl.when((slot >= low) & (slot < low + size))
            def _():
                pltpu.make_async_copy(source.at[slot - low], target, sem).start()

    for k in range(4):
        pltpu.make_async_copy(vertex.at[coupling[0, k]], chosen.at[k], sems.at[k, 4]).start()
        for item in range(2):
            at = energy + 4 + item
            fetch(at - offsets[k], lows.at[k, item], sems.at[k, 2 * item])
            fetch(at + offsets[k], highs.at[k, item], sems.at[k, 2 * item + 1])

    total[...] = jnp.zeros_like(total)

    @pl.loop(0, 4)
    def _(k):
        pltpu.make_async_copy(vertex.at[0], chosen.at[k], sems.at[k, 4]).wait()
        vr = chosen[k, 0]
        vi = chosen[k, 1]
        wide[:NB, :NB] = vr
        wide[:NB, NB:] = -vi
        wide[NB:, :NB] = vi
        wide[NB:, NB:] = vr
        side[:NB, :NB] = vr
        side[:NB, NB:] = vi
        side[NB:, :NB] = -vi
        side[NB:, NB:] = vr
        weight = occupation[k]
        for item in range(2):
            pltpu.make_async_copy(own.at[0], lows.at[k, item], sems.at[k, 2 * item]).wait()
            pltpu.make_async_copy(own.at[0], highs.at[k, item], sems.at[k, 2 * item + 1]).wait()
        for item in range(2):
            for part in range(2):
                low = lows[k, item, part].astype(F32)
                high = highs[k, item, part].astype(F32)
                value = weight * low + (weight + 1.0) * high
                mixed[part * NB : (part + 1) * NB, item * NB : (item + 1) * NB] = value.astype(BF16)
        for piece in range(2):
            begin = piece * 384
            part, row = begin // NB, begin % NB
            half = jnp.dot(
                wide[begin : begin + 384, :], mixed[...], preferred_element_type=F32
            ).astype(BF16)
            for item in range(2):
                stack[item * NB + row : item * NB + row + 384, part * NB : (part + 1) * NB] = half[
                    :, item * NB : (item + 1) * NB
                ]
        for piece in range(2):
            rows = slice(piece * 384, (piece + 1) * 384)
            term = lax.dot_general(
                stack[rows, :], side[...], (((1,), (1,)), ((), ())), preferred_element_type=F32
            )
            total[rows, :] += term

    out[...] = total[...].astype(BF16)


def born_call(place, offsets, occupation, coupling, arrays, vertex):
    early = len(arrays) == 3
    size = 2 * NB
    return pl.pallas_call(
        lambda *refs: born_body(early, *refs),
        out_shape=jax.ShapeDtypeStruct((size, size), BF16),
        in_specs=[SMEM] * 4 + [ANY] * (len(arrays) + 1),
        out_specs=VMEM,
        scratch_shapes=[
            pltpu.VMEM((4, 2, NB, NB), BF16),
            pltpu.VMEM((4, 2, 2, NB, NB), BF16),
            pltpu.VMEM((4, 2, 2, NB, NB), BF16),
            pltpu.VMEM((size, size), BF16),
            pltpu.VMEM((size, size), BF16),
            pltpu.VMEM((size, size), BF16),
            pltpu.VMEM((size, size), BF16),
            pltpu.VMEM((size, size), F32),
            pltpu.SemaphoreType.DMA((4, 5)),
        ],
        compiler_params=pltpu.CompilerParams(vmem_limit_bytes=22 << 20),
        cost_estimate=pl.CostEstimate(
            flops=16 * size**3, bytes_accessed=12_000_000, transcendentals=0
        ),
        name="born_early" if early else "born_late",
    )(place, offsets, occupation, coupling, *map(in_hbm, arrays[:3]), *arrays[3:], in_hbm(vertex))


def sum_body(count, copies, bands, out, buffer, value, *sems):
    loads = [
        pltpu.make_async_copy(bands.at[i], buffer.at[i], sems[0].at[i]) for i in range(count)
    ]
    for load in loads:
        load.start()
    for load in loads:
        load.wait()

    for begin in range(0, ROWS, 64):
        rows = slice(begin, min(begin + 64, ROWS))
        total = buffer[0, rows, :].astype(F32)
        for i in range(1, count):
            total += buffer[i, rows, :].astype(F32)
        value[rows, :] = total.astype(BF16)

    stores = [pltpu.make_async_copy(value, out.at[i], sems[1].at[i]) for i in range(copies)]
    for store in stores:
        store.start()
    for store in stores:
        store.wait()


def sum_call(bands, copies):
    count = bands.shape[0]
    return pl.pallas_call(
        lambda *refs: sum_body(count, copies, *refs),
        out_shape=jax.ShapeDtypeStruct((copies, ROWS, 128), BF16),
        in_specs=[ANY],
        out_specs=ANY,
        scratch_shapes=[
            pltpu.VMEM(bands.shape, BF16),
            pltpu.VMEM((ROWS, 128), BF16),
            pltpu.SemaphoreType.DMA((count,)),
            pltpu.SemaphoreType.DMA((copies,)),
        ],
        compiler_params=pltpu.CompilerParams(vmem_limit_bytes=4 << 20),
        cost_estimate=pl.CostEstimate(flops=500_000, bytes_accessed=1_900_000, transcendentals=0),
    )(bands)


def half_products(begin, offsets, half, source, joined, table, magnon, sums):
    for index in range(3):
        for part in range(2):
            for panel in range(3):
                start = ((index * 2 + part) * 3 + panel) * HALF
                joined[index, :, part * NB + panel * 128 : part * NB + (panel + 1) * 128] = source[
                    start : start + HALF, :
                ]
    top, bottom, first, last = offset_roles(offsets)
    rows = pl.ds(pl.multiple_of(half * HALF, HALF), HALF)

    def direct(index, k):
        value = jnp.dot(joined[index], table[k], preferred_element_type=F32)
        magnon[index, rows, :] = value.astype(BF16).astype(F32)

    def transposed(index, k):
        value = None
        for part in range(2):
            turned = joined[index, :, part * NB : (part + 1) * NB].astype(F32).T.astype(BF16)
            these = pl.ds(pl.multiple_of(part * NB + half * HALF, HALF), HALF)
            term = jnp.dot(turned, table[k, these, :], preferred_element_type=F32)
            value = term if value is None else value + term
        sums[index] = value if begin else sums[index] + value

    direct(0, top)
    transposed(0, bottom)
    for index, k in ((1, first), (2, last)):
        pl.when(offsets[k] > 0)(lambda: direct(index, k))
        pl.when(offsets[k] < 0)(lambda: transposed(index, k))


def start_body(
    place, offsets, mine, free, own, mate,
    slots, magnon, bottom_sum, table, source, plain, joined, sems,
):
    core = place[0]
    ready = [
        pltpu.make_async_copy(mine, source, sems.at[4]),
        pltpu.make_async_copy(free, plain, sems.at[5]),
    ]
    loads = [
        pltpu.make_async_copy(own, slots.at[pl.ds(4, 4)], sems.at[0]),
        pltpu.make_async_copy(mate, slots.at[pl.ds(8 - 8 * core, 4)], sems.at[1]),
    ]
    for load in ready + loads:
        load.start()
    for load in ready:
        load.wait()
    for k in range(4):
        fr = plain[k, 0]
        fi = plain[k, 1]
        table[k, :NB, :NB] = fr
        table[k, :NB, NB:] = fi
        table[k, NB:, :NB] = -fi
        table[k, NB:, NB:] = fr
    half_products(True, offsets, core, source, joined, table, magnon, bottom_sum)
    for load in loads:
        load.wait()


def start_call(place, offsets, mine, free, own, mate):
    size = 2 * NB
    return pl.pallas_call(
        start_body,
        out_shape=(
            jax.ShapeDtypeStruct((12, 2, NB, NB), BF16),
            jax.ShapeDtypeStruct((3, NB, size), F32),
            jax.ShapeDtypeStruct((3, NB, size), F32),
            jax.ShapeDtypeStruct((4, size, size), BF16),
        ),
        in_specs=[SMEM, SMEM] + [ANY] * 4,
        out_specs=(VMEM,) * 4,
        scratch_shapes=[
            pltpu.VMEM((FLAT, 128), BF16),
            pltpu.VMEM((4, 2, NB, NB), BF16),
            pltpu.VMEM((3, HALF, size), BF16),
            pltpu.SemaphoreType.DMA((6,)),
        ],
        compiler_params=pltpu.CompilerParams(vmem_limit_bytes=10 << 20),
        cost_estimate=pl.CostEstimate(
            flops=1_000_000_000, bytes_accessed=10_000_000, transcendentals=0
        ),
        name="final_start",
    )(place, offsets, mine, *(in_hbm(x) for x in (free, own, mate)))


def final_body(
    place, offsets, other, near, far, early, late, slots_in, magnon_in, sum_in, table,
    out, slots, magnon, bottom_sum, source, joined, result, sems,
):
    core = place[0]
    loads = [
        pltpu.make_async_copy(near, slots.at[pl.ds(2 + 6 * core, 2)], sems.at[5]),
        pltpu.make_async_copy(far, slots.at[pl.ds(10 * core, 2)], sems.at[6]),
    ]
    ready = pltpu.make_async_copy(other, source, sems.at[4])
    ready.start()
    for load in loads:
        load.start()
    ready.wait()
    half_products(False, offsets, 1 - core, source, joined, table, magnon, bottom_sum)
    _, _, first, last = offset_roles(offsets)
    magnon[0] += bottom_sum[0].astype(BF16).astype(F32)
    for index, k in ((1, first), (2, last)):

        @pl.when(offsets[k] < 0)
        def _():
            magnon[index] = bottom_sum[index].astype(BF16).astype(F32)

    for load in loads:
        load.wait()
    reach = spans(offsets, first, last)
    stores = []
    for item, energy in enumerate((2 - 2 * core, 3 - 2 * core, 2 * core, 2 * core + 1)):
        born = early if item < 2 else late

        @pl.loop(0, NB // 16)
        def _(block):
            rows = pl.ds(pl.multiple_of(block * 16, 16), 16)
            begin = pl.ds(pl.multiple_of((item % 2) * NB + block * 16, 16), 16)
            real = born[begin, :NB].astype(F32)
            imag = born[begin, NB:].astype(F32)
            for index in range(3):
                down = energy + 4 - reach[index]
                up = energy + 4 + reach[index]
                sr = slots[down, 0, rows, :].astype(F32) + slots[up, 0, rows, :].astype(F32)
                si = slots[down, 1, rows, :].astype(F32) + slots[up, 1, rows, :].astype(F32)
                mr = magnon[index, rows, :NB]
                mi = magnon[index, rows, NB:]
                real += mr * sr - mi * si
                imag += mr * si + mi * sr
            result[item, 0, rows, :] = real.astype(BF16)
            result[item, 1, rows, :] = imag.astype(BF16)

        store = pltpu.make_async_copy(result.at[item], out.at[energy, 0], sems.at[item])
        store.start()
        stores.append(store)
    for store in stores:
        store.wait()


def final_call(place, offsets, other, near, far, early, late, slots, magnon, bottom_sum, table):
    size = 2 * NB
    return pl.pallas_call(
        final_body,
        out_shape=(
            jax.ShapeDtypeStruct((4, 1, 2, NB, NB), BF16),
            jax.ShapeDtypeStruct(slots.shape, BF16),
            jax.ShapeDtypeStruct(magnon.shape, F32),
            jax.ShapeDtypeStruct(bottom_sum.shape, F32),
        ),
        in_specs=[SMEM, SMEM, ANY, ANY, ANY] + [VMEM] * 6,
        out_specs=(ANY, VMEM, VMEM, VMEM),
        input_output_aliases={7: 1, 8: 2, 9: 3},
        scratch_shapes=[
            pltpu.VMEM((FLAT, 128), BF16),
            pltpu.VMEM((3, HALF, size), BF16),
            pltpu.VMEM((4, 2, NB, NB), BF16),
            pltpu.SemaphoreType.DMA((7,)),
        ],
        compiler_params=pltpu.CompilerParams(vmem_limit_bytes=12 << 20),
        cost_estimate=pl.CostEstimate(
            flops=1_000_000_000, bytes_accessed=18_000_000, transcendentals=0
        ),
        name="final",
    )(place, offsets, other, in_hbm(near), in_hbm(far), early, late, slots, magnon, bottom_sum, table)[0]


def per_device(green_blocks, offsets, occupation, coupling, vertex, magnon_free):
    count = lax.axis_size(ENERGY)
    core = lax.axis_index("core").astype(jnp.int32)
    place = core[None]
    own = green_blocks.reshape(4, 2, NB, NB)
    across = [(i, i + 1) for i in range(1, count - 1, 2)]
    across += [(target, source) for source, target in across]
    along = [(i, i + 2) for i in range(1, count - 2, 2)]
    along += [(i + 1, i - 1) for i in range(1, count - 2, 2)]
    to_same, to_cross = edge_call(place, own)
    cross = lax.ppermute(to_cross, ENERGY, across)
    same = lax.ppermute(to_same, ENERGY, along)
    mate = lax.ppermute(own, "core", SWAP)
    inner = cut_call(place, own, 2, -2)
    far = lax.ppermute(inner, ENERGY, across)
    chip, turned, partial = prepare_call(place, offsets, own, mate)
    pair = polar_call(place, offsets, same, cross, chip, turned, partial)
    swapped = lax.ppermute(same, "core", SWAP)
    near = near_call(place, swapped, cross)
    bands = lax.all_to_all(pair.reshape(BANDS, ROWS, 128), PLANE, 0, 0, tiled=True)
    early = born_call(place, offsets, occupation, coupling, (own, mate, near), vertex)
    copies = sum_call(bands, 4)
    bands = lax.all_to_all(copies, ROW, 0, 0, tiled=True)
    copies = sum_call(bands, BANDS)
    mine = lax.all_to_all(copies, PLANE, 0, 0, tiled=True).reshape(FLAT, 128)
    late = born_call(
        place, offsets, occupation, coupling, (own, mate, near, far), vertex
    )
    other = lax.ppermute(mine, "core", SWAP)
    held = start_call(place, offsets, mine, magnon_free, own, mate)
    return final_call(place, offsets, other, near, far, early, late, *held)


def solution(mesh):
    fine = Mesh(mesh.devices.reshape(4, 2, 2, 2, 4), ("y", "xh", "core", "xl", "z"))
    blocks = P(ENERGY, LAYER, None, None, None)
    placed = (blocks, P(), P(), P(LAYER, None), P(), P())
    return jax.shard_map(
        per_device, mesh=fine, in_specs=placed, out_specs=blocks, check_vma=False
    )
```

```python
import jax
import jax.numpy as jnp
from jax import lax
from jax.experimental import pallas as pl
from jax.experimental.pallas import tpu as pltpu
from jax.sharding import Mesh
from jax.sharding import PartitionSpec as P


NB = 384
HALF = NB // 2
BANDS = 16
ROWS = 18 * HALF // BANDS
FLAT = BANDS * ROWS
F32 = jnp.float32
BF16 = jnp.bfloat16
SWAP = [(0, 1), (1, 0)]
PLANE = ("y", "z")
ROW = ("xh", "xl")
ENERGY = ("y", "xh", "core")
LAYER = ("xl", "z")
ANY = pl.BlockSpec(memory_space=pl.ANY)
SMEM = pl.BlockSpec(memory_space=pltpu.SMEM)
VMEM = pl.BlockSpec(memory_space=pltpu.VMEM)


def in_hbm(array):
    return pltpu.with_memory_space_constraint(array, pltpu.HBM)


def first_index(offsets, value):
    return jnp.where(
        offsets[0] == value, 0, jnp.where(offsets[1] == value, 1, jnp.where(offsets[2] == value, 2, 3))
    )


def offset_roles(offsets):
    top = first_index(offsets, 4)
    bottom = first_index(offsets, -4)
    low = jnp.minimum(top, bottom)
    high = jnp.maximum(top, bottom)
    first = jnp.where(low != 0, 0, jnp.where(high != 1, 1, 2))
    last = jnp.where(high != 3, 3, jnp.where(low != 2, 2, 1))
    return top, bottom, first, last


def spans(offsets, first, last):
    return (jnp.int32(4), jnp.abs(offsets[first]), jnp.abs(offsets[last]))


def cut_body(place, base, sign, own, out, sem):
    copy = pltpu.make_async_copy(own.at[pl.ds(base + sign * place[0], 2)], out, sem)
    copy.start()
    copy.wait()


def cut_call(place, own, base, sign):
    return pl.pallas_call(
        lambda place, own, out, sem: cut_body(place, base, sign, own, out, sem),
        out_shape=jax.ShapeDtypeStruct((2, 2, NB, NB), BF16),
        in_specs=[SMEM, ANY],
        out_specs=VMEM,
        scratch_shapes=[pltpu.SemaphoreType.DMA],
        compiler_params=pltpu.CompilerParams(vmem_limit_bytes=4 << 20),
        cost_estimate=pl.CostEstimate(flops=0, bytes_accessed=2_400_000, transcendentals=0),
    )(place, in_hbm(own))


def edge_body(place, own, same, cross, whole, sems):
    core = place[0]

    @pl.when(core == 1)
    def _():
        copies = [
            pltpu.make_async_copy(own.at[pl.ds(2, 2), :, pl.ds(HALF, HALF), :], same, sems.at[0]),
            pltpu.make_async_copy(own.at[pl.ds(2, 2), :, pl.ds(0, HALF), :], cross, sems.at[1]),
        ]
        for copy in copies:
            copy.start()
        for copy in copies:
            copy.wait()

    @pl.when(core == 0)
    def _():
        copy = pltpu.make_async_copy(own.at[pl.ds(0, 2)], whole, sems.at[0])
        copy.start()
        copy.wait()
        for item in range(2):
            for part in range(2):
                value = whole[item, part].astype(F32).T.astype(BF16)
                same[item, part] = value[:HALF]
                cross[item, part] = value[HALF:]


def edge_call(place, own):
    half = jax.ShapeDtypeStruct((2, 2, HALF, NB), BF16)
    return pl.pallas_call(
        edge_body,
        out_shape=(half, half),
        in_specs=[SMEM, ANY],
        out_specs=(VMEM, VMEM),
        scratch_shapes=[pltpu.VMEM((2, 2, NB, NB), BF16), pltpu.SemaphoreType.DMA((2,))],
        compiler_params=pltpu.CompilerParams(vmem_limit_bytes=6 << 20),
        cost_estimate=pl.CostEstimate(flops=0, bytes_accessed=2_400_000, transcendentals=0),
        name="edge",
    )(place, in_hbm(own))


def prepare_body(place, offsets, own, mate, chip, turned, partial, sems):
    core = place[0]
    copies = [
        pltpu.make_async_copy(own, chip.at[pl.ds(4 * core, 4)], sems.at[0]),
        pltpu.make_async_copy(mate, chip.at[pl.ds(4 - 4 * core, 4)], sems.at[1]),
    ]
    for copy in copies:
        copy.start()
    for copy in copies:
        copy.wait()

    @pl.loop(2, 16)
    def _(step):
        turned[step // 2, step % 2] = chip[step // 2, step % 2].astype(F32).T

    _, _, first, last = offset_roles(offsets)
    for index, span in enumerate(spans(offsets, first, last)):

        @pl.loop(0, HALF // 32)
        def _(block):
            rows = pl.ds(pl.multiple_of(block * 32, 32), 32)
            there = pl.ds(pl.multiple_of(core * HALF + block * 32, 32), 32)

            def step(s, carry):
                real, imag = carry
                ar = chip[s, 0, there, :].astype(F32)
                ai = chip[s, 1, there, :].astype(F32)
                br = turned[s + span, 0, there, :]
                bi = turned[s + span, 1, there, :]
                return real + (ar * br - ai * bi), imag + (ar * bi + ai * br)

            zero = jnp.zeros((32, NB), F32)
            real, imag = lax.fori_loop(0, 8 - span, step, (zero, zero))
            partial[index, 0, rows, :] = real
            partial[index, 1, rows, :] = imag


def prepare_call(place, offsets, own, mate):
    return pl.pallas_call(
        prepare_body,
        out_shape=(
            jax.ShapeDtypeStruct((8, 2, NB, NB), BF16),
            jax.ShapeDtypeStruct((8, 2, NB, NB), F32),
            jax.ShapeDtypeStruct((3, 2, HALF, NB), F32),
        ),
        in_specs=[SMEM, SMEM, ANY, ANY],
        out_specs=(VMEM, VMEM, VMEM),
        scratch_shapes=[pltpu.SemaphoreType.DMA((2,))],
        compiler_params=pltpu.CompilerParams(vmem_limit_bytes=4 << 20),
        cost_estimate=pl.CostEstimate(flops=20_000_000, bytes_accessed=9_000_000, transcendentals=0),
        name="prepare",
    )(place, offsets, own, mate)


def polar_body(place, offsets, same, cross, chip, turned, partial, out, flat, sems):
    core = place[0]

    def run(edges):
        _, _, first, last = offset_roles(offsets)
        for index, span in enumerate(spans(offsets, first, last)):

            @pl.loop(0, HALF // 32)
            def _(block):
                rows = pl.ds(pl.multiple_of(block * 32, 32), 32)
                there = pl.ds(pl.multiple_of(core * HALF + block * 32, 32), 32)

                def multiply(carry, ar, ai, br, bi):
                    real, imag = carry
                    return real + (ar * br - ai * bi), imag + (ar * bi + ai * br)

                def before(j, carry):
                    ar = edges[0][1 - j, 0, rows, :].astype(F32)
                    ai = edges[0][1 - j, 1, rows, :].astype(F32)
                    if index > 0:
                        keep = jnp.where(span > 2 + j, 1.0, 0.0)
                        ar, ai = ar * keep, ai * keep
                    at = jnp.maximum(span - 1 - j, 1)
                    return multiply(carry, ar, ai, turned[at, 0, there, :], turned[at, 1, there, :])

                def after(j, carry):
                    at = jnp.minimum(8 - span + j, 7)
                    ar = chip[at, 0, there, :].astype(F32)
                    ai = chip[at, 1, there, :].astype(F32)
                    if index > 0 and j > 0:
                        keep = jnp.where(span > j, 1.0, 0.0)
                        ar, ai = ar * keep, ai * keep
                    return multiply(
                        carry,
                        ar,
                        ai,
                        edges[1][j, 0, rows, :].astype(F32),
                        edges[1][j, 1, rows, :].astype(F32),
                    )

                pair = (partial[index, 0, rows, :], partial[index, 1, rows, :])
                for j in range(2):
                    pair = before(j, pair)
                for j in range(2):
                    pair = after(j, pair)
                for part, value in enumerate(pair):
                    for panel in range(3):
                        start = ((index * 2 + part) * 3 + panel) * HALF
                        flat[pl.ds(pl.multiple_of(start + block * 32, 32), 32), :] = value[
                            :, panel * 128 : (panel + 1) * 128
                        ].astype(BF16)

            done = pl.ds(index * 6 * HALF, 6 * HALF)
            store = pltpu.make_async_copy(flat.at[done], out.at[done], sems.at[index])
            store.start()

    @pl.when(core == 0)
    def _():
        run((cross, same))

    @pl.when(core == 1)
    def _():
        run((same, cross))

    for index in range(3):
        done = pl.ds(index * 6 * HALF, 6 * HALF)
        pltpu.make_async_copy(flat.at[done], out.at[done], sems.at[index]).wait()


def polar_call(place, offsets, same, cross, chip, turned, partial):
    return pl.pallas_call(
        polar_body,
        out_shape=pltpu.HBM((FLAT, 128), BF16),
        in_specs=[SMEM, SMEM, VMEM, VMEM, VMEM, VMEM, VMEM],
        out_specs=ANY,
        scratch_shapes=[
            pltpu.VMEM((FLAT, 128), BF16),
            pltpu.SemaphoreType.DMA((3,)),
        ],
        compiler_params=pltpu.CompilerParams(vmem_limit_bytes=6 << 20),
        cost_estimate=pl.CostEstimate(flops=20_000_000, bytes_accessed=9_000_000, transcendentals=0),
        name="polar",
    )(place, offsets, same, cross, chip, turned, partial)


def near_body(place, swapped, cross, target, out, sems):
    core = place[0]
    copies = [
        pltpu.make_async_copy(cross, out.at[:, :, pl.ds(core * HALF, HALF), :], sems.at[0]),
        pltpu.make_async_copy(
            swapped, out.at[:, :, pl.ds(HALF - core * HALF, HALF), :], sems.at[1]
        ),
    ]
    for copy in copies:
        copy.start()
    for copy in copies:
        copy.wait()

    @pl.when(core == 1)
    def _():
        for item in range(2):
            for part in range(2):
                out[item, part] = out[item, part].astype(F32).T.astype(BF16)

    store = pltpu.make_async_copy(out, target, sems.at[0])
    store.start()
    store.wait()


def near_call(place, swapped, cross):
    return pl.pallas_call(
        near_body,
        out_shape=pltpu.HBM((2, 2, NB, NB), BF16),
        in_specs=[SMEM, ANY, ANY],
        out_specs=ANY,
        scratch_shapes=[pltpu.VMEM((2, 2, NB, NB), BF16), pltpu.SemaphoreType.DMA((2,))],
        compiler_params=pltpu.CompilerParams(vmem_limit_bytes=4 << 20),
        cost_estimate=pl.CostEstimate(flops=0, bytes_accessed=2_400_000, transcendentals=0),
        name="near_join",
    )(place, swapped, in_hbm(cross))


def born_body(early, window, resumed, *refs):
    refs = list(refs)
    place, offsets, occupation, coupling, own, mate, near = refs[:7]
    refs = refs[7:]
    far = None if early else refs.pop(0)
    base = refs.pop(0) if resumed else None
    vertex, out, chosen, lows, highs, mixed, wide, stack, side, total, rounded, sems = refs
    core = place[0]
    energy = 2 * (1 - core) if early else 2 * core

    def fetch(slot, target, sem):
        sources = [(own, 4, 4), (mate, 8 - 8 * core, 4), (near, 2 + 6 * core, 2)]
        if far is not None:
            sources.append((far, 10 * core, 2))
        for source, low, size in sources:

            @pl.when((slot >= low) & (slot < low + size))
            def _():
                pltpu.make_async_copy(source.at[slot - low], target, sem).start()

    for k in range(*window):
        pltpu.make_async_copy(vertex.at[coupling[0, k]], chosen.at[k], sems.at[k, 4]).start()
        for item in range(2):
            at = energy + 4 + item
            fetch(at - offsets[k], lows.at[k, item], sems.at[k, 2 * item])
            fetch(at + offsets[k], highs.at[k, item], sems.at[k, 2 * item + 1])

    if resumed:
        resume = pltpu.make_async_copy(base, total, sems.at[0, 0])
        resume.start()
        resume.wait()
    else:
        total[...] = jnp.zeros_like(total)

    @pl.loop(*window)
    def _(k):
        pltpu.make_async_copy(vertex.at[0], chosen.at[k], sems.at[k, 4]).wait()
        vr = chosen[k, 0]
        vi = chosen[k, 1]
        wide[:NB, :NB] = vr
        wide[:NB, NB:] = -vi
        wide[NB:, :NB] = vi
        wide[NB:, NB:] = vr
        side[:NB, :NB] = vr
        side[:NB, NB:] = vi
        side[NB:, :NB] = -vi
        side[NB:, NB:] = vr
        weight = occupation[k]
        for item in range(2):
            pltpu.make_async_copy(own.at[0], lows.at[k, item], sems.at[k, 2 * item]).wait()
            pltpu.make_async_copy(own.at[0], highs.at[k, item], sems.at[k, 2 * item + 1]).wait()
        for item in range(2):
            for part in range(2):
                low = lows[k, item, part].astype(F32)
                high = highs[k, item, part].astype(F32)
                value = weight * low + (weight + 1.0) * high
                mixed[part * NB : (part + 1) * NB, item * NB : (item + 1) * NB] = value.astype(BF16)
        for piece in range(2):
            begin = piece * 384
            part, row = begin // NB, begin % NB
            half = jnp.dot(
                wide[begin : begin + 384, :], mixed[...], preferred_element_type=F32
            ).astype(BF16)
            for item in range(2):
                stack[item * NB + row : item * NB + row + 384, part * NB : (part + 1) * NB] = half[
                    :, item * NB : (item + 1) * NB
                ]
        for piece in range(2):
            rows = slice(piece * 384, (piece + 1) * 384)
            term = lax.dot_general(
                stack[rows, :], side[...], (((1,), (1,)), ((), ())), preferred_element_type=F32
            )
            total[rows, :] += term

    if out.dtype == BF16:
        rounded[...] = total[...].astype(BF16)
    store = pltpu.make_async_copy(rounded if out.dtype == BF16 else total, out, sems.at[0, 0])
    store.start()
    store.wait()


def born_call(place, offsets, occupation, coupling, arrays, vertex, window, base=None, kind=BF16):
    early = len(arrays) == 3
    resumed = base is not None
    size = 2 * NB
    held = (*map(in_hbm, arrays[:3]), *arrays[3:]) + ((in_hbm(base),) if resumed else ())
    part = window[1] - window[0]
    return pl.pallas_call(
        lambda *refs: born_body(early, window, resumed, *refs),
        out_shape=pltpu.HBM((size, size), kind),
        in_specs=[SMEM] * 4 + [ANY] * (len(held) + 1),
        out_specs=ANY,
        scratch_shapes=[
            pltpu.VMEM((4, 2, NB, NB), BF16),
            pltpu.VMEM((4, 2, 2, NB, NB), BF16),
            pltpu.VMEM((4, 2, 2, NB, NB), BF16),
            pltpu.VMEM((size, size), BF16),
            pltpu.VMEM((size, size), BF16),
            pltpu.VMEM((size, size), BF16),
            pltpu.VMEM((size, size), BF16),
            pltpu.VMEM((size, size), F32),
            pltpu.VMEM((size, size), BF16),
            pltpu.SemaphoreType.DMA((4, 5)),
        ],
        compiler_params=pltpu.CompilerParams(vmem_limit_bytes=22 << 20),
        cost_estimate=pl.CostEstimate(
            flops=4 * part * size**3, bytes_accessed=3_000_000 * part, transcendentals=0
        ),
        name="born_early" if early else "born_resumed" if resumed else "born_late",
    )(place, offsets, occupation, coupling, *held, in_hbm(vertex))


def sum_body(count, copies, bands, out, buffer, value, *sems):
    loads = [
        pltpu.make_async_copy(bands.at[i], buffer.at[i], sems[0].at[i]) for i in range(count)
    ]
    for load in loads:
        load.start()
    for load in loads:
        load.wait()

    for begin in range(0, ROWS, 64):
        rows = slice(begin, min(begin + 64, ROWS))
        total = buffer[0, rows, :].astype(F32)
        for i in range(1, count):
            total += buffer[i, rows, :].astype(F32)
        value[rows, :] = total.astype(BF16)

    stores = [pltpu.make_async_copy(value, out.at[i], sems[1].at[i]) for i in range(copies)]
    for store in stores:
        store.start()
    for store in stores:
        store.wait()


def sum_call(bands, copies):
    count = bands.shape[0]
    return pl.pallas_call(
        lambda *refs: sum_body(count, copies, *refs),
        out_shape=pltpu.HBM((copies, ROWS, 128), BF16),
        in_specs=[ANY],
        out_specs=ANY,
        scratch_shapes=[
            pltpu.VMEM(bands.shape, BF16),
            pltpu.VMEM((ROWS, 128), BF16),
            pltpu.SemaphoreType.DMA((count,)),
            pltpu.SemaphoreType.DMA((copies,)),
        ],
        compiler_params=pltpu.CompilerParams(vmem_limit_bytes=4 << 20),
        cost_estimate=pl.CostEstimate(flops=500_000, bytes_accessed=1_900_000, transcendentals=0),
    )(bands)


def unpack_half(source, joined):
    for index in range(3):
        for part in range(2):
            for panel in range(3):
                start = ((index * 2 + part) * 3 + panel) * HALF
                joined[index, :, part * NB + panel * 128 : part * NB + (panel + 1) * 128] = source[
                    start : start + HALF, :
                ]


def direct(index, role, half, joined, table, magnon):
    rows = pl.ds(pl.multiple_of(half * HALF, HALF), HALF)
    value = jnp.dot(joined[index], table[role], preferred_element_type=F32)
    magnon[index, rows, :] = value.astype(BF16).astype(F32)


def transposed(index, role, half, joined, table):
    value = None
    for part in range(2):
        turned = joined[index, :, part * NB : (part + 1) * NB].astype(F32).T.astype(BF16)
        these = pl.ds(pl.multiple_of(part * NB + half * HALF, HALF), HALF)
        term = jnp.dot(turned, table[role, these, :], preferred_element_type=F32)
        value = term if value is None else value + term
    return value


def start_body(
    place, offsets, mine, free, own, mate,
    slots, magnon, sums, table, source, plain, joined, sems,
):
    core = place[0]
    roles = offset_roles(offsets)
    ready = pltpu.make_async_copy(mine, source, sems.at[6])
    tables = [
        pltpu.make_async_copy(free.at[k], plain.at[role], sems.at[role])
        for role, k in enumerate(roles)
    ]
    loads = [
        pltpu.make_async_copy(own, slots.at[pl.ds(4, 4)], sems.at[4]),
        pltpu.make_async_copy(mate, slots.at[pl.ds(8 - 8 * core, 4)], sems.at[5]),
    ]
    for load in [ready] + tables + loads:
        load.start()
    ready.wait()
    unpack_half(source, joined)
    for role in range(4):
        tables[role].wait()
        fr = plain[role, 0]
        fi = plain[role, 1]
        table[role, :NB, :NB] = fr
        table[role, :NB, NB:] = fi
        table[role, NB:, :NB] = -fi
        table[role, NB:, NB:] = fr
        if role == 0:
            direct(0, 0, core, joined, table, magnon)
        elif role == 1:
            sums[0] = transposed(0, 1, core, joined, table)
        else:

            @pl.when(offsets[roles[role]] > 0)
            def _():
                direct(role - 1, role, core, joined, table, magnon)

            @pl.when(offsets[roles[role]] < 0)
            def _():
                sums[role - 1] = transposed(role - 1, role, core, joined, table)

    for load in loads:
        load.wait()


def start_call(place, offsets, mine, free, own, mate):
    size = 2 * NB
    return pl.pallas_call(
        start_body,
        out_shape=(
            jax.ShapeDtypeStruct((12, 2, NB, NB), BF16),
            jax.ShapeDtypeStruct((3, NB, size), F32),
            jax.ShapeDtypeStruct((3, NB, size), F32),
            jax.ShapeDtypeStruct((4, size, size), BF16),
        ),
        in_specs=[SMEM, SMEM] + [ANY] * 4,
        out_specs=(VMEM,) * 4,
        scratch_shapes=[
            pltpu.VMEM((FLAT, 128), BF16),
            pltpu.VMEM((4, 2, NB, NB), BF16),
            pltpu.VMEM((3, HALF, size), BF16),
            pltpu.SemaphoreType.DMA((7,)),
        ],
        compiler_params=pltpu.CompilerParams(vmem_limit_bytes=10 << 20),
        cost_estimate=pl.CostEstimate(
            flops=1_000_000_000, bytes_accessed=10_000_000, transcendentals=0
        ),
        name="final_start",
    )(place, offsets, mine, *(in_hbm(x) for x in (free, own, mate)))


def final_body(
    place, offsets, other, near, far, early, late, slots_in, magnon_in, sums, table,
    out, slots, magnon, source, joined, result, sems,
):
    core = place[0]
    loads = [
        pltpu.make_async_copy(near, slots.at[pl.ds(2 + 6 * core, 2)], sems.at[5]),
        pltpu.make_async_copy(far, slots.at[pl.ds(10 * core, 2)], sems.at[6]),
    ]
    ready = pltpu.make_async_copy(other, source, sems.at[4])
    ready.start()
    for load in loads:
        load.start()
    ready.wait()
    unpack_half(source, joined)
    roles = offset_roles(offsets)
    _, _, first, last = roles
    half = 1 - core
    direct(0, 0, half, joined, table, magnon)
    total = sums[0] + transposed(0, 1, half, joined, table)
    magnon[0] += total.astype(BF16).astype(F32)
    for role in (2, 3):

        @pl.when(offsets[roles[role]] > 0)
        def _():
            direct(role - 1, role, half, joined, table, magnon)

        @pl.when(offsets[roles[role]] < 0)
        def _():
            total = sums[role - 1] + transposed(role - 1, role, half, joined, table)
            magnon[role - 1] = total.astype(BF16).astype(F32)

    for load in loads:
        load.wait()
    reach = spans(offsets, first, last)
    stores = []
    for item, energy in enumerate((2 - 2 * core, 3 - 2 * core, 2 * core, 2 * core + 1)):
        born = early if item < 2 else late

        @pl.loop(0, NB // 32)
        def _(block):
            rows = pl.ds(pl.multiple_of(block * 32, 32), 32)
            begin = pl.ds(pl.multiple_of((item % 2) * NB + block * 32, 32), 32)
            real = born[begin, :NB].astype(F32)
            imag = born[begin, NB:].astype(F32)
            for index in range(3):
                down = energy + 4 - reach[index]
                up = energy + 4 + reach[index]
                sr = slots[down, 0, rows, :].astype(F32) + slots[up, 0, rows, :].astype(F32)
                si = slots[down, 1, rows, :].astype(F32) + slots[up, 1, rows, :].astype(F32)
                mr = magnon[index, rows, :NB]
                mi = magnon[index, rows, NB:]
                real += mr * sr - mi * si
                imag += mr * si + mi * sr
            result[item, 0, rows, :] = real.astype(BF16)
            result[item, 1, rows, :] = imag.astype(BF16)

        store = pltpu.make_async_copy(result.at[item], out.at[energy, 0], sems.at[item])
        store.start()
        stores.append(store)
    for store in stores:
        store.wait()


def final_call(place, offsets, other, near, far, early, late, slots, magnon, sums, table):
    size = 2 * NB
    return pl.pallas_call(
        final_body,
        out_shape=(
            jax.ShapeDtypeStruct((4, 1, 2, NB, NB), BF16),
            jax.ShapeDtypeStruct(slots.shape, BF16),
            jax.ShapeDtypeStruct(magnon.shape, F32),
        ),
        in_specs=[SMEM, SMEM, ANY, ANY, ANY] + [VMEM] * 6,
        out_specs=(ANY, VMEM, VMEM),
        input_output_aliases={7: 1, 8: 2},
        scratch_shapes=[
            pltpu.VMEM((FLAT, 128), BF16),
            pltpu.VMEM((3, HALF, size), BF16),
            pltpu.VMEM((4, 2, NB, NB), BF16),
            pltpu.SemaphoreType.DMA((7,)),
        ],
        compiler_params=pltpu.CompilerParams(vmem_limit_bytes=12 << 20),
        cost_estimate=pl.CostEstimate(
            flops=1_000_000_000, bytes_accessed=18_000_000, transcendentals=0
        ),
        name="final",
    )(place, offsets, other, in_hbm(near), in_hbm(far), early, late, slots, magnon, sums, table)[0]


def per_device(green_blocks, offsets, occupation, coupling, vertex, magnon_free):
    count = lax.axis_size(ENERGY)
    core = lax.axis_index("core").astype(jnp.int32)
    place = core[None]
    own = green_blocks.reshape(4, 2, NB, NB)
    across = [(i, i + 1) for i in range(1, count - 1, 2)]
    across += [(target, source) for source, target in across]
    along = [(i, i + 2) for i in range(1, count - 2, 2)]
    along += [(i + 1, i - 1) for i in range(1, count - 2, 2)]
    to_same, to_cross = edge_call(place, own)
    cross = lax.ppermute(to_cross, ENERGY, across)
    same = lax.ppermute(to_same, ENERGY, along)
    mate = lax.ppermute(own, "core", SWAP)
    inner = cut_call(place, own, 2, -2)
    far = lax.ppermute(inner, ENERGY, across)
    chip, turned, partial = prepare_call(place, offsets, own, mate)
    pair = polar_call(place, offsets, same, cross, chip, turned, partial)
    swapped = lax.ppermute(same, "core", SWAP)
    near = near_call(place, swapped, cross)
    bands = lax.all_to_all(pair.reshape(BANDS, ROWS, 128), PLANE, 0, 0, tiled=True)
    early = born_call(place, offsets, occupation, coupling, (own, mate, near), vertex, (0, 4))
    copies = sum_call(bands, 4)
    bands = lax.all_to_all(copies, ROW, 0, 0, tiled=True)
    base = born_call(
        place, offsets, occupation, coupling, (own, mate, near, far), vertex, (0, 1), None, F32
    )
    copies = sum_call(bands, BANDS)
    mine = lax.all_to_all(copies, PLANE, 0, 0, tiled=True).reshape(FLAT, 128)
    late = born_call(
        place, offsets, occupation, coupling, (own, mate, near, far), vertex, (1, 4), base
    )
    other = lax.ppermute(mine, "core", SWAP)
    held = start_call(place, offsets, mine, magnon_free, own, mate)
    return final_call(place, offsets, other, near, far, early, late, *held)


def solution(mesh):
    fine = Mesh(mesh.devices.reshape(4, 2, 2, 2, 4), ("y", "xh", "core", "xl", "z"))
    blocks = P(ENERGY, LAYER, None, None, None)
    placed = (blocks, P(), P(), P(LAYER, None), P(), P())
    return jax.shard_map(
        per_device, mesh=fine, in_specs=placed, out_specs=blocks, check_vma=False
    )
```

```python
import jax
import jax.numpy as jnp
from jax import lax
from jax.experimental import pallas as pl
from jax.experimental.pallas import tpu as pltpu
from jax.sharding import Mesh
from jax.sharding import PartitionSpec as P


NB = 384
HALF = NB // 2
BANDS = 16
ROWS = 18 * HALF // BANDS
FLAT = BANDS * ROWS
F32 = jnp.float32
BF16 = jnp.bfloat16
SWAP = [(0, 1), (1, 0)]
PLANE = ("y", "z")
ROW = ("xh", "xl")
ENERGY = ("y", "xh", "core")
LAYER = ("xl", "z")
ANY = pl.BlockSpec(memory_space=pl.ANY)
SMEM = pl.BlockSpec(memory_space=pltpu.SMEM)
VMEM = pl.BlockSpec(memory_space=pltpu.VMEM)


def in_hbm(array):
    return pltpu.with_memory_space_constraint(array, pltpu.HBM)


def first_index(offsets, value):
    return jnp.where(
        offsets[0] == value, 0, jnp.where(offsets[1] == value, 1, jnp.where(offsets[2] == value, 2, 3))
    )


def offset_roles(offsets):
    top = first_index(offsets, 4)
    bottom = first_index(offsets, -4)
    low = jnp.minimum(top, bottom)
    high = jnp.maximum(top, bottom)
    first = jnp.where(low != 0, 0, jnp.where(high != 1, 1, 2))
    last = jnp.where(high != 3, 3, jnp.where(low != 2, 2, 1))
    return top, bottom, first, last


def spans(offsets, first, last):
    return (jnp.int32(4), jnp.abs(offsets[first]), jnp.abs(offsets[last]))


def cut_body(place, base, sign, own, out, sem):
    copy = pltpu.make_async_copy(own.at[pl.ds(base + sign * place[0], 2)], out, sem)
    copy.start()
    copy.wait()


def cut_call(place, own, base, sign):
    return pl.pallas_call(
        lambda place, own, out, sem: cut_body(place, base, sign, own, out, sem),
        out_shape=jax.ShapeDtypeStruct((2, 2, NB, NB), BF16),
        in_specs=[SMEM, ANY],
        out_specs=VMEM,
        scratch_shapes=[pltpu.SemaphoreType.DMA],
        compiler_params=pltpu.CompilerParams(vmem_limit_bytes=4 << 20),
        cost_estimate=pl.CostEstimate(flops=0, bytes_accessed=2_400_000, transcendentals=0),
    )(place, in_hbm(own))


def edge_body(place, own, same, cross, whole, sems):
    core = place[0]

    @pl.when(core == 1)
    def _():
        copies = [
            pltpu.make_async_copy(own.at[pl.ds(2, 2), :, pl.ds(HALF, HALF), :], same, sems.at[0]),
            pltpu.make_async_copy(own.at[pl.ds(2, 2), :, pl.ds(0, HALF), :], cross, sems.at[1]),
        ]
        for copy in copies:
            copy.start()
        for copy in copies:
            copy.wait()

    @pl.when(core == 0)
    def _():
        copy = pltpu.make_async_copy(own.at[pl.ds(0, 2)], whole, sems.at[0])
        copy.start()
        copy.wait()
        for item in range(2):
            for part in range(2):
                value = whole[item, part].astype(F32).T.astype(BF16)
                same[item, part] = value[:HALF]
                cross[item, part] = value[HALF:]


def edge_call(place, own):
    half = jax.ShapeDtypeStruct((2, 2, HALF, NB), BF16)
    return pl.pallas_call(
        edge_body,
        out_shape=(half, half),
        in_specs=[SMEM, ANY],
        out_specs=(VMEM, VMEM),
        scratch_shapes=[pltpu.VMEM((2, 2, NB, NB), BF16), pltpu.SemaphoreType.DMA((2,))],
        compiler_params=pltpu.CompilerParams(vmem_limit_bytes=6 << 20),
        cost_estimate=pl.CostEstimate(flops=0, bytes_accessed=2_400_000, transcendentals=0),
        name="edge",
    )(place, in_hbm(own))


def prepare_body(place, offsets, own, mate, chip, turned, partial, sems):
    core = place[0]
    copies = [
        pltpu.make_async_copy(own, chip.at[pl.ds(4 * core, 4)], sems.at[0]),
        pltpu.make_async_copy(mate, chip.at[pl.ds(4 - 4 * core, 4)], sems.at[1]),
    ]
    for copy in copies:
        copy.start()
    for copy in copies:
        copy.wait()

    @pl.loop(2, 16)
    def _(step):
        turned[step // 2, step % 2] = chip[step // 2, step % 2].astype(F32).T

    _, _, first, last = offset_roles(offsets)
    for index, span in enumerate(spans(offsets, first, last)):

        @pl.loop(0, HALF // 32)
        def _(block):
            rows = pl.ds(pl.multiple_of(block * 32, 32), 32)
            there = pl.ds(pl.multiple_of(core * HALF + block * 32, 32), 32)

            def step(s, carry):
                real, imag = carry
                ar = chip[s, 0, there, :].astype(F32)
                ai = chip[s, 1, there, :].astype(F32)
                br = turned[s + span, 0, there, :]
                bi = turned[s + span, 1, there, :]
                return real + (ar * br - ai * bi), imag + (ar * bi + ai * br)

            zero = jnp.zeros((32, NB), F32)
            real, imag = lax.fori_loop(0, 8 - span, step, (zero, zero))
            partial[index, 0, rows, :] = real
            partial[index, 1, rows, :] = imag


def prepare_call(place, offsets, own, mate):
    return pl.pallas_call(
        prepare_body,
        out_shape=(
            jax.ShapeDtypeStruct((8, 2, NB, NB), BF16),
            jax.ShapeDtypeStruct((8, 2, NB, NB), F32),
            jax.ShapeDtypeStruct((3, 2, HALF, NB), F32),
        ),
        in_specs=[SMEM, SMEM, ANY, ANY],
        out_specs=(VMEM, VMEM, VMEM),
        scratch_shapes=[pltpu.SemaphoreType.DMA((2,))],
        compiler_params=pltpu.CompilerParams(vmem_limit_bytes=4 << 20),
        cost_estimate=pl.CostEstimate(flops=20_000_000, bytes_accessed=9_000_000, transcendentals=0),
        name="prepare",
    )(place, offsets, own, mate)


def polar_body(place, offsets, same, cross, chip, turned, partial, out, flat, sems):
    core = place[0]

    def run(edges):
        _, _, first, last = offset_roles(offsets)
        for index, span in enumerate(spans(offsets, first, last)):

            @pl.loop(0, HALF // 32)
            def _(block):
                rows = pl.ds(pl.multiple_of(block * 32, 32), 32)
                there = pl.ds(pl.multiple_of(core * HALF + block * 32, 32), 32)

                def multiply(carry, ar, ai, br, bi):
                    real, imag = carry
                    return real + (ar * br - ai * bi), imag + (ar * bi + ai * br)

                def before(j, carry):
                    ar = edges[0][1 - j, 0, rows, :].astype(F32)
                    ai = edges[0][1 - j, 1, rows, :].astype(F32)
                    if index > 0:
                        keep = jnp.where(span > 2 + j, 1.0, 0.0)
                        ar, ai = ar * keep, ai * keep
                    at = jnp.maximum(span - 1 - j, 1)
                    return multiply(carry, ar, ai, turned[at, 0, there, :], turned[at, 1, there, :])

                def after(j, carry):
                    at = jnp.minimum(8 - span + j, 7)
                    ar = chip[at, 0, there, :].astype(F32)
                    ai = chip[at, 1, there, :].astype(F32)
                    if index > 0 and j > 0:
                        keep = jnp.where(span > j, 1.0, 0.0)
                        ar, ai = ar * keep, ai * keep
                    return multiply(
                        carry,
                        ar,
                        ai,
                        edges[1][j, 0, rows, :].astype(F32),
                        edges[1][j, 1, rows, :].astype(F32),
                    )

                pair = (partial[index, 0, rows, :], partial[index, 1, rows, :])
                for j in range(2):
                    pair = before(j, pair)
                for j in range(2):
                    pair = after(j, pair)
                for part, value in enumerate(pair):
                    for panel in range(3):
                        start = ((index * 2 + part) * 3 + panel) * HALF
                        flat[pl.ds(pl.multiple_of(start + block * 32, 32), 32), :] = value[
                            :, panel * 128 : (panel + 1) * 128
                        ].astype(BF16)

            done = pl.ds(index * 6 * HALF, 6 * HALF)
            store = pltpu.make_async_copy(flat.at[done], out.at[done], sems.at[index])
            store.start()

    @pl.when(core == 0)
    def _():
        run((cross, same))

    @pl.when(core == 1)
    def _():
        run((same, cross))

    for index in range(3):
        done = pl.ds(index * 6 * HALF, 6 * HALF)
        pltpu.make_async_copy(flat.at[done], out.at[done], sems.at[index]).wait()


def polar_call(place, offsets, same, cross, chip, turned, partial):
    return pl.pallas_call(
        polar_body,
        out_shape=pltpu.HBM((FLAT, 128), BF16),
        in_specs=[SMEM, SMEM, VMEM, VMEM, VMEM, VMEM, VMEM],
        out_specs=ANY,
        scratch_shapes=[
            pltpu.VMEM((FLAT, 128), BF16),
            pltpu.SemaphoreType.DMA((3,)),
        ],
        compiler_params=pltpu.CompilerParams(vmem_limit_bytes=6 << 20),
        cost_estimate=pl.CostEstimate(flops=20_000_000, bytes_accessed=9_000_000, transcendentals=0),
        name="polar",
    )(place, offsets, same, cross, chip, turned, partial)


def near_body(place, swapped, cross, out, sems):
    core = place[0]
    copies = [
        pltpu.make_async_copy(cross, out.at[:, :, pl.ds(core * HALF, HALF), :], sems.at[0]),
        pltpu.make_async_copy(
            swapped, out.at[:, :, pl.ds(HALF - core * HALF, HALF), :], sems.at[1]
        ),
    ]
    for copy in copies:
        copy.start()
    for copy in copies:
        copy.wait()

    @pl.when(core == 1)
    def _():
        for item in range(2):
            for part in range(2):
                out[item, part] = out[item, part].astype(F32).T.astype(BF16)


def near_call(place, swapped, cross):
    return pl.pallas_call(
        near_body,
        out_shape=jax.ShapeDtypeStruct((2, 2, NB, NB), BF16),
        in_specs=[SMEM, ANY, ANY],
        out_specs=VMEM,
        scratch_shapes=[pltpu.SemaphoreType.DMA((2,))],
        compiler_params=pltpu.CompilerParams(vmem_limit_bytes=4 << 20),
        cost_estimate=pl.CostEstimate(flops=0, bytes_accessed=2_400_000, transcendentals=0),
        name="near_join",
    )(place, swapped, in_hbm(cross))


def born_body(early, *refs):
    refs = list(refs)
    place, offsets, occupation, coupling, own, mate, near = refs[:7]
    refs = refs[7:]
    far = None if early else refs.pop(0)
    vertex, out, chosen, lows, highs, mixed, wide, stack, side, total, rounded, sems = refs
    core = place[0]
    energy = 2 * (1 - core) if early else 2 * core

    def fetch(slot, target, sem):
        sources = [(own, 4, 4), (mate, 8 - 8 * core, 4), (near, 2 + 6 * core, 2)]
        if far is not None:
            sources.append((far, 10 * core, 2))
        for source, low, size in sources:

            @pl.when((slot >= low) & (slot < low + size))
            def _():
                pltpu.make_async_copy(source.at[slot - low], target, sem).start()

    for k in range(4):
        pltpu.make_async_copy(vertex.at[coupling[0, k]], chosen.at[k], sems.at[k, 4]).start()
        for item in range(2):
            at = energy + 4 + item
            fetch(at - offsets[k], lows.at[k, item], sems.at[k, 2 * item])
            fetch(at + offsets[k], highs.at[k, item], sems.at[k, 2 * item + 1])

    total[...] = jnp.zeros_like(total)

    @pl.loop(0, 4)
    def _(k):
        pltpu.make_async_copy(vertex.at[0], chosen.at[k], sems.at[k, 4]).wait()
        vr = chosen[k, 0]
        vi = chosen[k, 1]
        wide[:NB, :NB] = vr
        wide[:NB, NB:] = -vi
        wide[NB:, :NB] = vi
        wide[NB:, NB:] = vr
        side[:NB, :NB] = vr
        side[:NB, NB:] = vi
        side[NB:, :NB] = -vi
        side[NB:, NB:] = vr
        weight = occupation[k]
        for item in range(2):
            pltpu.make_async_copy(own.at[0], lows.at[k, item], sems.at[k, 2 * item]).wait()
            pltpu.make_async_copy(own.at[0], highs.at[k, item], sems.at[k, 2 * item + 1]).wait()
        for item in range(2):
            for part in range(2):
                low = lows[k, item, part].astype(F32)
                high = highs[k, item, part].astype(F32)
                value = weight * low + (weight + 1.0) * high
                mixed[part * NB : (part + 1) * NB, item * NB : (item + 1) * NB] = value.astype(BF16)
        for piece in range(2):
            begin = piece * 384
            part, row = begin // NB, begin % NB
            half = jnp.dot(
                wide[begin : begin + 384, :], mixed[...], preferred_element_type=F32
            ).astype(BF16)
            for item in range(2):
                stack[item * NB + row : item * NB + row + 384, part * NB : (part + 1) * NB] = half[
                    :, item * NB : (item + 1) * NB
                ]
        for piece in range(2):
            rows = slice(piece * 384, (piece + 1) * 384)
            term = lax.dot_general(
                stack[rows, :], side[...], (((1,), (1,)), ((), ())), preferred_element_type=F32
            )
            total[rows, :] += term

    if early:
        rounded[...] = total[...].astype(BF16)
        store = pltpu.make_async_copy(rounded, out, sems.at[0, 0])
        store.start()
        store.wait()
    else:
        out[...] = total[...].astype(BF16)


def born_call(place, offsets, occupation, coupling, arrays, vertex):
    early = len(arrays) == 3
    size = 2 * NB
    held = (*map(in_hbm, arrays[:2]), *arrays[2:])
    shape = (size, size)
    return pl.pallas_call(
        lambda *refs: born_body(early, *refs),
        out_shape=pltpu.HBM(shape, BF16) if early else jax.ShapeDtypeStruct(shape, BF16),
        in_specs=[SMEM] * 4 + [ANY] * (len(held) + 1),
        out_specs=ANY if early else VMEM,
        scratch_shapes=[
            pltpu.VMEM((4, 2, NB, NB), BF16),
            pltpu.VMEM((4, 2, 2, NB, NB), BF16),
            pltpu.VMEM((4, 2, 2, NB, NB), BF16),
            pltpu.VMEM((size, size), BF16),
            pltpu.VMEM((size, size), BF16),
            pltpu.VMEM((size, size), BF16),
            pltpu.VMEM((size, size), BF16),
            pltpu.VMEM((size, size), F32),
            pltpu.VMEM((size, size), BF16),
            pltpu.SemaphoreType.DMA((4, 5)),
        ],
        compiler_params=pltpu.CompilerParams(vmem_limit_bytes=22 << 20),
        cost_estimate=pl.CostEstimate(
            flops=16 * size**3, bytes_accessed=12_000_000, transcendentals=0
        ),
        name="born_early" if early else "born_late",
    )(place, offsets, occupation, coupling, *held, in_hbm(vertex))


def sum_body(count, copies, bands, out, buffer, value, *sems):
    loads = [
        pltpu.make_async_copy(bands.at[i], buffer.at[i], sems[0].at[i]) for i in range(count)
    ]
    for load in loads:
        load.start()
    for load in loads:
        load.wait()

    for begin in range(0, ROWS, 64):
        rows = slice(begin, min(begin + 64, ROWS))
        total = buffer[0, rows, :].astype(F32)
        for i in range(1, count):
            total += buffer[i, rows, :].astype(F32)
        value[rows, :] = total.astype(BF16)

    stores = [pltpu.make_async_copy(value, out.at[i], sems[1].at[i]) for i in range(copies)]
    for store in stores:
        store.start()
    for store in stores:
        store.wait()


def sum_call(bands, copies):
    count = bands.shape[0]
    return pl.pallas_call(
        lambda *refs: sum_body(count, copies, *refs),
        out_shape=pltpu.HBM((copies, ROWS, 128), BF16),
        in_specs=[ANY],
        out_specs=ANY,
        scratch_shapes=[
            pltpu.VMEM(bands.shape, BF16),
            pltpu.VMEM((ROWS, 128), BF16),
            pltpu.SemaphoreType.DMA((count,)),
            pltpu.SemaphoreType.DMA((copies,)),
        ],
        compiler_params=pltpu.CompilerParams(vmem_limit_bytes=4 << 20),
        cost_estimate=pl.CostEstimate(flops=500_000, bytes_accessed=1_900_000, transcendentals=0),
    )(bands)


def unpack_half(source, joined):
    for index in range(3):
        for part in range(2):
            for panel in range(3):
                start = ((index * 2 + part) * 3 + panel) * HALF
                joined[index, :, part * NB + panel * 128 : part * NB + (panel + 1) * 128] = source[
                    start : start + HALF, :
                ]


def direct(index, role, half, joined, table, magnon):
    rows = pl.ds(pl.multiple_of(half * HALF, HALF), HALF)
    value = jnp.dot(joined[index], table[role], preferred_element_type=F32)
    magnon[index, rows, :] = value.astype(BF16).astype(F32)


def transposed(index, role, half, joined, table):
    value = None
    for part in range(2):
        turned = joined[index, :, part * NB : (part + 1) * NB].astype(F32).T.astype(BF16)
        these = pl.ds(pl.multiple_of(part * NB + half * HALF, HALF), HALF)
        term = jnp.dot(turned, table[role, these, :], preferred_element_type=F32)
        value = term if value is None else value + term
    return value


def start_body(
    place, offsets, mine, free, own, mate,
    slots, magnon, sums, table, source, plain, joined, sems,
):
    core = place[0]
    roles = offset_roles(offsets)
    ready = pltpu.make_async_copy(mine, source, sems.at[6])
    tables = [
        pltpu.make_async_copy(free.at[k], plain.at[role], sems.at[role])
        for role, k in enumerate(roles)
    ]
    loads = [
        pltpu.make_async_copy(own, slots.at[pl.ds(4, 4)], sems.at[4]),
        pltpu.make_async_copy(mate, slots.at[pl.ds(8 - 8 * core, 4)], sems.at[5]),
    ]
    for load in [ready] + tables + loads:
        load.start()
    ready.wait()
    unpack_half(source, joined)
    for role in range(4):
        tables[role].wait()
        fr = plain[role, 0]
        fi = plain[role, 1]
        table[role, :NB, :NB] = fr
        table[role, :NB, NB:] = fi
        table[role, NB:, :NB] = -fi
        table[role, NB:, NB:] = fr
        if role == 0:
            direct(0, 0, core, joined, table, magnon)
        elif role == 1:
            sums[0] = transposed(0, 1, core, joined, table)
        else:

            @pl.when(offsets[roles[role]] > 0)
            def _():
                direct(role - 1, role, core, joined, table, magnon)

            @pl.when(offsets[roles[role]] < 0)
            def _():
                sums[role - 1] = transposed(role - 1, role, core, joined, table)

    for load in loads:
        load.wait()


def start_call(place, offsets, mine, free, own, mate):
    size = 2 * NB
    return pl.pallas_call(
        start_body,
        out_shape=(
            jax.ShapeDtypeStruct((12, 2, NB, NB), BF16),
            jax.ShapeDtypeStruct((3, NB, size), F32),
            jax.ShapeDtypeStruct((3, NB, size), F32),
            jax.ShapeDtypeStruct((4, size, size), BF16),
        ),
        in_specs=[SMEM, SMEM] + [ANY] * 4,
        out_specs=(VMEM,) * 4,
        scratch_shapes=[
            pltpu.VMEM((FLAT, 128), BF16),
            pltpu.VMEM((4, 2, NB, NB), BF16),
            pltpu.VMEM((3, HALF, size), BF16),
            pltpu.SemaphoreType.DMA((7,)),
        ],
        compiler_params=pltpu.CompilerParams(vmem_limit_bytes=10 << 20),
        cost_estimate=pl.CostEstimate(
            flops=1_000_000_000, bytes_accessed=10_000_000, transcendentals=0
        ),
        name="final_start",
    )(place, offsets, mine, *(in_hbm(x) for x in (free, own, mate)))


def final_body(
    place, offsets, other, near, far, early, late, slots_in, magnon_in, sums, table,
    out, slots, magnon, source, joined, result, sems,
):
    core = place[0]
    loads = [
        pltpu.make_async_copy(near, slots.at[pl.ds(2 + 6 * core, 2)], sems.at[5]),
        pltpu.make_async_copy(far, slots.at[pl.ds(10 * core, 2)], sems.at[6]),
    ]
    ready = pltpu.make_async_copy(other, source, sems.at[4])
    ready.start()
    for load in loads:
        load.start()
    ready.wait()
    unpack_half(source, joined)
    roles = offset_roles(offsets)
    _, _, first, last = roles
    half = 1 - core
    direct(0, 0, half, joined, table, magnon)
    total = sums[0] + transposed(0, 1, half, joined, table)
    magnon[0] += total.astype(BF16).astype(F32)
    for role in (2, 3):

        @pl.when(offsets[roles[role]] > 0)
        def _():
            direct(role - 1, role, half, joined, table, magnon)

        @pl.when(offsets[roles[role]] < 0)
        def _():
            total = sums[role - 1] + transposed(role - 1, role, half, joined, table)
            magnon[role - 1] = total.astype(BF16).astype(F32)

    for load in loads:
        load.wait()
    reach = spans(offsets, first, last)
    stores = []
    for item, energy in enumerate((2 - 2 * core, 3 - 2 * core, 2 * core, 2 * core + 1)):
        born = early if item < 2 else late

        @pl.loop(0, NB // 32)
        def _(block):
            rows = pl.ds(pl.multiple_of(block * 32, 32), 32)
            begin = pl.ds(pl.multiple_of((item % 2) * NB + block * 32, 32), 32)
            real = born[begin, :NB].astype(F32)
            imag = born[begin, NB:].astype(F32)
            for index in range(3):
                down = energy + 4 - reach[index]
                up = energy + 4 + reach[index]
                sr = slots[down, 0, rows, :].astype(F32) + slots[up, 0, rows, :].astype(F32)
                si = slots[down, 1, rows, :].astype(F32) + slots[up, 1, rows, :].astype(F32)
                mr = magnon[index, rows, :NB]
                mi = magnon[index, rows, NB:]
                real += mr * sr - mi * si
                imag += mr * si + mi * sr
            result[item, 0, rows, :] = real.astype(BF16)
            result[item, 1, rows, :] = imag.astype(BF16)

        store = pltpu.make_async_copy(result.at[item], out.at[energy, 0], sems.at[item])
        store.start()
        stores.append(store)
    for store in stores:
        store.wait()


def final_call(place, offsets, other, near, far, early, late, slots, magnon, sums, table):
    size = 2 * NB
    return pl.pallas_call(
        final_body,
        out_shape=(
            jax.ShapeDtypeStruct((4, 1, 2, NB, NB), BF16),
            jax.ShapeDtypeStruct(slots.shape, BF16),
            jax.ShapeDtypeStruct(magnon.shape, F32),
        ),
        in_specs=[SMEM, SMEM, ANY, ANY, ANY] + [VMEM] * 6,
        out_specs=(ANY, VMEM, VMEM),
        input_output_aliases={7: 1, 8: 2},
        scratch_shapes=[
            pltpu.VMEM((FLAT, 128), BF16),
            pltpu.VMEM((3, HALF, size), BF16),
            pltpu.VMEM((4, 2, NB, NB), BF16),
            pltpu.SemaphoreType.DMA((7,)),
        ],
        compiler_params=pltpu.CompilerParams(vmem_limit_bytes=12 << 20),
        cost_estimate=pl.CostEstimate(
            flops=1_000_000_000, bytes_accessed=18_000_000, transcendentals=0
        ),
        name="final",
    )(place, offsets, other, in_hbm(near), in_hbm(far), early, late, slots, magnon, sums, table)[0]


def per_device(green_blocks, offsets, occupation, coupling, vertex, magnon_free):
    count = lax.axis_size(ENERGY)
    core = lax.axis_index("core").astype(jnp.int32)
    place = core[None]
    own = green_blocks.reshape(4, 2, NB, NB)
    across = [(i, i + 1) for i in range(1, count - 1, 2)]
    across += [(target, source) for source, target in across]
    along = [(i, i + 2) for i in range(1, count - 2, 2)]
    along += [(i + 1, i - 1) for i in range(1, count - 2, 2)]
    to_same, to_cross = edge_call(place, own)
    cross = lax.ppermute(to_cross, ENERGY, across)
    same = lax.ppermute(to_same, ENERGY, along)
    mate = lax.ppermute(own, "core", SWAP)
    inner = cut_call(place, own, 2, -2)
    far = lax.ppermute(inner, ENERGY, across)
    chip, turned, partial = prepare_call(place, offsets, own, mate)
    pair = polar_call(place, offsets, same, cross, chip, turned, partial)
    swapped = lax.ppermute(same, "core", SWAP)
    near = near_call(place, swapped, cross)
    bands = lax.all_to_all(pair.reshape(BANDS, ROWS, 128), PLANE, 0, 0, tiled=True)
    early = born_call(place, offsets, occupation, coupling, (own, mate, near), vertex)
    copies = sum_call(bands, 4)
    bands = lax.all_to_all(copies, ROW, 0, 0, tiled=True)
    copies = sum_call(bands, BANDS)
    mine = lax.all_to_all(copies, PLANE, 0, 0, tiled=True).reshape(FLAT, 128)
    late = born_call(
        place, offsets, occupation, coupling, (own, mate, near, far), vertex
    )
    other = lax.ppermute(mine, "core", SWAP)
    held = start_call(place, offsets, mine, magnon_free, own, mate)
    return final_call(place, offsets, other, near, far, early, late, *held)


def solution(mesh):
    fine = Mesh(mesh.devices.reshape(4, 2, 2, 2, 4), ("y", "xh", "core", "xl", "z"))
    blocks = P(ENERGY, LAYER, None, None, None)
    placed = (blocks, P(), P(), P(LAYER, None), P(), P())
    return jax.shard_map(
        per_device, mesh=fine, in_specs=placed, out_specs=blocks, check_vma=False
    )
```

```python
import jax
import jax.numpy as jnp
from jax import lax
from jax.experimental import pallas as pl
from jax.experimental.pallas import tpu as pltpu
from jax.sharding import Mesh
from jax.sharding import PartitionSpec as P


NB = 384
HALF = NB // 2
BANDS = 16
ROWS = 18 * HALF // BANDS
FLAT = BANDS * ROWS
F32 = jnp.float32
BF16 = jnp.bfloat16
SWAP = [(0, 1), (1, 0)]
PLANE = ("y", "z")
ROW = ("xh", "xl")
ENERGY = ("y", "xh", "core")
LAYER = ("xl", "z")
ANY = pl.BlockSpec(memory_space=pl.ANY)
SMEM = pl.BlockSpec(memory_space=pltpu.SMEM)
VMEM = pl.BlockSpec(memory_space=pltpu.VMEM)


def in_hbm(array):
    return pltpu.with_memory_space_constraint(array, pltpu.HBM)


def first_index(offsets, value):
    return jnp.where(
        offsets[0] == value, 0, jnp.where(offsets[1] == value, 1, jnp.where(offsets[2] == value, 2, 3))
    )


def offset_roles(offsets):
    top = first_index(offsets, 4)
    bottom = first_index(offsets, -4)
    low = jnp.minimum(top, bottom)
    high = jnp.maximum(top, bottom)
    first = jnp.where(low != 0, 0, jnp.where(high != 1, 1, 2))
    last = jnp.where(high != 3, 3, jnp.where(low != 2, 2, 1))
    return top, bottom, first, last


def spans(offsets, first, last):
    return (jnp.int32(4), jnp.abs(offsets[first]), jnp.abs(offsets[last]))


def cut_body(place, base, sign, own, out, sem):
    copy = pltpu.make_async_copy(own.at[pl.ds(base + sign * place[0], 2)], out, sem)
    copy.start()
    copy.wait()


def cut_call(place, own, base, sign):
    return pl.pallas_call(
        lambda place, own, out, sem: cut_body(place, base, sign, own, out, sem),
        out_shape=jax.ShapeDtypeStruct((2, 2, NB, NB), BF16),
        in_specs=[SMEM, ANY],
        out_specs=VMEM,
        scratch_shapes=[pltpu.SemaphoreType.DMA],
        compiler_params=pltpu.CompilerParams(vmem_limit_bytes=4 << 20),
        cost_estimate=pl.CostEstimate(flops=0, bytes_accessed=2_400_000, transcendentals=0),
    )(place, in_hbm(own))


def edge_body(place, own, same, cross, whole, sems):
    core = place[0]

    @pl.when(core == 1)
    def _():
        copies = [
            pltpu.make_async_copy(own.at[pl.ds(2, 2), :, pl.ds(HALF, HALF), :], same, sems.at[0]),
            pltpu.make_async_copy(own.at[pl.ds(2, 2), :, pl.ds(0, HALF), :], cross, sems.at[1]),
        ]
        for copy in copies:
            copy.start()
        for copy in copies:
            copy.wait()

    @pl.when(core == 0)
    def _():
        copy = pltpu.make_async_copy(own.at[pl.ds(0, 2)], whole, sems.at[0])
        copy.start()
        copy.wait()
        for item in range(2):
            for part in range(2):
                value = whole[item, part].astype(F32).T.astype(BF16)
                same[item, part] = value[:HALF]
                cross[item, part] = value[HALF:]


def edge_call(place, own):
    half = jax.ShapeDtypeStruct((2, 2, HALF, NB), BF16)
    return pl.pallas_call(
        edge_body,
        out_shape=(half, half),
        in_specs=[SMEM, ANY],
        out_specs=(VMEM, VMEM),
        scratch_shapes=[pltpu.VMEM((2, 2, NB, NB), BF16), pltpu.SemaphoreType.DMA((2,))],
        compiler_params=pltpu.CompilerParams(vmem_limit_bytes=6 << 20),
        cost_estimate=pl.CostEstimate(flops=0, bytes_accessed=2_400_000, transcendentals=0),
        name="edge",
    )(place, in_hbm(own))


def prepare_body(place, offsets, own, mate, chip, turned, partial, sems):
    core = place[0]
    copies = [
        pltpu.make_async_copy(own, chip.at[pl.ds(4 * core, 4)], sems.at[0]),
        pltpu.make_async_copy(mate, chip.at[pl.ds(4 - 4 * core, 4)], sems.at[1]),
    ]
    for copy in copies:
        copy.start()
    for copy in copies:
        copy.wait()

    @pl.loop(2, 16)
    def _(step):
        turned[step // 2, step % 2] = chip[step // 2, step % 2].astype(F32).T

    _, _, first, last = offset_roles(offsets)
    for index, span in enumerate(spans(offsets, first, last)):

        @pl.loop(0, HALF // 32)
        def _(block):
            rows = pl.ds(pl.multiple_of(block * 32, 32), 32)
            there = pl.ds(pl.multiple_of(core * HALF + block * 32, 32), 32)

            def step(s, carry):
                real, imag = carry
                ar = chip[s, 0, there, :].astype(F32)
                ai = chip[s, 1, there, :].astype(F32)
                br = turned[s + span, 0, there, :]
                bi = turned[s + span, 1, there, :]
                return real + (ar * br - ai * bi), imag + (ar * bi + ai * br)

            zero = jnp.zeros((32, NB), F32)
            real, imag = lax.fori_loop(0, 8 - span, step, (zero, zero))
            partial[index, 0, rows, :] = real
            partial[index, 1, rows, :] = imag


def prepare_call(place, offsets, own, mate):
    return pl.pallas_call(
        prepare_body,
        out_shape=(
            jax.ShapeDtypeStruct((8, 2, NB, NB), BF16),
            jax.ShapeDtypeStruct((8, 2, NB, NB), F32),
            jax.ShapeDtypeStruct((3, 2, HALF, NB), F32),
        ),
        in_specs=[SMEM, SMEM, ANY, ANY],
        out_specs=(VMEM, VMEM, VMEM),
        scratch_shapes=[pltpu.SemaphoreType.DMA((2,))],
        compiler_params=pltpu.CompilerParams(vmem_limit_bytes=4 << 20),
        cost_estimate=pl.CostEstimate(flops=20_000_000, bytes_accessed=9_000_000, transcendentals=0),
        name="prepare",
    )(place, offsets, own, mate)


def polar_body(place, offsets, same, cross, chip, turned, partial, out, flat, sems):
    core = place[0]

    def run(edges):
        _, _, first, last = offset_roles(offsets)
        for index, span in enumerate(spans(offsets, first, last)):

            @pl.loop(0, HALF // 32)
            def _(block):
                rows = pl.ds(pl.multiple_of(block * 32, 32), 32)
                there = pl.ds(pl.multiple_of(core * HALF + block * 32, 32), 32)

                def multiply(carry, ar, ai, br, bi):
                    real, imag = carry
                    return real + (ar * br - ai * bi), imag + (ar * bi + ai * br)

                def before(j, carry):
                    ar = edges[0][1 - j, 0, rows, :].astype(F32)
                    ai = edges[0][1 - j, 1, rows, :].astype(F32)
                    if index > 0:
                        keep = jnp.where(span > 2 + j, 1.0, 0.0)
                        ar, ai = ar * keep, ai * keep
                    at = jnp.maximum(span - 1 - j, 1)
                    return multiply(carry, ar, ai, turned[at, 0, there, :], turned[at, 1, there, :])

                def after(j, carry):
                    at = jnp.minimum(8 - span + j, 7)
                    ar = chip[at, 0, there, :].astype(F32)
                    ai = chip[at, 1, there, :].astype(F32)
                    if index > 0 and j > 0:
                        keep = jnp.where(span > j, 1.0, 0.0)
                        ar, ai = ar * keep, ai * keep
                    return multiply(
                        carry,
                        ar,
                        ai,
                        edges[1][j, 0, rows, :].astype(F32),
                        edges[1][j, 1, rows, :].astype(F32),
                    )

                pair = (partial[index, 0, rows, :], partial[index, 1, rows, :])
                for j in range(2):
                    pair = before(j, pair)
                for j in range(2):
                    pair = after(j, pair)
                for part, value in enumerate(pair):
                    for panel in range(3):
                        start = ((index * 2 + part) * 3 + panel) * HALF
                        flat[pl.ds(pl.multiple_of(start + block * 32, 32), 32), :] = value[
                            :, panel * 128 : (panel + 1) * 128
                        ].astype(BF16)

            done = pl.ds(index * 6 * HALF, 6 * HALF)
            store = pltpu.make_async_copy(flat.at[done], out.at[done], sems.at[index])
            store.start()

    @pl.when(core == 0)
    def _():
        run((cross, same))

    @pl.when(core == 1)
    def _():
        run((same, cross))

    for index in range(3):
        done = pl.ds(index * 6 * HALF, 6 * HALF)
        pltpu.make_async_copy(flat.at[done], out.at[done], sems.at[index]).wait()


def polar_call(place, offsets, same, cross, chip, turned, partial):
    return pl.pallas_call(
        polar_body,
        out_shape=pltpu.HBM((FLAT, 128), BF16),
        in_specs=[SMEM, SMEM, VMEM, VMEM, VMEM, VMEM, VMEM],
        out_specs=ANY,
        scratch_shapes=[
            pltpu.VMEM((FLAT, 128), BF16),
            pltpu.SemaphoreType.DMA((3,)),
        ],
        compiler_params=pltpu.CompilerParams(vmem_limit_bytes=6 << 20),
        cost_estimate=pl.CostEstimate(flops=20_000_000, bytes_accessed=9_000_000, transcendentals=0),
        name="polar",
    )(place, offsets, same, cross, chip, turned, partial)


def near_body(place, swapped, cross, out, sems):
    core = place[0]
    copies = [
        pltpu.make_async_copy(cross, out.at[:, :, pl.ds(core * HALF, HALF), :], sems.at[0]),
        pltpu.make_async_copy(
            swapped, out.at[:, :, pl.ds(HALF - core * HALF, HALF), :], sems.at[1]
        ),
    ]
    for copy in copies:
        copy.start()
    for copy in copies:
        copy.wait()

    @pl.when(core == 1)
    def _():
        for item in range(2):
            for part in range(2):
                out[item, part] = out[item, part].astype(F32).T.astype(BF16)


def near_call(place, swapped, cross):
    return pl.pallas_call(
        near_body,
        out_shape=jax.ShapeDtypeStruct((2, 2, NB, NB), BF16),
        in_specs=[SMEM, ANY, ANY],
        out_specs=VMEM,
        scratch_shapes=[pltpu.SemaphoreType.DMA((2,))],
        compiler_params=pltpu.CompilerParams(vmem_limit_bytes=4 << 20),
        cost_estimate=pl.CostEstimate(flops=0, bytes_accessed=2_400_000, transcendentals=0),
        name="near_join",
    )(place, swapped, in_hbm(cross))


def born_body(early, *refs):
    refs = list(refs)
    place, offsets, occupation, coupling, own, mate, near = refs[:7]
    refs = refs[7:]
    far = None if early else refs.pop(0)
    vertex, out, chosen, lows, highs, mixed, wide, stack, side, total, rounded, sems = refs
    core = place[0]
    energy = 2 * (1 - core) if early else 2 * core

    def fetch(slot, target, sem):
        sources = [(own, 4, 4), (mate, 8 - 8 * core, 4), (near, 2 + 6 * core, 2)]
        if far is not None:
            sources.append((far, 10 * core, 2))
        for source, low, size in sources:

            @pl.when((slot >= low) & (slot < low + size))
            def _():
                pltpu.make_async_copy(source.at[slot - low], target, sem).start()

    for k in range(4):
        pltpu.make_async_copy(vertex.at[coupling[0, k]], chosen.at[k], sems.at[k, 4]).start()
        for item in range(2):
            at = energy + 4 + item
            fetch(at - offsets[k], lows.at[k, item], sems.at[k, 2 * item])
            fetch(at + offsets[k], highs.at[k, item], sems.at[k, 2 * item + 1])

    total[...] = jnp.zeros_like(total)

    @pl.loop(0, 4)
    def _(k):
        pltpu.make_async_copy(vertex.at[0], chosen.at[k], sems.at[k, 4]).wait()
        vr = chosen[k, 0]
        vi = chosen[k, 1]
        wide[:NB, :NB] = vr
        wide[:NB, NB:] = -vi
        wide[NB:, :NB] = vi
        wide[NB:, NB:] = vr
        side[:NB, :NB] = vr
        side[:NB, NB:] = vi
        side[NB:, :NB] = -vi
        side[NB:, NB:] = vr
        weight = occupation[k]
        for item in range(2):
            pltpu.make_async_copy(own.at[0], lows.at[k, item], sems.at[k, 2 * item]).wait()
            pltpu.make_async_copy(own.at[0], highs.at[k, item], sems.at[k, 2 * item + 1]).wait()
        for item in range(2):
            for part in range(2):
                low = lows[k, item, part].astype(F32)
                high = highs[k, item, part].astype(F32)
                value = weight * low + (weight + 1.0) * high
                mixed[part * NB : (part + 1) * NB, item * NB : (item + 1) * NB] = value.astype(BF16)
        for piece in range(2):
            begin = piece * 384
            part, row = begin // NB, begin % NB
            half = jnp.dot(
                wide[begin : begin + 384, :], mixed[...], preferred_element_type=F32
            ).astype(BF16)
            for item in range(2):
                stack[item * NB + row : item * NB + row + 384, part * NB : (part + 1) * NB] = half[
                    :, item * NB : (item + 1) * NB
                ]
        for piece in range(2):
            rows = slice(piece * 384, (piece + 1) * 384)
            term = lax.dot_general(
                stack[rows, :], side[...], (((1,), (1,)), ((), ())), preferred_element_type=F32
            )
            total[rows, :] += term

    if early:
        rounded[...] = total[...].astype(BF16)
        store = pltpu.make_async_copy(rounded, out, sems.at[0, 0])
        store.start()
        store.wait()
    else:
        out[...] = total[...].astype(BF16)


def born_call(place, offsets, occupation, coupling, arrays, vertex):
    early = len(arrays) == 3
    size = 2 * NB
    held = (*map(in_hbm, arrays[:2]), *arrays[2:])
    shape = (size, size)
    return pl.pallas_call(
        lambda *refs: born_body(early, *refs),
        out_shape=pltpu.HBM(shape, BF16) if early else jax.ShapeDtypeStruct(shape, BF16),
        in_specs=[SMEM] * 4 + [ANY] * (len(held) + 1),
        out_specs=ANY if early else VMEM,
        scratch_shapes=[
            pltpu.VMEM((4, 2, NB, NB), BF16),
            pltpu.VMEM((4, 2, 2, NB, NB), BF16),
            pltpu.VMEM((4, 2, 2, NB, NB), BF16),
            pltpu.VMEM((size, size), BF16),
            pltpu.VMEM((size, size), BF16),
            pltpu.VMEM((size, size), BF16),
            pltpu.VMEM((size, size), BF16),
            pltpu.VMEM((size, size), F32),
            pltpu.VMEM((size, size), BF16),
            pltpu.SemaphoreType.DMA((4, 5)),
        ],
        compiler_params=pltpu.CompilerParams(vmem_limit_bytes=22 << 20),
        cost_estimate=pl.CostEstimate(
            flops=16 * size**3, bytes_accessed=12_000_000, transcendentals=0
        ),
        name="born_early" if early else "born_late",
    )(place, offsets, occupation, coupling, *held, in_hbm(vertex))


def band_total(bands, rows):
    total = bands[0, rows, :].astype(F32)
    for i in range(1, bands.shape[0]):
        total += bands[i, rows, :].astype(F32)
    return total.astype(BF16)


def plane_body(bands, out):
    for begin in range(0, ROWS, 64):
        rows = slice(begin, min(begin + 64, ROWS))
        value = band_total(bands, rows)
        for i in range(out.shape[0]):
            out[i, rows, :] = value


def plane_call(bands):
    return pl.pallas_call(
        plane_body,
        out_shape=jax.ShapeDtypeStruct((4, ROWS, 128), BF16),
        in_specs=[VMEM],
        out_specs=VMEM,
        compiler_params=pltpu.CompilerParams(vmem_limit_bytes=4 << 20),
        cost_estimate=pl.CostEstimate(flops=500_000, bytes_accessed=1_200_000, transcendentals=0),
        name="plane_sum",
    )(bands)


def row_body(bands, out, value, sems):
    for begin in range(0, ROWS, 64):
        rows = slice(begin, min(begin + 64, ROWS))
        value[rows, :] = band_total(bands, rows)
    stores = [pltpu.make_async_copy(value, out.at[i], sems.at[i]) for i in range(BANDS)]
    for store in stores:
        store.start()
    for store in stores:
        store.wait()


def row_call(bands):
    return pl.pallas_call(
        row_body,
        out_shape=pltpu.HBM((BANDS, ROWS, 128), BF16),
        in_specs=[VMEM],
        out_specs=ANY,
        scratch_shapes=[pltpu.VMEM((ROWS, 128), BF16), pltpu.SemaphoreType.DMA((BANDS,))],
        compiler_params=pltpu.CompilerParams(vmem_limit_bytes=4 << 20),
        cost_estimate=pl.CostEstimate(flops=500_000, bytes_accessed=1_200_000, transcendentals=0),
        name="row_sum",
    )(bands)


def unpack_half(source, joined):
    for index in range(3):
        for part in range(2):
            for panel in range(3):
                start = ((index * 2 + part) * 3 + panel) * HALF
                joined[index, :, part * NB + panel * 128 : part * NB + (panel + 1) * 128] = source[
                    start : start + HALF, :
                ]


def direct(index, role, half, joined, table, magnon):
    rows = pl.ds(pl.multiple_of(half * HALF, HALF), HALF)
    value = jnp.dot(joined[index], table[role], preferred_element_type=F32)
    magnon[index, rows, :] = value.astype(BF16).astype(F32)


def transposed(index, role, half, joined, table):
    value = None
    for part in range(2):
        turned = joined[index, :, part * NB : (part + 1) * NB].astype(F32).T.astype(BF16)
        these = pl.ds(pl.multiple_of(part * NB + half * HALF, HALF), HALF)
        term = jnp.dot(turned, table[role, these, :], preferred_element_type=F32)
        value = term if value is None else value + term
    return value


def start_body(
    place, offsets, mine, free, own, mate,
    slots, magnon, sums, table, plain, joined, sems,
):
    core = place[0]
    roles = offset_roles(offsets)
    tables = [
        pltpu.make_async_copy(free.at[k], plain.at[role], sems.at[role])
        for role, k in enumerate(roles)
    ]
    loads = [
        pltpu.make_async_copy(own, slots.at[pl.ds(4, 4)], sems.at[4]),
        pltpu.make_async_copy(mate, slots.at[pl.ds(8 - 8 * core, 4)], sems.at[5]),
    ]
    for load in tables + loads:
        load.start()
    unpack_half(mine, joined)
    for role in range(4):
        tables[role].wait()
        fr = plain[role, 0]
        fi = plain[role, 1]
        table[role, :NB, :NB] = fr
        table[role, :NB, NB:] = fi
        table[role, NB:, :NB] = -fi
        table[role, NB:, NB:] = fr
        if role == 0:
            direct(0, 0, core, joined, table, magnon)
        elif role == 1:
            sums[0] = transposed(0, 1, core, joined, table)
        else:

            @pl.when(offsets[roles[role]] > 0)
            def _():
                direct(role - 1, role, core, joined, table, magnon)

            @pl.when(offsets[roles[role]] < 0)
            def _():
                sums[role - 1] = transposed(role - 1, role, core, joined, table)

    for load in loads:
        load.wait()


def start_call(place, offsets, mine, free, own, mate):
    size = 2 * NB
    return pl.pallas_call(
        start_body,
        out_shape=(
            jax.ShapeDtypeStruct((12, 2, NB, NB), BF16),
            jax.ShapeDtypeStruct((3, NB, size), F32),
            jax.ShapeDtypeStruct((3, NB, size), F32),
            jax.ShapeDtypeStruct((4, size, size), BF16),
        ),
        in_specs=[SMEM, SMEM, VMEM] + [ANY] * 3,
        out_specs=(VMEM,) * 4,
        scratch_shapes=[
            pltpu.VMEM((4, 2, NB, NB), BF16),
            pltpu.VMEM((3, HALF, size), BF16),
            pltpu.SemaphoreType.DMA((6,)),
        ],
        compiler_params=pltpu.CompilerParams(vmem_limit_bytes=10 << 20),
        cost_estimate=pl.CostEstimate(
            flops=1_000_000_000, bytes_accessed=10_000_000, transcendentals=0
        ),
        name="final_start",
    )(place, offsets, mine, *(in_hbm(x) for x in (free, own, mate)))


def final_body(
    place, offsets, other, near, far, early, late, slots_in, magnon_in, sums, table,
    out, slots, magnon, joined, result, sems,
):
    core = place[0]
    loads = [
        pltpu.make_async_copy(near, slots.at[pl.ds(2 + 6 * core, 2)], sems.at[5]),
        pltpu.make_async_copy(far, slots.at[pl.ds(10 * core, 2)], sems.at[6]),
    ]
    for load in loads:
        load.start()
    unpack_half(other, joined)
    roles = offset_roles(offsets)
    _, _, first, last = roles
    half = 1 - core
    direct(0, 0, half, joined, table, magnon)
    total = sums[0] + transposed(0, 1, half, joined, table)
    magnon[0] += total.astype(BF16).astype(F32)
    for role in (2, 3):

        @pl.when(offsets[roles[role]] > 0)
        def _():
            direct(role - 1, role, half, joined, table, magnon)

        @pl.when(offsets[roles[role]] < 0)
        def _():
            total = sums[role - 1] + transposed(role - 1, role, half, joined, table)
            magnon[role - 1] = total.astype(BF16).astype(F32)

    for load in loads:
        load.wait()
    reach = spans(offsets, first, last)
    stores = []
    for item, energy in enumerate((2 - 2 * core, 3 - 2 * core, 2 * core, 2 * core + 1)):
        born = early if item < 2 else late

        @pl.loop(0, NB // 32)
        def _(block):
            rows = pl.ds(pl.multiple_of(block * 32, 32), 32)
            begin = pl.ds(pl.multiple_of((item % 2) * NB + block * 32, 32), 32)
            real = born[begin, :NB].astype(F32)
            imag = born[begin, NB:].astype(F32)
            for index in range(3):
                down = energy + 4 - reach[index]
                up = energy + 4 + reach[index]
                sr = slots[down, 0, rows, :].astype(F32) + slots[up, 0, rows, :].astype(F32)
                si = slots[down, 1, rows, :].astype(F32) + slots[up, 1, rows, :].astype(F32)
                mr = magnon[index, rows, :NB]
                mi = magnon[index, rows, NB:]
                real += mr * sr - mi * si
                imag += mr * si + mi * sr
            result[item, 0, rows, :] = real.astype(BF16)
            result[item, 1, rows, :] = imag.astype(BF16)

        store = pltpu.make_async_copy(result.at[item], out.at[energy, 0], sems.at[item])
        store.start()
        stores.append(store)
    for store in stores:
        store.wait()


def final_call(place, offsets, other, near, far, early, late, slots, magnon, sums, table):
    size = 2 * NB
    return pl.pallas_call(
        final_body,
        out_shape=(
            jax.ShapeDtypeStruct((4, 1, 2, NB, NB), BF16),
            jax.ShapeDtypeStruct(slots.shape, BF16),
            jax.ShapeDtypeStruct(magnon.shape, F32),
        ),
        in_specs=[SMEM, SMEM, VMEM, ANY, ANY] + [VMEM] * 6,
        out_specs=(ANY, VMEM, VMEM),
        input_output_aliases={7: 1, 8: 2},
        scratch_shapes=[
            pltpu.VMEM((3, HALF, size), BF16),
            pltpu.VMEM((4, 2, NB, NB), BF16),
            pltpu.SemaphoreType.DMA((7,)),
        ],
        compiler_params=pltpu.CompilerParams(vmem_limit_bytes=12 << 20),
        cost_estimate=pl.CostEstimate(
            flops=1_000_000_000, bytes_accessed=18_000_000, transcendentals=0
        ),
        name="final",
    )(place, offsets, other, in_hbm(near), in_hbm(far), early, late, slots, magnon, sums, table)[0]


def per_device(green_blocks, offsets, occupation, coupling, vertex, magnon_free):
    count = lax.axis_size(ENERGY)
    core = lax.axis_index("core").astype(jnp.int32)
    place = core[None]
    own = green_blocks.reshape(4, 2, NB, NB)
    across = [(i, i + 1) for i in range(1, count - 1, 2)]
    across += [(target, source) for source, target in across]
    along = [(i, i + 2) for i in range(1, count - 2, 2)]
    along += [(i + 1, i - 1) for i in range(1, count - 2, 2)]
    to_same, to_cross = edge_call(place, own)
    cross = lax.ppermute(to_cross, ENERGY, across)
    same = lax.ppermute(to_same, ENERGY, along)
    mate = lax.ppermute(own, "core", SWAP)
    inner = cut_call(place, own, 2, -2)
    far = lax.ppermute(inner, ENERGY, across)
    chip, turned, partial = prepare_call(place, offsets, own, mate)
    pair = polar_call(place, offsets, same, cross, chip, turned, partial)
    swapped = lax.ppermute(same, "core", SWAP)
    near = near_call(place, swapped, cross)
    bands = lax.all_to_all(pair.reshape(BANDS, ROWS, 128), PLANE, 0, 0, tiled=True)
    early = born_call(place, offsets, occupation, coupling, (own, mate, near), vertex)
    copies = plane_call(bands)
    bands = lax.all_to_all(copies, ROW, 0, 0, tiled=True)
    copies = row_call(bands)
    mine = lax.all_to_all(copies, PLANE, 0, 0, tiled=True).reshape(FLAT, 128)
    late = born_call(
        place, offsets, occupation, coupling, (own, mate, near, far), vertex
    )
    other = lax.ppermute(mine, "core", SWAP)
    held = start_call(place, offsets, mine, magnon_free, own, mate)
    return final_call(place, offsets, other, near, far, early, late, *held)


def solution(mesh):
    fine = Mesh(mesh.devices.reshape(4, 2, 2, 2, 4), ("y", "xh", "core", "xl", "z"))
    blocks = P(ENERGY, LAYER, None, None, None)
    placed = (blocks, P(), P(), P(LAYER, None), P(), P())
    return jax.shard_map(
        per_device, mesh=fine, in_specs=placed, out_specs=blocks, check_vma=False
    )
```

```python
import jax
import jax.numpy as jnp
from jax import lax
from jax.experimental import pallas as pl
from jax.experimental.pallas import tpu as pltpu
from jax.sharding import Mesh
from jax.sharding import PartitionSpec as P


NB = 384
HALF = NB // 2
BANDS = 16
ROWS = 18 * HALF // BANDS
FLAT = BANDS * ROWS
F32 = jnp.float32
BF16 = jnp.bfloat16
SWAP = [(0, 1), (1, 0)]
PLANE = ("y", "z")
ROW = ("xh", "xl")
ENERGY = ("y", "xh", "core")
LAYER = ("xl", "z")
ANY = pl.BlockSpec(memory_space=pl.ANY)
SMEM = pl.BlockSpec(memory_space=pltpu.SMEM)
VMEM = pl.BlockSpec(memory_space=pltpu.VMEM)


def in_hbm(array):
    return pltpu.with_memory_space_constraint(array, pltpu.HBM)


def in_vmem(array):
    return pltpu.with_memory_space_constraint(array, pltpu.VMEM)


def first_index(offsets, value):
    return jnp.where(
        offsets[0] == value, 0, jnp.where(offsets[1] == value, 1, jnp.where(offsets[2] == value, 2, 3))
    )


def offset_roles(offsets):
    top = first_index(offsets, 4)
    bottom = first_index(offsets, -4)
    low = jnp.minimum(top, bottom)
    high = jnp.maximum(top, bottom)
    first = jnp.where(low != 0, 0, jnp.where(high != 1, 1, 2))
    last = jnp.where(high != 3, 3, jnp.where(low != 2, 2, 1))
    return top, bottom, first, last


def spans(offsets, first, last):
    return (jnp.int32(4), jnp.abs(offsets[first]), jnp.abs(offsets[last]))


def cut_body(place, base, sign, own, out, sem):
    copy = pltpu.make_async_copy(own.at[pl.ds(base + sign * place[0], 2)], out, sem)
    copy.start()
    copy.wait()


def cut_call(place, own, base, sign):
    return pl.pallas_call(
        lambda place, own, out, sem: cut_body(place, base, sign, own, out, sem),
        out_shape=jax.ShapeDtypeStruct((2, 2, NB, NB), BF16),
        in_specs=[SMEM, ANY],
        out_specs=VMEM,
        scratch_shapes=[pltpu.SemaphoreType.DMA],
        compiler_params=pltpu.CompilerParams(vmem_limit_bytes=4 << 20),
        cost_estimate=pl.CostEstimate(flops=0, bytes_accessed=2_400_000, transcendentals=0),
    )(place, in_hbm(own))


def edge_body(place, own, same, cross, whole, sems):
    core = place[0]

    @pl.when(core == 1)
    def _():
        copies = [
            pltpu.make_async_copy(own.at[pl.ds(2, 2), :, pl.ds(HALF, HALF), :], same, sems.at[0]),
            pltpu.make_async_copy(own.at[pl.ds(2, 2), :, pl.ds(0, HALF), :], cross, sems.at[1]),
        ]
        for copy in copies:
            copy.start()
        for copy in copies:
            copy.wait()

    @pl.when(core == 0)
    def _():
        copy = pltpu.make_async_copy(own.at[pl.ds(0, 2)], whole, sems.at[0])
        copy.start()
        copy.wait()
        for item in range(2):
            for part in range(2):
                value = whole[item, part].astype(F32).T.astype(BF16)
                same[item, part] = value[:HALF]
                cross[item, part] = value[HALF:]


def edge_call(place, own):
    half = jax.ShapeDtypeStruct((2, 2, HALF, NB), BF16)
    return pl.pallas_call(
        edge_body,
        out_shape=(half, half),
        in_specs=[SMEM, ANY],
        out_specs=(VMEM, VMEM),
        scratch_shapes=[pltpu.VMEM((2, 2, NB, NB), BF16), pltpu.SemaphoreType.DMA((2,))],
        compiler_params=pltpu.CompilerParams(vmem_limit_bytes=6 << 20),
        cost_estimate=pl.CostEstimate(flops=0, bytes_accessed=2_400_000, transcendentals=0),
        name="edge",
    )(place, in_hbm(own))


def prepare_body(place, offsets, own, mate, chip, turned, partial, sems):
    core = place[0]
    copies = [
        pltpu.make_async_copy(own, chip.at[pl.ds(4 * core, 4)], sems.at[0]),
        pltpu.make_async_copy(mate, chip.at[pl.ds(4 - 4 * core, 4)], sems.at[1]),
    ]
    for copy in copies:
        copy.start()
    for copy in copies:
        copy.wait()

    @pl.loop(2, 16)
    def _(step):
        turned[step // 2, step % 2] = chip[step // 2, step % 2].astype(F32).T

    _, _, first, last = offset_roles(offsets)
    for index, span in enumerate(spans(offsets, first, last)):

        @pl.loop(0, HALF // 32)
        def _(block):
            rows = pl.ds(pl.multiple_of(block * 32, 32), 32)
            there = pl.ds(pl.multiple_of(core * HALF + block * 32, 32), 32)

            def step(s, carry):
                real, imag = carry
                ar = chip[s, 0, there, :].astype(F32)
                ai = chip[s, 1, there, :].astype(F32)
                br = turned[s + span, 0, there, :]
                bi = turned[s + span, 1, there, :]
                return real + (ar * br - ai * bi), imag + (ar * bi + ai * br)

            zero = jnp.zeros((32, NB), F32)
            real, imag = lax.fori_loop(0, 8 - span, step, (zero, zero))
            partial[index, 0, rows, :] = real
            partial[index, 1, rows, :] = imag


def prepare_call(place, offsets, own, mate):
    return pl.pallas_call(
        prepare_body,
        out_shape=(
            jax.ShapeDtypeStruct((8, 2, NB, NB), BF16),
            jax.ShapeDtypeStruct((8, 2, NB, NB), F32),
            jax.ShapeDtypeStruct((3, 2, HALF, NB), F32),
        ),
        in_specs=[SMEM, SMEM, ANY, ANY],
        out_specs=(VMEM, VMEM, VMEM),
        scratch_shapes=[pltpu.SemaphoreType.DMA((2,))],
        compiler_params=pltpu.CompilerParams(vmem_limit_bytes=4 << 20),
        cost_estimate=pl.CostEstimate(flops=20_000_000, bytes_accessed=9_000_000, transcendentals=0),
        name="prepare",
    )(place, offsets, own, mate)


def polar_body(place, offsets, same, cross, chip, turned, partial, out, flat, sems):
    core = place[0]

    def run(edges):
        _, _, first, last = offset_roles(offsets)
        for index, span in enumerate(spans(offsets, first, last)):

            @pl.loop(0, HALF // 32)
            def _(block):
                rows = pl.ds(pl.multiple_of(block * 32, 32), 32)
                there = pl.ds(pl.multiple_of(core * HALF + block * 32, 32), 32)

                def multiply(carry, ar, ai, br, bi):
                    real, imag = carry
                    return real + (ar * br - ai * bi), imag + (ar * bi + ai * br)

                def before(j, carry):
                    ar = edges[0][1 - j, 0, rows, :].astype(F32)
                    ai = edges[0][1 - j, 1, rows, :].astype(F32)
                    if index > 0:
                        keep = jnp.where(span > 2 + j, 1.0, 0.0)
                        ar, ai = ar * keep, ai * keep
                    at = jnp.maximum(span - 1 - j, 1)
                    return multiply(carry, ar, ai, turned[at, 0, there, :], turned[at, 1, there, :])

                def after(j, carry):
                    at = jnp.minimum(8 - span + j, 7)
                    ar = chip[at, 0, there, :].astype(F32)
                    ai = chip[at, 1, there, :].astype(F32)
                    if index > 0 and j > 0:
                        keep = jnp.where(span > j, 1.0, 0.0)
                        ar, ai = ar * keep, ai * keep
                    return multiply(
                        carry,
                        ar,
                        ai,
                        edges[1][j, 0, rows, :].astype(F32),
                        edges[1][j, 1, rows, :].astype(F32),
                    )

                pair = (partial[index, 0, rows, :], partial[index, 1, rows, :])
                for j in range(2):
                    pair = before(j, pair)
                for j in range(2):
                    pair = after(j, pair)
                for part, value in enumerate(pair):
                    for panel in range(3):
                        start = ((index * 2 + part) * 3 + panel) * HALF
                        flat[pl.ds(pl.multiple_of(start + block * 32, 32), 32), :] = value[
                            :, panel * 128 : (panel + 1) * 128
                        ].astype(BF16)

            done = pl.ds(index * 6 * HALF, 6 * HALF)
            store = pltpu.make_async_copy(flat.at[done], out.at[done], sems.at[index])
            store.start()

    @pl.when(core == 0)
    def _():
        run((cross, same))

    @pl.when(core == 1)
    def _():
        run((same, cross))

    for index in range(3):
        done = pl.ds(index * 6 * HALF, 6 * HALF)
        pltpu.make_async_copy(flat.at[done], out.at[done], sems.at[index]).wait()


def polar_call(place, offsets, same, cross, chip, turned, partial):
    return pl.pallas_call(
        polar_body,
        out_shape=pltpu.HBM((FLAT, 128), BF16),
        in_specs=[SMEM, SMEM, VMEM, VMEM, VMEM, VMEM, VMEM],
        out_specs=ANY,
        scratch_shapes=[
            pltpu.VMEM((FLAT, 128), BF16),
            pltpu.SemaphoreType.DMA((3,)),
        ],
        compiler_params=pltpu.CompilerParams(vmem_limit_bytes=6 << 20),
        cost_estimate=pl.CostEstimate(flops=20_000_000, bytes_accessed=9_000_000, transcendentals=0),
        name="polar",
    )(place, offsets, in_vmem(same), in_vmem(cross), chip, turned, partial)


def near_body(place, swapped, cross, out, sems):
    core = place[0]
    copies = [
        pltpu.make_async_copy(cross, out.at[:, :, pl.ds(core * HALF, HALF), :], sems.at[0]),
        pltpu.make_async_copy(
            swapped, out.at[:, :, pl.ds(HALF - core * HALF, HALF), :], sems.at[1]
        ),
    ]
    for copy in copies:
        copy.start()
    for copy in copies:
        copy.wait()

    @pl.when(core == 1)
    def _():
        for item in range(2):
            for part in range(2):
                out[item, part] = out[item, part].astype(F32).T.astype(BF16)


def near_call(place, swapped, cross):
    return pl.pallas_call(
        near_body,
        out_shape=jax.ShapeDtypeStruct((2, 2, NB, NB), BF16),
        in_specs=[SMEM, ANY, ANY],
        out_specs=VMEM,
        scratch_shapes=[pltpu.SemaphoreType.DMA((2,))],
        compiler_params=pltpu.CompilerParams(vmem_limit_bytes=4 << 20),
        cost_estimate=pl.CostEstimate(flops=0, bytes_accessed=2_400_000, transcendentals=0),
        name="near_join",
    )(place, swapped, in_hbm(cross))


def born_body(early, *refs):
    refs = list(refs)
    place, offsets, occupation, coupling, own, mate, near = refs[:7]
    refs = refs[7:]
    fars = () if early else (refs.pop(0), refs.pop(0))
    side_of = None if early else refs.pop(0)
    vertex, out, chosen, lows, highs, mixed, wide, stack, side, total, rounded, sems = refs
    core = place[0]
    energy = 2 * (1 - core) if early else 2 * core

    def fetch(slot, target, sem):
        sources = [(own, 4, 4), (mate, 8 - 8 * core, 4), (near, 2 + 6 * core, 2)]
        if fars:
            crossing = side_of[0] == core
            sources.append((fars[0], jnp.where(crossing, 10 * core, 16), 2))
            sources.append((fars[1], jnp.where(crossing, 16, 10 * core), 2))
        for source, low, size in sources:

            @pl.when((slot >= low) & (slot < low + size))
            def _():
                pltpu.make_async_copy(source.at[slot - low], target, sem).start()

    for k in range(4):
        pltpu.make_async_copy(vertex.at[coupling[0, k]], chosen.at[k], sems.at[k, 4]).start()
        for item in range(2):
            at = energy + 4 + item
            fetch(at - offsets[k], lows.at[k, item], sems.at[k, 2 * item])
            fetch(at + offsets[k], highs.at[k, item], sems.at[k, 2 * item + 1])

    total[...] = jnp.zeros_like(total)

    @pl.loop(0, 4)
    def _(k):
        pltpu.make_async_copy(vertex.at[0], chosen.at[k], sems.at[k, 4]).wait()
        vr = chosen[k, 0]
        vi = chosen[k, 1]
        wide[:NB, :NB] = vr
        wide[:NB, NB:] = -vi
        wide[NB:, :NB] = vi
        wide[NB:, NB:] = vr
        side[:NB, :NB] = vr
        side[:NB, NB:] = vi
        side[NB:, :NB] = -vi
        side[NB:, NB:] = vr
        weight = occupation[k]
        for item in range(2):
            pltpu.make_async_copy(own.at[0], lows.at[k, item], sems.at[k, 2 * item]).wait()
            pltpu.make_async_copy(own.at[0], highs.at[k, item], sems.at[k, 2 * item + 1]).wait()
        for item in range(2):
            for part in range(2):
                low = lows[k, item, part].astype(F32)
                high = highs[k, item, part].astype(F32)
                value = weight * low + (weight + 1.0) * high
                mixed[part * NB : (part + 1) * NB, item * NB : (item + 1) * NB] = value.astype(BF16)
        for piece in range(2):
            begin = piece * 384
            part, row = begin // NB, begin % NB
            half = jnp.dot(
                wide[begin : begin + 384, :], mixed[...], preferred_element_type=F32
            ).astype(BF16)
            for item in range(2):
                stack[item * NB + row : item * NB + row + 384, part * NB : (part + 1) * NB] = half[
                    :, item * NB : (item + 1) * NB
                ]
        for piece in range(2):
            rows = slice(piece * 384, (piece + 1) * 384)
            term = lax.dot_general(
                stack[rows, :], side[...], (((1,), (1,)), ((), ())), preferred_element_type=F32
            )
            total[rows, :] += term

    stores = []
    for piece in range(2):
        rows = slice(piece * NB, (piece + 1) * NB)
        rounded[rows, :] = total[rows, :].astype(BF16)
        store = pltpu.make_async_copy(rounded.at[rows], out.at[rows], sems.at[piece, 0])
        store.start()
        stores.append(store)
    for store in stores:
        store.wait()


def born_call(place, offsets, occupation, coupling, arrays, vertex, *extra):
    early = len(arrays) == 3
    size = 2 * NB
    held = (*map(in_hbm, arrays[:2]), *arrays[2:])
    shape = (size, size)
    return pl.pallas_call(
        lambda *refs: born_body(early, *refs),
        out_shape=pltpu.HBM(shape, BF16),
        in_specs=[SMEM] * 4 + [ANY] * len(arrays) + [SMEM] * len(extra) + [ANY],
        out_specs=ANY,
        scratch_shapes=[
            pltpu.VMEM((4, 2, NB, NB), BF16),
            pltpu.VMEM((4, 2, 2, NB, NB), BF16),
            pltpu.VMEM((4, 2, 2, NB, NB), BF16),
            pltpu.VMEM((size, size), BF16),
            pltpu.VMEM((size, size), BF16),
            pltpu.VMEM((size, size), BF16),
            pltpu.VMEM((size, size), BF16),
            pltpu.VMEM((size, size), F32),
            pltpu.VMEM((size, size), BF16),
            pltpu.SemaphoreType.DMA((4, 5)),
        ],
        compiler_params=pltpu.CompilerParams(vmem_limit_bytes=22 << 20),
        cost_estimate=pl.CostEstimate(
            flops=16 * size**3, bytes_accessed=12_000_000, transcendentals=0
        ),
        name="born_early" if early else "born_late",
    )(place, offsets, occupation, coupling, *held, *extra, in_hbm(vertex))


def band_total(bands, rows):
    total = bands[0, rows, :].astype(F32)
    for i in range(1, bands.shape[0]):
        total += bands[i, rows, :].astype(F32)
    return total.astype(BF16)


def plane_body(bands, out):
    for begin in range(0, ROWS, 64):
        rows = slice(begin, min(begin + 64, ROWS))
        value = band_total(bands, rows)
        for i in range(out.shape[0]):
            out[i, rows, :] = value


def plane_call(bands):
    return pl.pallas_call(
        plane_body,
        out_shape=jax.ShapeDtypeStruct((4, ROWS, 128), BF16),
        in_specs=[VMEM],
        out_specs=VMEM,
        compiler_params=pltpu.CompilerParams(vmem_limit_bytes=4 << 20),
        cost_estimate=pl.CostEstimate(flops=500_000, bytes_accessed=1_200_000, transcendentals=0),
        name="plane_sum",
    )(bands)


def row_body(bands, out, value, sems):
    for begin in range(0, ROWS, 64):
        rows = slice(begin, min(begin + 64, ROWS))
        value[rows, :] = band_total(bands, rows)
    stores = [pltpu.make_async_copy(value, out.at[i], sems.at[i]) for i in range(BANDS)]
    for store in stores:
        store.start()
    for store in stores:
        store.wait()


def row_call(bands):
    return pl.pallas_call(
        row_body,
        out_shape=pltpu.HBM((BANDS, ROWS, 128), BF16),
        in_specs=[VMEM],
        out_specs=ANY,
        scratch_shapes=[pltpu.VMEM((ROWS, 128), BF16), pltpu.SemaphoreType.DMA((BANDS,))],
        compiler_params=pltpu.CompilerParams(vmem_limit_bytes=4 << 20),
        cost_estimate=pl.CostEstimate(flops=500_000, bytes_accessed=1_200_000, transcendentals=0),
        name="row_sum",
    )(bands)


def unpack_half(source, joined):
    for index in range(3):
        for part in range(2):
            for panel in range(3):
                start = ((index * 2 + part) * 3 + panel) * HALF
                joined[index, :, part * NB + panel * 128 : part * NB + (panel + 1) * 128] = source[
                    start : start + HALF, :
                ]


def direct(index, role, half, joined, table, magnon):
    rows = pl.ds(pl.multiple_of(half * HALF, HALF), HALF)
    value = jnp.dot(joined[index], table[role], preferred_element_type=F32)
    magnon[index, rows, :] = value.astype(BF16).astype(F32)


def transposed(index, role, half, joined, table):
    value = None
    for part in range(2):
        turned = joined[index, :, part * NB : (part + 1) * NB].astype(F32).T.astype(BF16)
        these = pl.ds(pl.multiple_of(part * NB + half * HALF, HALF), HALF)
        term = jnp.dot(turned, table[role, these, :], preferred_element_type=F32)
        value = term if value is None else value + term
    return value


def start_body(
    place, offsets, mine, free, own, mate,
    slots, magnon, sums, table, plain, joined, sems,
):
    core = place[0]
    roles = offset_roles(offsets)
    tables = [
        pltpu.make_async_copy(free.at[k], plain.at[role], sems.at[role])
        for role, k in enumerate(roles)
    ]
    loads = [
        pltpu.make_async_copy(own, slots.at[pl.ds(4, 4)], sems.at[4]),
        pltpu.make_async_copy(mate, slots.at[pl.ds(8 - 8 * core, 4)], sems.at[5]),
    ]
    for load in tables + loads:
        load.start()
    unpack_half(mine, joined)
    for role in range(4):
        tables[role].wait()
        fr = plain[role, 0]
        fi = plain[role, 1]
        table[role, :NB, :NB] = fr
        table[role, :NB, NB:] = fi
        table[role, NB:, :NB] = -fi
        table[role, NB:, NB:] = fr
        if role == 0:
            direct(0, 0, core, joined, table, magnon)
        elif role == 1:
            sums[0] = transposed(0, 1, core, joined, table)
        else:

            @pl.when(offsets[roles[role]] > 0)
            def _():
                direct(role - 1, role, core, joined, table, magnon)

            @pl.when(offsets[roles[role]] < 0)
            def _():
                sums[role - 1] = transposed(role - 1, role, core, joined, table)

    for load in loads:
        load.wait()


def start_call(place, offsets, mine, free, own, mate):
    size = 2 * NB
    return pl.pallas_call(
        start_body,
        out_shape=(
            jax.ShapeDtypeStruct((12, 2, NB, NB), BF16),
            jax.ShapeDtypeStruct((3, NB, size), F32),
            jax.ShapeDtypeStruct((3, NB, size), F32),
            jax.ShapeDtypeStruct((4, size, size), BF16),
        ),
        in_specs=[SMEM, SMEM, VMEM] + [ANY] * 3,
        out_specs=(VMEM,) * 4,
        scratch_shapes=[
            pltpu.VMEM((4, 2, NB, NB), BF16),
            pltpu.VMEM((3, HALF, size), BF16),
            pltpu.SemaphoreType.DMA((6,)),
        ],
        compiler_params=pltpu.CompilerParams(vmem_limit_bytes=10 << 20),
        cost_estimate=pl.CostEstimate(
            flops=1_000_000_000, bytes_accessed=10_000_000, transcendentals=0
        ),
        name="final_start",
    )(place, offsets, mine, *(in_hbm(x) for x in (free, own, mate)))


def final_body(
    place, side_of, offsets, other, near, far_cross, far_row, early, late, slots_in, magnon_in, sums, table,
    out, slots, magnon, joined, result, sems,
):
    core = place[0]
    loads = [
        pltpu.make_async_copy(near, slots.at[pl.ds(2 + 6 * core, 2)], sems.at[5]),
        pltpu.make_async_copy(far_cross, slots.at[pl.ds(10 * core, 2)], sems.at[6]),
        pltpu.make_async_copy(far_row, slots.at[pl.ds(10 * core, 2)], sems.at[6]),
    ]
    crossing = side_of[0] == core
    loads[0].start()
    pl.when(crossing)(loads[1].start)
    pl.when(jnp.logical_not(crossing))(loads[2].start)
    unpack_half(other, joined)
    roles = offset_roles(offsets)
    _, _, first, last = roles
    half = 1 - core
    direct(0, 0, half, joined, table, magnon)
    total = sums[0] + transposed(0, 1, half, joined, table)
    magnon[0] += total.astype(BF16).astype(F32)
    for role in (2, 3):

        @pl.when(offsets[roles[role]] > 0)
        def _():
            direct(role - 1, role, half, joined, table, magnon)

        @pl.when(offsets[roles[role]] < 0)
        def _():
            total = sums[role - 1] + transposed(role - 1, role, half, joined, table)
            magnon[role - 1] = total.astype(BF16).astype(F32)

    for load in loads[:2]:
        load.wait()
    reach = spans(offsets, first, last)
    stores = []
    for item, energy in enumerate((2 - 2 * core, 3 - 2 * core, 2 * core, 2 * core + 1)):
        born = early if item < 2 else late

        @pl.loop(0, NB // 32)
        def _(block):
            rows = pl.ds(pl.multiple_of(block * 32, 32), 32)
            begin = pl.ds(pl.multiple_of((item % 2) * NB + block * 32, 32), 32)
            real = born[begin, :NB].astype(F32)
            imag = born[begin, NB:].astype(F32)
            for index in range(3):
                down = energy + 4 - reach[index]
                up = energy + 4 + reach[index]
                sr = slots[down, 0, rows, :].astype(F32) + slots[up, 0, rows, :].astype(F32)
                si = slots[down, 1, rows, :].astype(F32) + slots[up, 1, rows, :].astype(F32)
                mr = magnon[index, rows, :NB]
                mi = magnon[index, rows, NB:]
                real += mr * sr - mi * si
                imag += mr * si + mi * sr
            result[item, 0, rows, :] = real.astype(BF16)
            result[item, 1, rows, :] = imag.astype(BF16)

        store = pltpu.make_async_copy(result.at[item], out.at[energy, 0], sems.at[item])
        store.start()
        stores.append(store)
    for store in stores:
        store.wait()


def final_call(place, side_of, offsets, other, near, far_cross, far_row, early, late, slots, magnon, sums, table):
    size = 2 * NB
    return pl.pallas_call(
        final_body,
        out_shape=(
            jax.ShapeDtypeStruct((4, 1, 2, NB, NB), BF16),
            jax.ShapeDtypeStruct(slots.shape, BF16),
            jax.ShapeDtypeStruct(magnon.shape, F32),
        ),
        in_specs=[SMEM, SMEM, SMEM, VMEM, ANY, ANY, ANY] + [VMEM] * 6,
        out_specs=(ANY, VMEM, VMEM),
        input_output_aliases={9: 1, 10: 2},
        scratch_shapes=[
            pltpu.VMEM((3, HALF, size), BF16),
            pltpu.VMEM((4, 2, NB, NB), BF16),
            pltpu.SemaphoreType.DMA((7,)),
        ],
        compiler_params=pltpu.CompilerParams(vmem_limit_bytes=12 << 20),
        cost_estimate=pl.CostEstimate(
            flops=1_000_000_000, bytes_accessed=18_000_000, transcendentals=0
        ),
        name="final",
    )(place, side_of, offsets, other, in_hbm(near), in_hbm(far_cross), in_hbm(far_row), early, late, slots, magnon, sums, table)[0]


def per_device(green_blocks, offsets, occupation, coupling, vertex, magnon_free):
    count = lax.axis_size(ENERGY)
    core = lax.axis_index("core").astype(jnp.int32)
    place = core[None]
    side_of = lax.axis_index("xh").astype(jnp.int32)[None]
    own = green_blocks.reshape(4, 2, NB, NB)
    across = [(i, i + 1) for i in range(1, count - 1, 2)]
    across += [(target, source) for source, target in across]
    rowwise = [(i, j) for i, j in across if min(i, j) % 4 == 1]
    crosswise = [(i, j) for i, j in across if min(i, j) % 4 == 3]
    along = [(i, i + 2) for i in range(1, count - 2, 2)]
    along += [(i + 1, i - 1) for i in range(1, count - 2, 2)]
    to_same, to_cross = edge_call(place, own)
    cross = lax.ppermute(to_cross, ENERGY, across)
    same = lax.ppermute(to_same, ENERGY, along)
    mate = lax.ppermute(own, "core", SWAP)
    inner = cut_call(place, own, 2, -2)
    far_cross = lax.ppermute(inner, ENERGY, crosswise)
    far_row = lax.ppermute(inner, ENERGY, rowwise)
    chip, turned, partial = prepare_call(place, offsets, own, mate)
    pair = polar_call(place, offsets, same, cross, chip, turned, partial)
    swapped = lax.ppermute(same, "core", SWAP)
    near = near_call(place, swapped, cross)
    bands = lax.all_to_all(pair.reshape(BANDS, ROWS, 128), PLANE, 0, 0, tiled=True)
    early = born_call(place, offsets, occupation, coupling, (own, mate, near), vertex)
    copies = plane_call(bands)
    bands = lax.all_to_all(copies, ROW, 0, 0, tiled=True)
    copies = row_call(bands)
    mine = lax.all_to_all(copies, PLANE, 0, 0, tiled=True).reshape(FLAT, 128)
    late = born_call(
        place, offsets, occupation, coupling, (own, mate, near, far_cross, far_row), vertex, side_of
    )
    other = lax.ppermute(mine, "core", SWAP)
    held = start_call(place, offsets, mine, magnon_free, own, mate)
    return final_call(place, side_of, offsets, other, near, far_cross, far_row, early, late, *held)


def solution(mesh):
    fine = Mesh(mesh.devices.reshape(4, 2, 2, 2, 4), ("y", "xh", "core", "xl", "z"))
    blocks = P(ENERGY, LAYER, None, None, None)
    placed = (blocks, P(), P(), P(LAYER, None), P(), P())
    return jax.shard_map(
        per_device, mesh=fine, in_specs=placed, out_specs=blocks, check_vma=False
    )
```

```python
import jax
import jax.numpy as jnp
from jax import lax
from jax.experimental import pallas as pl
from jax.experimental.pallas import tpu as pltpu
from jax.sharding import Mesh
from jax.sharding import PartitionSpec as P


NB = 384
HALF = NB // 2
BANDS = 16
ROWS = 18 * HALF // BANDS
FLAT = BANDS * ROWS
F32 = jnp.float32
BF16 = jnp.bfloat16
SWAP = [(0, 1), (1, 0)]
PLANE = ("y", "z")
ROW = ("xh", "xl")
ENERGY = ("y", "xh", "core")
LAYER = ("xl", "z")
ANY = pl.BlockSpec(memory_space=pl.ANY)
SMEM = pl.BlockSpec(memory_space=pltpu.SMEM)
VMEM = pl.BlockSpec(memory_space=pltpu.VMEM)


def in_hbm(array):
    return pltpu.with_memory_space_constraint(array, pltpu.HBM)


def in_vmem(array):
    return pltpu.with_memory_space_constraint(array, pltpu.VMEM)


def first_index(offsets, value):
    return jnp.where(
        offsets[0] == value, 0, jnp.where(offsets[1] == value, 1, jnp.where(offsets[2] == value, 2, 3))
    )


def offset_roles(offsets):
    top = first_index(offsets, 4)
    bottom = first_index(offsets, -4)
    low = jnp.minimum(top, bottom)
    high = jnp.maximum(top, bottom)
    first = jnp.where(low != 0, 0, jnp.where(high != 1, 1, 2))
    last = jnp.where(high != 3, 3, jnp.where(low != 2, 2, 1))
    return top, bottom, first, last


def spans(offsets, first, last):
    return (jnp.int32(4), jnp.abs(offsets[first]), jnp.abs(offsets[last]))


def cut_body(place, base, sign, own, out, sem):
    copy = pltpu.make_async_copy(own.at[pl.ds(base + sign * place[0], out.shape[0])], out, sem)
    copy.start()
    copy.wait()


def cut_call(place, own, base, sign, size):
    return pl.pallas_call(
        lambda place, own, out, sem: cut_body(place, base, sign, own, out, sem),
        out_shape=jax.ShapeDtypeStruct((size, 2, NB, NB), BF16),
        in_specs=[SMEM, ANY],
        out_specs=VMEM,
        scratch_shapes=[pltpu.SemaphoreType.DMA],
        compiler_params=pltpu.CompilerParams(vmem_limit_bytes=4 << 20),
        cost_estimate=pl.CostEstimate(flops=0, bytes_accessed=2_400_000, transcendentals=0),
    )(place, in_hbm(own))


def edge_body(place, own, same, cross, whole, sems):
    core = place[0]

    @pl.when(core == 1)
    def _():
        copies = [
            pltpu.make_async_copy(own.at[pl.ds(2, 2), :, pl.ds(HALF, HALF), :], same, sems.at[0]),
            pltpu.make_async_copy(own.at[pl.ds(2, 2), :, pl.ds(0, HALF), :], cross, sems.at[1]),
        ]
        for copy in copies:
            copy.start()
        for copy in copies:
            copy.wait()

    @pl.when(core == 0)
    def _():
        copy = pltpu.make_async_copy(own.at[pl.ds(0, 2)], whole, sems.at[0])
        copy.start()
        copy.wait()
        for item in range(2):
            for part in range(2):
                value = whole[item, part].astype(F32).T.astype(BF16)
                same[item, part] = value[:HALF]
                cross[item, part] = value[HALF:]


def edge_call(place, own):
    half = jax.ShapeDtypeStruct((2, 2, HALF, NB), BF16)
    return pl.pallas_call(
        edge_body,
        out_shape=(half, half),
        in_specs=[SMEM, ANY],
        out_specs=(VMEM, VMEM),
        scratch_shapes=[pltpu.VMEM((2, 2, NB, NB), BF16), pltpu.SemaphoreType.DMA((2,))],
        compiler_params=pltpu.CompilerParams(vmem_limit_bytes=6 << 20),
        cost_estimate=pl.CostEstimate(flops=0, bytes_accessed=2_400_000, transcendentals=0),
        name="edge",
    )(place, in_hbm(own))


def prepare_body(place, offsets, own, mate, chip, turned, partial, sems):
    core = place[0]
    copies = [
        pltpu.make_async_copy(own, chip.at[pl.ds(4 * core, 4)], sems.at[0]),
        pltpu.make_async_copy(mate, chip.at[pl.ds(4 - 4 * core, 4)], sems.at[1]),
    ]
    for copy in copies:
        copy.start()
    for copy in copies:
        copy.wait()

    @pl.loop(2, 16)
    def _(step):
        turned[step // 2, step % 2] = chip[step // 2, step % 2].astype(F32).T

    _, _, first, last = offset_roles(offsets)
    for index, span in enumerate(spans(offsets, first, last)):

        @pl.loop(0, HALF // 32)
        def _(block):
            rows = pl.ds(pl.multiple_of(block * 32, 32), 32)
            there = pl.ds(pl.multiple_of(core * HALF + block * 32, 32), 32)

            def step(s, carry):
                real, imag = carry
                ar = chip[s, 0, there, :].astype(F32)
                ai = chip[s, 1, there, :].astype(F32)
                br = turned[s + span, 0, there, :]
                bi = turned[s + span, 1, there, :]
                return real + (ar * br - ai * bi), imag + (ar * bi + ai * br)

            zero = jnp.zeros((32, NB), F32)
            real, imag = lax.fori_loop(0, 8 - span, step, (zero, zero))
            partial[index, 0, rows, :] = real
            partial[index, 1, rows, :] = imag


def prepare_call(place, offsets, own, mate):
    return pl.pallas_call(
        prepare_body,
        out_shape=(
            jax.ShapeDtypeStruct((8, 2, NB, NB), BF16),
            jax.ShapeDtypeStruct((8, 2, NB, NB), F32),
            jax.ShapeDtypeStruct((3, 2, HALF, NB), F32),
        ),
        in_specs=[SMEM, SMEM, ANY, ANY],
        out_specs=(VMEM, VMEM, VMEM),
        scratch_shapes=[pltpu.SemaphoreType.DMA((2,))],
        compiler_params=pltpu.CompilerParams(vmem_limit_bytes=4 << 20),
        cost_estimate=pl.CostEstimate(flops=20_000_000, bytes_accessed=9_000_000, transcendentals=0),
        name="prepare",
    )(place, offsets, own, mate)


def polar_body(place, offsets, same, cross, chip, turned, partial, out, flat, sems):
    core = place[0]

    def run(edges):
        _, _, first, last = offset_roles(offsets)
        for index, span in enumerate(spans(offsets, first, last)):

            @pl.loop(0, HALF // 32)
            def _(block):
                rows = pl.ds(pl.multiple_of(block * 32, 32), 32)
                there = pl.ds(pl.multiple_of(core * HALF + block * 32, 32), 32)

                def multiply(carry, ar, ai, br, bi):
                    real, imag = carry
                    return real + (ar * br - ai * bi), imag + (ar * bi + ai * br)

                def before(j, carry):
                    ar = edges[0][1 - j, 0, rows, :].astype(F32)
                    ai = edges[0][1 - j, 1, rows, :].astype(F32)
                    if index > 0:
                        keep = jnp.where(span > 2 + j, 1.0, 0.0)
                        ar, ai = ar * keep, ai * keep
                    at = jnp.maximum(span - 1 - j, 1)
                    return multiply(carry, ar, ai, turned[at, 0, there, :], turned[at, 1, there, :])

                def after(j, carry):
                    at = jnp.minimum(8 - span + j, 7)
                    ar = chip[at, 0, there, :].astype(F32)
                    ai = chip[at, 1, there, :].astype(F32)
                    if index > 0 and j > 0:
                        keep = jnp.where(span > j, 1.0, 0.0)
                        ar, ai = ar * keep, ai * keep
                    return multiply(
                        carry,
                        ar,
                        ai,
                        edges[1][j, 0, rows, :].astype(F32),
                        edges[1][j, 1, rows, :].astype(F32),
                    )

                pair = (partial[index, 0, rows, :], partial[index, 1, rows, :])
                for j in range(2):
                    pair = before(j, pair)
                for j in range(2):
                    pair = after(j, pair)
                for part, value in enumerate(pair):
                    for panel in range(3):
                        start = ((index * 2 + part) * 3 + panel) * HALF
                        flat[pl.ds(pl.multiple_of(start + block * 32, 32), 32), :] = value[
                            :, panel * 128 : (panel + 1) * 128
                        ].astype(BF16)

            done = pl.ds(index * 6 * HALF, 6 * HALF)
            store = pltpu.make_async_copy(flat.at[done], out.at[done], sems.at[index])
            store.start()

    @pl.when(core == 0)
    def _():
        run((cross, same))

    @pl.when(core == 1)
    def _():
        run((same, cross))

    for index in range(3):
        done = pl.ds(index * 6 * HALF, 6 * HALF)
        pltpu.make_async_copy(flat.at[done], out.at[done], sems.at[index]).wait()


def polar_call(place, offsets, same, cross, chip, turned, partial):
    return pl.pallas_call(
        polar_body,
        out_shape=pltpu.HBM((FLAT, 128), BF16),
        in_specs=[SMEM, SMEM, VMEM, VMEM, VMEM, VMEM, VMEM],
        out_specs=ANY,
        scratch_shapes=[
            pltpu.VMEM((FLAT, 128), BF16),
            pltpu.SemaphoreType.DMA((3,)),
        ],
        compiler_params=pltpu.CompilerParams(vmem_limit_bytes=6 << 20),
        cost_estimate=pl.CostEstimate(flops=20_000_000, bytes_accessed=9_000_000, transcendentals=0),
        name="polar",
    )(place, offsets, in_vmem(same), in_vmem(cross), chip, turned, partial)


def near_body(place, swapped, cross, out, sems):
    core = place[0]
    copies = [
        pltpu.make_async_copy(cross, out.at[:, :, pl.ds(core * HALF, HALF), :], sems.at[0]),
        pltpu.make_async_copy(
            swapped, out.at[:, :, pl.ds(HALF - core * HALF, HALF), :], sems.at[1]
        ),
    ]
    for copy in copies:
        copy.start()
    for copy in copies:
        copy.wait()

    @pl.when(core == 1)
    def _():
        for item in range(2):
            for part in range(2):
                out[item, part] = out[item, part].astype(F32).T.astype(BF16)


def near_call(place, swapped, cross):
    return pl.pallas_call(
        near_body,
        out_shape=jax.ShapeDtypeStruct((2, 2, NB, NB), BF16),
        in_specs=[SMEM, ANY, ANY],
        out_specs=VMEM,
        scratch_shapes=[pltpu.SemaphoreType.DMA((2,))],
        compiler_params=pltpu.CompilerParams(vmem_limit_bytes=4 << 20),
        cost_estimate=pl.CostEstimate(flops=0, bytes_accessed=2_400_000, transcendentals=0),
        name="near_join",
    )(place, swapped, in_hbm(cross))


def born_body(early, *refs):
    refs = list(refs)
    place, offsets, occupation, coupling, own, mate, near = refs[:7]
    refs = refs[7:]
    fars = () if early else (refs.pop(0), refs.pop(0), refs.pop(0))
    side_of = None if early else refs.pop(0)
    vertex, out, chosen, lows, highs, mixed, wide, stack, side, total, rounded, sems = refs
    core = place[0]
    energy = 2 * (1 - core) if early else 2 * core

    def fetch(slot, target, sem):
        sources = [(own, 4, 4), (mate, 8 - 8 * core, 4), (near, 2 + 6 * core, 2)]
        if fars:
            crossing = side_of[0] == core
            sources.append((fars[0], jnp.where(crossing, 10 * core, 16), 2))
            sources.append((fars[1], jnp.where(crossing, 16, 10 * core), 1))
            sources.append((fars[2], jnp.where(crossing, 16, 10 * core + 1), 1))
        for source, low, size in sources:

            @pl.when((slot >= low) & (slot < low + size))
            def _():
                pltpu.make_async_copy(source.at[slot - low], target, sem).start()

    for k in range(4):
        pltpu.make_async_copy(vertex.at[coupling[0, k]], chosen.at[k], sems.at[k, 4]).start()
        for item in range(2):
            at = energy + 4 + item
            fetch(at - offsets[k], lows.at[k, item], sems.at[k, 2 * item])
            fetch(at + offsets[k], highs.at[k, item], sems.at[k, 2 * item + 1])

    total[...] = jnp.zeros_like(total)

    @pl.loop(0, 4)
    def _(k):
        pltpu.make_async_copy(vertex.at[0], chosen.at[k], sems.at[k, 4]).wait()
        vr = chosen[k, 0]
        vi = chosen[k, 1]
        wide[:NB, :NB] = vr
        wide[:NB, NB:] = -vi
        wide[NB:, :NB] = vi
        wide[NB:, NB:] = vr
        side[:NB, :NB] = vr
        side[:NB, NB:] = vi
        side[NB:, :NB] = -vi
        side[NB:, NB:] = vr
        weight = occupation[k]
        for item in range(2):
            pltpu.make_async_copy(own.at[0], lows.at[k, item], sems.at[k, 2 * item]).wait()
            pltpu.make_async_copy(own.at[0], highs.at[k, item], sems.at[k, 2 * item + 1]).wait()
        for item in range(2):
            for part in range(2):
                low = lows[k, item, part].astype(F32)
                high = highs[k, item, part].astype(F32)
                value = weight * low + (weight + 1.0) * high
                mixed[part * NB : (part + 1) * NB, item * NB : (item + 1) * NB] = value.astype(BF16)
        for piece in range(2):
            begin = piece * 384
            part, row = begin // NB, begin % NB
            half = jnp.dot(
                wide[begin : begin + 384, :], mixed[...], preferred_element_type=F32
            ).astype(BF16)
            for item in range(2):
                stack[item * NB + row : item * NB + row + 384, part * NB : (part + 1) * NB] = half[
                    :, item * NB : (item + 1) * NB
                ]
        for piece in range(2):
            rows = slice(piece * 384, (piece + 1) * 384)
            term = lax.dot_general(
                stack[rows, :], side[...], (((1,), (1,)), ((), ())), preferred_element_type=F32
            )
            total[rows, :] += term

    stores = []
    for piece in range(2):
        rows = slice(piece * NB, (piece + 1) * NB)
        rounded[rows, :] = total[rows, :].astype(BF16)
        store = pltpu.make_async_copy(rounded.at[rows], out.at[rows], sems.at[piece, 0])
        store.start()
        stores.append(store)
    for store in stores:
        store.wait()


def born_call(place, offsets, occupation, coupling, arrays, vertex, *extra):
    early = len(arrays) == 3
    size = 2 * NB
    held = (*map(in_hbm, arrays[:2]), *arrays[2:])
    shape = (size, size)
    return pl.pallas_call(
        lambda *refs: born_body(early, *refs),
        out_shape=pltpu.HBM(shape, BF16),
        in_specs=[SMEM] * 4 + [ANY] * len(arrays) + [SMEM] * len(extra) + [ANY],
        out_specs=ANY,
        scratch_shapes=[
            pltpu.VMEM((4, 2, NB, NB), BF16),
            pltpu.VMEM((4, 2, 2, NB, NB), BF16),
            pltpu.VMEM((4, 2, 2, NB, NB), BF16),
            pltpu.VMEM((size, size), BF16),
            pltpu.VMEM((size, size), BF16),
            pltpu.VMEM((size, size), BF16),
            pltpu.VMEM((size, size), BF16),
            pltpu.VMEM((size, size), F32),
            pltpu.VMEM((size, size), BF16),
            pltpu.SemaphoreType.DMA((4, 5)),
        ],
        compiler_params=pltpu.CompilerParams(vmem_limit_bytes=22 << 20),
        cost_estimate=pl.CostEstimate(
            flops=16 * size**3, bytes_accessed=12_000_000, transcendentals=0
        ),
        name="born_early" if early else "born_late",
    )(place, offsets, occupation, coupling, *held, *extra, in_hbm(vertex))


def band_total(bands, rows):
    total = bands[0, rows, :].astype(F32)
    for i in range(1, bands.shape[0]):
        total += bands[i, rows, :].astype(F32)
    return total.astype(BF16)


def plane_body(bands, out):
    for begin in range(0, ROWS, 64):
        rows = slice(begin, min(begin + 64, ROWS))
        value = band_total(bands, rows)
        for i in range(out.shape[0]):
            out[i, rows, :] = value


def plane_call(bands):
    return pl.pallas_call(
        plane_body,
        out_shape=jax.ShapeDtypeStruct((4, ROWS, 128), BF16),
        in_specs=[VMEM],
        out_specs=VMEM,
        compiler_params=pltpu.CompilerParams(vmem_limit_bytes=4 << 20),
        cost_estimate=pl.CostEstimate(flops=500_000, bytes_accessed=1_200_000, transcendentals=0),
        name="plane_sum",
    )(bands)


def row_body(bands, out, value, sems):
    for begin in range(0, ROWS, 64):
        rows = slice(begin, min(begin + 64, ROWS))
        value[rows, :] = band_total(bands, rows)
    stores = [pltpu.make_async_copy(value, out.at[i], sems.at[i]) for i in range(BANDS)]
    for store in stores:
        store.start()
    for store in stores:
        store.wait()


def row_call(bands):
    return pl.pallas_call(
        row_body,
        out_shape=pltpu.HBM((BANDS, ROWS, 128), BF16),
        in_specs=[VMEM],
        out_specs=ANY,
        scratch_shapes=[pltpu.VMEM((ROWS, 128), BF16), pltpu.SemaphoreType.DMA((BANDS,))],
        compiler_params=pltpu.CompilerParams(vmem_limit_bytes=4 << 20),
        cost_estimate=pl.CostEstimate(flops=500_000, bytes_accessed=1_200_000, transcendentals=0),
        name="row_sum",
    )(bands)


def unpack_half(source, joined):
    for index in range(3):
        for part in range(2):
            for panel in range(3):
                start = ((index * 2 + part) * 3 + panel) * HALF
                joined[index, :, part * NB + panel * 128 : part * NB + (panel + 1) * 128] = source[
                    start : start + HALF, :
                ]


def direct(index, role, half, joined, table, magnon):
    rows = pl.ds(pl.multiple_of(half * HALF, HALF), HALF)
    value = jnp.dot(joined[index], table[role], preferred_element_type=F32)
    magnon[index, rows, :] = value.astype(BF16).astype(F32)


def transposed(index, role, half, joined, table):
    value = None
    for part in range(2):
        turned = joined[index, :, part * NB : (part + 1) * NB].astype(F32).T.astype(BF16)
        these = pl.ds(pl.multiple_of(part * NB + half * HALF, HALF), HALF)
        term = jnp.dot(turned, table[role, these, :], preferred_element_type=F32)
        value = term if value is None else value + term
    return value


def start_body(
    place, offsets, mine, free, own, mate,
    slots, magnon, sums, table, plain, joined, sems,
):
    core = place[0]
    roles = offset_roles(offsets)
    tables = [
        pltpu.make_async_copy(free.at[k], plain.at[role], sems.at[role])
        for role, k in enumerate(roles)
    ]
    loads = [
        pltpu.make_async_copy(own, slots.at[pl.ds(4, 4)], sems.at[4]),
        pltpu.make_async_copy(mate, slots.at[pl.ds(8 - 8 * core, 4)], sems.at[5]),
    ]
    for load in tables + loads:
        load.start()
    unpack_half(mine, joined)
    for role in range(4):
        tables[role].wait()
        fr = plain[role, 0]
        fi = plain[role, 1]
        table[role, :NB, :NB] = fr
        table[role, :NB, NB:] = fi
        table[role, NB:, :NB] = -fi
        table[role, NB:, NB:] = fr
        if role == 0:
            direct(0, 0, core, joined, table, magnon)
        elif role == 1:
            sums[0] = transposed(0, 1, core, joined, table)
        else:

            @pl.when(offsets[roles[role]] > 0)
            def _():
                direct(role - 1, role, core, joined, table, magnon)

            @pl.when(offsets[roles[role]] < 0)
            def _():
                sums[role - 1] = transposed(role - 1, role, core, joined, table)

    for load in loads:
        load.wait()


def start_call(place, offsets, mine, free, own, mate):
    size = 2 * NB
    return pl.pallas_call(
        start_body,
        out_shape=(
            jax.ShapeDtypeStruct((12, 2, NB, NB), BF16),
            jax.ShapeDtypeStruct((3, NB, size), F32),
            jax.ShapeDtypeStruct((3, NB, size), F32),
            jax.ShapeDtypeStruct((4, size, size), BF16),
        ),
        in_specs=[SMEM, SMEM, VMEM] + [ANY] * 3,
        out_specs=(VMEM,) * 4,
        scratch_shapes=[
            pltpu.VMEM((4, 2, NB, NB), BF16),
            pltpu.VMEM((3, HALF, size), BF16),
            pltpu.SemaphoreType.DMA((6,)),
        ],
        compiler_params=pltpu.CompilerParams(vmem_limit_bytes=10 << 20),
        cost_estimate=pl.CostEstimate(
            flops=1_000_000_000, bytes_accessed=10_000_000, transcendentals=0
        ),
        name="final_start",
    )(place, offsets, mine, *(in_hbm(x) for x in (free, own, mate)))


def final_body(
    place, side_of, offsets, other, near, far_cross, far_soon, far_late, early, late, slots_in, magnon_in, sums, table,
    out, slots, magnon, joined, result, sems,
):
    core = place[0]
    loads = [
        pltpu.make_async_copy(near, slots.at[pl.ds(2 + 6 * core, 2)], sems.at[5]),
        pltpu.make_async_copy(far_cross, slots.at[pl.ds(10 * core, 2)], sems.at[6]),
        pltpu.make_async_copy(far_soon, slots.at[pl.ds(10 * core, 1)], sems.at[6]),
        pltpu.make_async_copy(far_late, slots.at[pl.ds(10 * core + 1, 1)], sems.at[6]),
    ]
    crossing = side_of[0] == core
    loads[0].start()
    pl.when(crossing)(loads[1].start)
    pl.when(jnp.logical_not(crossing))(loads[2].start)
    pl.when(jnp.logical_not(crossing))(loads[3].start)
    unpack_half(other, joined)
    roles = offset_roles(offsets)
    _, _, first, last = roles
    half = 1 - core
    direct(0, 0, half, joined, table, magnon)
    total = sums[0] + transposed(0, 1, half, joined, table)
    magnon[0] += total.astype(BF16).astype(F32)
    for role in (2, 3):

        @pl.when(offsets[roles[role]] > 0)
        def _():
            direct(role - 1, role, half, joined, table, magnon)

        @pl.when(offsets[roles[role]] < 0)
        def _():
            total = sums[role - 1] + transposed(role - 1, role, half, joined, table)
            magnon[role - 1] = total.astype(BF16).astype(F32)

    for load in loads[:2]:
        load.wait()
    reach = spans(offsets, first, last)
    stores = []
    for item, energy in enumerate((2 - 2 * core, 3 - 2 * core, 2 * core, 2 * core + 1)):
        born = early if item < 2 else late

        @pl.loop(0, NB // 32)
        def _(block):
            rows = pl.ds(pl.multiple_of(block * 32, 32), 32)
            begin = pl.ds(pl.multiple_of((item % 2) * NB + block * 32, 32), 32)
            real = born[begin, :NB].astype(F32)
            imag = born[begin, NB:].astype(F32)
            for index in range(3):
                down = energy + 4 - reach[index]
                up = energy + 4 + reach[index]
                sr = slots[down, 0, rows, :].astype(F32) + slots[up, 0, rows, :].astype(F32)
                si = slots[down, 1, rows, :].astype(F32) + slots[up, 1, rows, :].astype(F32)
                mr = magnon[index, rows, :NB]
                mi = magnon[index, rows, NB:]
                real += mr * sr - mi * si
                imag += mr * si + mi * sr
            result[item, 0, rows, :] = real.astype(BF16)
            result[item, 1, rows, :] = imag.astype(BF16)

        store = pltpu.make_async_copy(result.at[item], out.at[energy, 0], sems.at[item])
        store.start()
        stores.append(store)
    for store in stores:
        store.wait()


def final_call(place, side_of, offsets, other, near, far_cross, far_soon, far_late, early, late, slots, magnon, sums, table):
    size = 2 * NB
    return pl.pallas_call(
        final_body,
        out_shape=(
            jax.ShapeDtypeStruct((4, 1, 2, NB, NB), BF16),
            jax.ShapeDtypeStruct(slots.shape, BF16),
            jax.ShapeDtypeStruct(magnon.shape, F32),
        ),
        in_specs=[SMEM, SMEM, SMEM, VMEM, ANY, ANY, ANY, ANY] + [VMEM] * 6,
        out_specs=(ANY, VMEM, VMEM),
        input_output_aliases={10: 1, 11: 2},
        scratch_shapes=[
            pltpu.VMEM((3, HALF, size), BF16),
            pltpu.VMEM((4, 2, NB, NB), BF16),
            pltpu.SemaphoreType.DMA((7,)),
        ],
        compiler_params=pltpu.CompilerParams(vmem_limit_bytes=12 << 20),
        cost_estimate=pl.CostEstimate(
            flops=1_000_000_000, bytes_accessed=18_000_000, transcendentals=0
        ),
        name="final",
    )(place, side_of, offsets, other, in_hbm(near), in_hbm(far_cross), in_hbm(far_soon), in_hbm(far_late), early, late, slots, magnon, sums, table)[0]


def per_device(green_blocks, offsets, occupation, coupling, vertex, magnon_free):
    count = lax.axis_size(ENERGY)
    core = lax.axis_index("core").astype(jnp.int32)
    place = core[None]
    side_of = lax.axis_index("xh").astype(jnp.int32)[None]
    own = green_blocks.reshape(4, 2, NB, NB)
    across = [(i, i + 1) for i in range(1, count - 1, 2)]
    across += [(target, source) for source, target in across]
    rowwise = [(i, j) for i, j in across if min(i, j) % 4 == 1]
    crosswise = [(i, j) for i, j in across if min(i, j) % 4 == 3]
    along = [(i, i + 2) for i in range(1, count - 2, 2)]
    along += [(i + 1, i - 1) for i in range(1, count - 2, 2)]
    to_same, to_cross = edge_call(place, own)
    cross = lax.ppermute(to_cross, ENERGY, across)
    same = lax.ppermute(to_same, ENERGY, along)
    mate = lax.ppermute(own, "core", SWAP)
    inner = cut_call(place, own, 2, -2, 2)
    inner_soon = cut_call(place, own, 2, -2, 1)
    inner_late = cut_call(place, own, 3, -2, 1)
    far_cross = lax.ppermute(inner, ENERGY, crosswise)
    far_soon = lax.ppermute(inner_soon, ENERGY, rowwise)
    far_late = lax.ppermute(inner_late, ENERGY, rowwise)
    chip, turned, partial = prepare_call(place, offsets, own, mate)
    pair = polar_call(place, offsets, same, cross, chip, turned, partial)
    swapped = lax.ppermute(same, "core", SWAP)
    near = near_call(place, swapped, cross)
    bands = lax.all_to_all(pair.reshape(BANDS, ROWS, 128), PLANE, 0, 0, tiled=True)
    early = born_call(place, offsets, occupation, coupling, (own, mate, near), vertex)
    copies = plane_call(bands)
    bands = lax.all_to_all(copies, ROW, 0, 0, tiled=True)
    copies = row_call(bands)
    mine = lax.all_to_all(copies, PLANE, 0, 0, tiled=True).reshape(FLAT, 128)
    late = born_call(
        place, offsets, occupation, coupling, (own, mate, near, far_cross, far_soon, far_late), vertex, side_of
    )
    other = lax.ppermute(mine, "core", SWAP)
    held = start_call(place, offsets, mine, magnon_free, own, mate)
    return final_call(
        place, side_of, offsets, other, near, far_cross, far_soon, far_late, early, late, *held
    )


def solution(mesh):
    fine = Mesh(mesh.devices.reshape(4, 2, 2, 2, 4), ("y", "xh", "core", "xl", "z"))
    blocks = P(ENERGY, LAYER, None, None, None)
    placed = (blocks, P(), P(), P(LAYER, None), P(), P())
    return jax.shard_map(
        per_device, mesh=fine, in_specs=placed, out_specs=blocks, check_vma=False
    )
```

```python
import jax
import jax.numpy as jnp
from jax import lax
from jax.experimental import pallas as pl
from jax.experimental.pallas import tpu as pltpu
from jax.sharding import Mesh
from jax.sharding import PartitionSpec as P


NB = 384
HALF = NB // 2
BANDS = 16
ROWS = 18 * HALF // BANDS
FLAT = BANDS * ROWS
F32 = jnp.float32
BF16 = jnp.bfloat16
SWAP = [(0, 1), (1, 0)]
PLANE = ("y", "z")
ROW = ("xh", "xl")
ENERGY = ("y", "xh", "core")
LAYER = ("xl", "z")
ANY = pl.BlockSpec(memory_space=pl.ANY)
SMEM = pl.BlockSpec(memory_space=pltpu.SMEM)
VMEM = pl.BlockSpec(memory_space=pltpu.VMEM)


def in_hbm(array):
    return pltpu.with_memory_space_constraint(array, pltpu.HBM)


def in_vmem(array):
    return pltpu.with_memory_space_constraint(array, pltpu.VMEM)


def first_index(offsets, value):
    return jnp.where(
        offsets[0] == value, 0, jnp.where(offsets[1] == value, 1, jnp.where(offsets[2] == value, 2, 3))
    )


def offset_roles(offsets):
    top = first_index(offsets, 4)
    bottom = first_index(offsets, -4)
    low = jnp.minimum(top, bottom)
    high = jnp.maximum(top, bottom)
    first = jnp.where(low != 0, 0, jnp.where(high != 1, 1, 2))
    last = jnp.where(high != 3, 3, jnp.where(low != 2, 2, 1))
    return top, bottom, first, last


def spans(offsets, first, last):
    return (jnp.int32(4), jnp.abs(offsets[first]), jnp.abs(offsets[last]))


def cut_body(place, base, sign, own, out, sem):
    copy = pltpu.make_async_copy(own.at[pl.ds(base + sign * place[0], 2)], out, sem)
    copy.start()
    copy.wait()


def cut_call(place, own, base, sign):
    return pl.pallas_call(
        lambda place, own, out, sem: cut_body(place, base, sign, own, out, sem),
        out_shape=jax.ShapeDtypeStruct((2, 2, NB, NB), BF16),
        in_specs=[SMEM, ANY],
        out_specs=VMEM,
        scratch_shapes=[pltpu.SemaphoreType.DMA],
        compiler_params=pltpu.CompilerParams(vmem_limit_bytes=4 << 20),
        cost_estimate=pl.CostEstimate(flops=0, bytes_accessed=2_400_000, transcendentals=0),
    )(place, in_hbm(own))


def edge_body(place, own, same, cross, whole, sems):
    core = place[0]

    @pl.when(core == 1)
    def _():
        copies = [
            pltpu.make_async_copy(own.at[pl.ds(2, 2), :, pl.ds(HALF, HALF), :], same, sems.at[0]),
            pltpu.make_async_copy(own.at[pl.ds(2, 2), :, pl.ds(0, HALF), :], cross, sems.at[1]),
        ]
        for copy in copies:
            copy.start()
        for copy in copies:
            copy.wait()

    @pl.when(core == 0)
    def _():
        copy = pltpu.make_async_copy(own.at[pl.ds(0, 2)], whole, sems.at[0])
        copy.start()
        copy.wait()
        for item in range(2):
            for part in range(2):
                value = whole[item, part].astype(F32).T.astype(BF16)
                same[item, part] = value[:HALF]
                cross[item, part] = value[HALF:]


def edge_call(place, own):
    half = jax.ShapeDtypeStruct((2, 2, HALF, NB), BF16)
    return pl.pallas_call(
        edge_body,
        out_shape=(half, half),
        in_specs=[SMEM, ANY],
        out_specs=(VMEM, VMEM),
        scratch_shapes=[pltpu.VMEM((2, 2, NB, NB), BF16), pltpu.SemaphoreType.DMA((2,))],
        compiler_params=pltpu.CompilerParams(vmem_limit_bytes=6 << 20),
        cost_estimate=pl.CostEstimate(flops=0, bytes_accessed=2_400_000, transcendentals=0),
        name="edge",
    )(place, in_hbm(own))


def prepare_body(place, offsets, own, mate, chip, turned, partial, sems):
    core = place[0]
    copies = [
        pltpu.make_async_copy(own, chip.at[pl.ds(4 * core, 4)], sems.at[0]),
        pltpu.make_async_copy(mate, chip.at[pl.ds(4 - 4 * core, 4)], sems.at[1]),
    ]
    for copy in copies:
        copy.start()
    for copy in copies:
        copy.wait()

    @pl.loop(2, 16)
    def _(step):
        turned[step // 2, step % 2] = chip[step // 2, step % 2].astype(F32).T

    _, _, first, last = offset_roles(offsets)
    for index, span in enumerate(spans(offsets, first, last)):

        @pl.loop(0, HALF // 32)
        def _(block):
            rows = pl.ds(pl.multiple_of(block * 32, 32), 32)
            there = pl.ds(pl.multiple_of(core * HALF + block * 32, 32), 32)

            def step(s, carry):
                real, imag = carry
                ar = chip[s, 0, there, :].astype(F32)
                ai = chip[s, 1, there, :].astype(F32)
                br = turned[s + span, 0, there, :]
                bi = turned[s + span, 1, there, :]
                return real + (ar * br - ai * bi), imag + (ar * bi + ai * br)

            zero = jnp.zeros((32, NB), F32)
            real, imag = lax.fori_loop(0, 8 - span, step, (zero, zero))
            partial[index, 0, rows, :] = real
            partial[index, 1, rows, :] = imag


def prepare_call(place, offsets, own, mate):
    return pl.pallas_call(
        prepare_body,
        out_shape=(
            jax.ShapeDtypeStruct((8, 2, NB, NB), BF16),
            jax.ShapeDtypeStruct((8, 2, NB, NB), F32),
            jax.ShapeDtypeStruct((3, 2, HALF, NB), F32),
        ),
        in_specs=[SMEM, SMEM, ANY, ANY],
        out_specs=(VMEM, VMEM, VMEM),
        scratch_shapes=[pltpu.SemaphoreType.DMA((2,))],
        compiler_params=pltpu.CompilerParams(vmem_limit_bytes=4 << 20),
        cost_estimate=pl.CostEstimate(flops=20_000_000, bytes_accessed=9_000_000, transcendentals=0),
        name="prepare",
    )(place, offsets, own, mate)


def polar_body(place, offsets, same, cross, chip, turned, partial, out, flat, sems):
    core = place[0]

    def run(edges):
        _, _, first, last = offset_roles(offsets)
        for index, span in enumerate(spans(offsets, first, last)):

            @pl.loop(0, HALF // 32)
            def _(block):
                rows = pl.ds(pl.multiple_of(block * 32, 32), 32)
                there = pl.ds(pl.multiple_of(core * HALF + block * 32, 32), 32)

                def multiply(carry, ar, ai, br, bi):
                    real, imag = carry
                    return real + (ar * br - ai * bi), imag + (ar * bi + ai * br)

                def before(j, carry):
                    ar = edges[0][1 - j, 0, rows, :].astype(F32)
                    ai = edges[0][1 - j, 1, rows, :].astype(F32)
                    if index > 0:
                        keep = jnp.where(span > 2 + j, 1.0, 0.0)
                        ar, ai = ar * keep, ai * keep
                    at = jnp.maximum(span - 1 - j, 1)
                    return multiply(carry, ar, ai, turned[at, 0, there, :], turned[at, 1, there, :])

                def after(j, carry):
                    at = jnp.minimum(8 - span + j, 7)
                    ar = chip[at, 0, there, :].astype(F32)
                    ai = chip[at, 1, there, :].astype(F32)
                    if index > 0 and j > 0:
                        keep = jnp.where(span > j, 1.0, 0.0)
                        ar, ai = ar * keep, ai * keep
                    return multiply(
                        carry,
                        ar,
                        ai,
                        edges[1][j, 0, rows, :].astype(F32),
                        edges[1][j, 1, rows, :].astype(F32),
                    )

                pair = (partial[index, 0, rows, :], partial[index, 1, rows, :])
                for j in range(2):
                    pair = before(j, pair)
                for j in range(2):
                    pair = after(j, pair)
                for part, value in enumerate(pair):
                    for panel in range(3):
                        start = ((index * 2 + part) * 3 + panel) * HALF
                        flat[pl.ds(pl.multiple_of(start + block * 32, 32), 32), :] = value[
                            :, panel * 128 : (panel + 1) * 128
                        ].astype(BF16)

            done = pl.ds(index * 6 * HALF, 6 * HALF)
            store = pltpu.make_async_copy(flat.at[done], out.at[done], sems.at[index])
            store.start()

    @pl.when(core == 0)
    def _():
        run((cross, same))

    @pl.when(core == 1)
    def _():
        run((same, cross))

    for index in range(3):
        done = pl.ds(index * 6 * HALF, 6 * HALF)
        pltpu.make_async_copy(flat.at[done], out.at[done], sems.at[index]).wait()


def polar_call(place, offsets, same, cross, chip, turned, partial):
    return pl.pallas_call(
        polar_body,
        out_shape=pltpu.HBM((FLAT, 128), BF16),
        in_specs=[SMEM, SMEM, VMEM, VMEM, VMEM, VMEM, VMEM],
        out_specs=ANY,
        scratch_shapes=[
            pltpu.VMEM((FLAT, 128), BF16),
            pltpu.SemaphoreType.DMA((3,)),
        ],
        compiler_params=pltpu.CompilerParams(vmem_limit_bytes=6 << 20),
        cost_estimate=pl.CostEstimate(flops=20_000_000, bytes_accessed=9_000_000, transcendentals=0),
        name="polar",
    )(place, offsets, in_vmem(same), in_vmem(cross), chip, turned, partial)


def near_body(place, swapped, cross, out, sems):
    core = place[0]
    copies = [
        pltpu.make_async_copy(cross, out.at[:, :, pl.ds(core * HALF, HALF), :], sems.at[0]),
        pltpu.make_async_copy(
            swapped, out.at[:, :, pl.ds(HALF - core * HALF, HALF), :], sems.at[1]
        ),
    ]
    for copy in copies:
        copy.start()
    for copy in copies:
        copy.wait()

    @pl.when(core == 1)
    def _():
        for item in range(2):
            for part in range(2):
                out[item, part] = out[item, part].astype(F32).T.astype(BF16)


def near_call(place, swapped, cross):
    return pl.pallas_call(
        near_body,
        out_shape=jax.ShapeDtypeStruct((2, 2, NB, NB), BF16),
        in_specs=[SMEM, ANY, ANY],
        out_specs=VMEM,
        scratch_shapes=[pltpu.SemaphoreType.DMA((2,))],
        compiler_params=pltpu.CompilerParams(vmem_limit_bytes=4 << 20),
        cost_estimate=pl.CostEstimate(flops=0, bytes_accessed=2_400_000, transcendentals=0),
        name="near_join",
    )(place, swapped, in_hbm(cross))


def born_body(early, *refs):
    refs = list(refs)
    place, offsets, occupation, coupling, own, mate, near = refs[:7]
    refs = refs[7:]
    far = None if early else refs.pop(0)
    vertex, out, chosen, lows, highs, mixed, wide, stack, side, total, rounded, sems = refs
    core = place[0]
    energy = 2 * (1 - core) if early else 2 * core

    def fetch(slot, target, sem):
        sources = [(own, 4, 4), (mate, 8 - 8 * core, 4), (near, 2 + 6 * core, 2)]
        if far is not None:
            sources.append((far, 10 * core, 2))
        for source, low, size in sources:

            @pl.when((slot >= low) & (slot < low + size))
            def _():
                pltpu.make_async_copy(source.at[slot - low], target, sem).start()

    for k in range(4):
        pltpu.make_async_copy(vertex.at[coupling[0, k]], chosen.at[k], sems.at[k, 4]).start()
        for item in range(2):
            at = energy + 4 + item
            fetch(at - offsets[k], lows.at[k, item], sems.at[k, 2 * item])
            fetch(at + offsets[k], highs.at[k, item], sems.at[k, 2 * item + 1])

    total[...] = jnp.zeros_like(total)

    @pl.loop(0, 4)
    def _(k):
        pltpu.make_async_copy(vertex.at[0], chosen.at[k], sems.at[k, 4]).wait()
        vr = chosen[k, 0]
        vi = chosen[k, 1]
        wide[:NB, :NB] = vr
        wide[:NB, NB:] = -vi
        wide[NB:, :NB] = vi
        wide[NB:, NB:] = vr
        side[:NB, :NB] = vr
        side[:NB, NB:] = vi
        side[NB:, :NB] = -vi
        side[NB:, NB:] = vr
        weight = occupation[k]
        for item in range(2):
            pltpu.make_async_copy(own.at[0], lows.at[k, item], sems.at[k, 2 * item]).wait()
            pltpu.make_async_copy(own.at[0], highs.at[k, item], sems.at[k, 2 * item + 1]).wait()
        for item in range(2):
            for part in range(2):
                low = lows[k, item, part].astype(F32)
                high = highs[k, item, part].astype(F32)
                value = weight * low + (weight + 1.0) * high
                mixed[part * NB : (part + 1) * NB, item * NB : (item + 1) * NB] = value.astype(BF16)
        for piece in range(2):
            begin = piece * 384
            part, row = begin // NB, begin % NB
            half = jnp.dot(
                wide[begin : begin + 384, :], mixed[...], preferred_element_type=F32
            ).astype(BF16)
            for item in range(2):
                stack[item * NB + row : item * NB + row + 384, part * NB : (part + 1) * NB] = half[
                    :, item * NB : (item + 1) * NB
                ]
        for piece in range(2):
            rows = slice(piece * 384, (piece + 1) * 384)
            term = lax.dot_general(
                stack[rows, :], side[...], (((1,), (1,)), ((), ())), preferred_element_type=F32
            )
            total[rows, :] += term

    if early:
        rounded[...] = total[...].astype(BF16)
        store = pltpu.make_async_copy(rounded, out, sems.at[0, 0])
        store.start()
        store.wait()
    else:
        out[...] = total[...].astype(BF16)


def born_call(place, offsets, occupation, coupling, arrays, vertex):
    early = len(arrays) == 3
    size = 2 * NB
    held = (*map(in_hbm, arrays[:2]), *arrays[2:])
    shape = (size, size)
    return pl.pallas_call(
        lambda *refs: born_body(early, *refs),
        out_shape=pltpu.HBM(shape, BF16) if early else jax.ShapeDtypeStruct(shape, BF16),
        in_specs=[SMEM] * 4 + [ANY] * (len(held) + 1),
        out_specs=ANY if early else VMEM,
        scratch_shapes=[
            pltpu.VMEM((4, 2, NB, NB), BF16),
            pltpu.VMEM((4, 2, 2, NB, NB), BF16),
            pltpu.VMEM((4, 2, 2, NB, NB), BF16),
            pltpu.VMEM((size, size), BF16),
            pltpu.VMEM((size, size), BF16),
            pltpu.VMEM((size, size), BF16),
            pltpu.VMEM((size, size), BF16),
            pltpu.VMEM((size, size), F32),
            pltpu.VMEM((size, size), BF16),
            pltpu.SemaphoreType.DMA((4, 5)),
        ],
        compiler_params=pltpu.CompilerParams(vmem_limit_bytes=22 << 20),
        cost_estimate=pl.CostEstimate(
            flops=16 * size**3, bytes_accessed=12_000_000, transcendentals=0
        ),
        name="born_early" if early else "born_late",
    )(place, offsets, occupation, coupling, *held, in_hbm(vertex))


def band_total(bands, rows):
    total = bands[0, rows, :].astype(F32)
    for i in range(1, bands.shape[0]):
        total += bands[i, rows, :].astype(F32)
    return total.astype(BF16)


def plane_body(bands, out):
    for begin in range(0, ROWS, 64):
        rows = slice(begin, min(begin + 64, ROWS))
        value = band_total(bands, rows)
        for i in range(out.shape[0]):
            out[i, rows, :] = value


def plane_call(bands):
    return pl.pallas_call(
        plane_body,
        out_shape=jax.ShapeDtypeStruct((4, ROWS, 128), BF16),
        in_specs=[VMEM],
        out_specs=VMEM,
        compiler_params=pltpu.CompilerParams(vmem_limit_bytes=4 << 20),
        cost_estimate=pl.CostEstimate(flops=500_000, bytes_accessed=1_200_000, transcendentals=0),
        name="plane_sum",
    )(bands)


def row_body(bands, out, value, sems):
    for begin in range(0, ROWS, 64):
        rows = slice(begin, min(begin + 64, ROWS))
        value[rows, :] = band_total(bands, rows)
    stores = [pltpu.make_async_copy(value, out.at[i], sems.at[i]) for i in range(BANDS)]
    for store in stores:
        store.start()
    for store in stores:
        store.wait()


def row_call(bands):
    return pl.pallas_call(
        row_body,
        out_shape=pltpu.HBM((BANDS, ROWS, 128), BF16),
        in_specs=[VMEM],
        out_specs=ANY,
        scratch_shapes=[pltpu.VMEM((ROWS, 128), BF16), pltpu.SemaphoreType.DMA((BANDS,))],
        compiler_params=pltpu.CompilerParams(vmem_limit_bytes=4 << 20),
        cost_estimate=pl.CostEstimate(flops=500_000, bytes_accessed=1_200_000, transcendentals=0),
        name="row_sum",
    )(bands)


def unpack_half(source, joined):
    for index in range(3):
        for part in range(2):
            for panel in range(3):
                start = ((index * 2 + part) * 3 + panel) * HALF
                joined[index, :, part * NB + panel * 128 : part * NB + (panel + 1) * 128] = source[
                    start : start + HALF, :
                ]


def direct(index, role, half, joined, table, magnon):
    rows = pl.ds(pl.multiple_of(half * HALF, HALF), HALF)
    value = jnp.dot(joined[index], table[role], preferred_element_type=F32)
    magnon[index, rows, :] = value.astype(BF16).astype(F32)


def transposed(index, role, half, joined, table):
    value = None
    for part in range(2):
        turned = joined[index, :, part * NB : (part + 1) * NB].astype(F32).T.astype(BF16)
        these = pl.ds(pl.multiple_of(part * NB + half * HALF, HALF), HALF)
        term = jnp.dot(turned, table[role, these, :], preferred_element_type=F32)
        value = term if value is None else value + term
    return value


def tables_body(offsets, free, out, plain, table, sems):
    roles = offset_roles(offsets)
    loads = [
        pltpu.make_async_copy(free.at[k], plain.at[role], sems.at[role])
        for role, k in enumerate(roles)
    ]
    for load in loads:
        load.start()
    stores = []
    for role in range(4):
        loads[role].wait()
        fr = plain[role, 0]
        fi = plain[role, 1]
        table[role, :NB, :NB] = fr
        table[role, :NB, NB:] = fi
        table[role, NB:, :NB] = -fi
        table[role, NB:, NB:] = fr
        store = pltpu.make_async_copy(table.at[role], out.at[role], sems.at[4 + role])
        store.start()
        stores.append(store)
    for store in stores:
        store.wait()


def tables_call(offsets, free):
    size = 2 * NB
    return pl.pallas_call(
        tables_body,
        out_shape=pltpu.HBM((4, size, size), BF16),
        in_specs=[SMEM, ANY],
        out_specs=ANY,
        scratch_shapes=[
            pltpu.VMEM((4, 2, NB, NB), BF16),
            pltpu.VMEM((4, size, size), BF16),
            pltpu.SemaphoreType.DMA((8,)),
        ],
        compiler_params=pltpu.CompilerParams(vmem_limit_bytes=9 << 20),
        cost_estimate=pl.CostEstimate(flops=0, bytes_accessed=7_000_000, transcendentals=0),
        name="tables",
    )(offsets, in_hbm(free))


def start_body(
    place, offsets, mine, free, own, mate,
    slots, magnon, sums, table, joined, sems,
):
    core = place[0]
    roles = offset_roles(offsets)
    tables = [
        pltpu.make_async_copy(free.at[role], table.at[role], sems.at[role]) for role in range(4)
    ]
    loads = [
        pltpu.make_async_copy(own, slots.at[pl.ds(4, 4)], sems.at[4]),
        pltpu.make_async_copy(mate, slots.at[pl.ds(8 - 8 * core, 4)], sems.at[5]),
    ]
    for load in tables + loads:
        load.start()
    unpack_half(mine, joined)
    for role in range(4):
        tables[role].wait()
        if role == 0:
            direct(0, 0, core, joined, table, magnon)
        elif role == 1:
            sums[0] = transposed(0, 1, core, joined, table)
        else:

            @pl.when(offsets[roles[role]] > 0)
            def _():
                direct(role - 1, role, core, joined, table, magnon)

            @pl.when(offsets[roles[role]] < 0)
            def _():
                sums[role - 1] = transposed(role - 1, role, core, joined, table)

    for load in loads:
        load.wait()


def start_call(place, offsets, mine, free, own, mate):
    size = 2 * NB
    return pl.pallas_call(
        start_body,
        out_shape=(
            jax.ShapeDtypeStruct((12, 2, NB, NB), BF16),
            jax.ShapeDtypeStruct((3, NB, size), F32),
            jax.ShapeDtypeStruct((3, NB, size), F32),
            jax.ShapeDtypeStruct((4, size, size), BF16),
        ),
        in_specs=[SMEM, SMEM, VMEM] + [ANY] * 3,
        out_specs=(VMEM,) * 4,
        scratch_shapes=[
            pltpu.VMEM((3, HALF, size), BF16),
            pltpu.SemaphoreType.DMA((6,)),
        ],
        compiler_params=pltpu.CompilerParams(vmem_limit_bytes=10 << 20),
        cost_estimate=pl.CostEstimate(
            flops=1_000_000_000, bytes_accessed=10_000_000, transcendentals=0
        ),
        name="final_start",
    )(place, offsets, mine, *(in_hbm(x) for x in (free, own, mate)))


def final_body(
    place, offsets, other, near, far, early, late, slots_in, magnon_in, sums, table,
    out, slots, magnon, joined, result, sems,
):
    core = place[0]
    loads = [
        pltpu.make_async_copy(near, slots.at[pl.ds(2 + 6 * core, 2)], sems.at[5]),
        pltpu.make_async_copy(far, slots.at[pl.ds(10 * core, 2)], sems.at[6]),
    ]
    for load in loads:
        load.start()
    unpack_half(other, joined)
    roles = offset_roles(offsets)
    _, _, first, last = roles
    half = 1 - core
    direct(0, 0, half, joined, table, magnon)
    total = sums[0] + transposed(0, 1, half, joined, table)
    magnon[0] += total.astype(BF16).astype(F32)
    for role in (2, 3):

        @pl.when(offsets[roles[role]] > 0)
        def _():
            direct(role - 1, role, half, joined, table, magnon)

        @pl.when(offsets[roles[role]] < 0)
        def _():
            total = sums[role - 1] + transposed(role - 1, role, half, joined, table)
            magnon[role - 1] = total.astype(BF16).astype(F32)

    for load in loads:
        load.wait()
    reach = spans(offsets, first, last)
    stores = []
    for item, energy in enumerate((2 - 2 * core, 3 - 2 * core, 2 * core, 2 * core + 1)):
        born = early if item < 2 else late

        @pl.loop(0, NB // 32)
        def _(block):
            rows = pl.ds(pl.multiple_of(block * 32, 32), 32)
            begin = pl.ds(pl.multiple_of((item % 2) * NB + block * 32, 32), 32)
            real = born[begin, :NB].astype(F32)
            imag = born[begin, NB:].astype(F32)
            for index in range(3):
                down = energy + 4 - reach[index]
                up = energy + 4 + reach[index]
                sr = slots[down, 0, rows, :].astype(F32) + slots[up, 0, rows, :].astype(F32)
                si = slots[down, 1, rows, :].astype(F32) + slots[up, 1, rows, :].astype(F32)
                mr = magnon[index, rows, :NB]
                mi = magnon[index, rows, NB:]
                real += mr * sr - mi * si
                imag += mr * si + mi * sr
            result[item, 0, rows, :] = real.astype(BF16)
            result[item, 1, rows, :] = imag.astype(BF16)

        store = pltpu.make_async_copy(result.at[item], out.at[energy, 0], sems.at[item])
        store.start()
        stores.append(store)
    for store in stores:
        store.wait()


def final_call(place, offsets, other, near, far, early, late, slots, magnon, sums, table):
    size = 2 * NB
    return pl.pallas_call(
        final_body,
        out_shape=(
            jax.ShapeDtypeStruct((4, 1, 2, NB, NB), BF16),
            jax.ShapeDtypeStruct(slots.shape, BF16),
            jax.ShapeDtypeStruct(magnon.shape, F32),
        ),
        in_specs=[SMEM, SMEM, VMEM, ANY, ANY] + [VMEM] * 6,
        out_specs=(ANY, VMEM, VMEM),
        input_output_aliases={7: 1, 8: 2},
        scratch_shapes=[
            pltpu.VMEM((3, HALF, size), BF16),
            pltpu.VMEM((4, 2, NB, NB), BF16),
            pltpu.SemaphoreType.DMA((7,)),
        ],
        compiler_params=pltpu.CompilerParams(vmem_limit_bytes=12 << 20),
        cost_estimate=pl.CostEstimate(
            flops=1_000_000_000, bytes_accessed=18_000_000, transcendentals=0
        ),
        name="final",
    )(place, offsets, other, in_hbm(near), in_hbm(far), early, late, slots, magnon, sums, table)[0]


def per_device(green_blocks, offsets, occupation, coupling, vertex, magnon_free):
    count = lax.axis_size(ENERGY)
    core = lax.axis_index("core").astype(jnp.int32)
    place = core[None]
    own = green_blocks.reshape(4, 2, NB, NB)
    across = [(i, i + 1) for i in range(1, count - 1, 2)]
    across += [(target, source) for source, target in across]
    along = [(i, i + 2) for i in range(1, count - 2, 2)]
    along += [(i + 1, i - 1) for i in range(1, count - 2, 2)]
    to_same, to_cross = edge_call(place, own)
    cross = lax.ppermute(to_cross, ENERGY, across)
    same = lax.ppermute(to_same, ENERGY, along)
    mate = lax.ppermute(own, "core", SWAP)
    inner = cut_call(place, own, 2, -2)
    far = lax.ppermute(inner, ENERGY, across)
    tables = tables_call(offsets, magnon_free)
    chip, turned, partial = prepare_call(place, offsets, own, mate)
    pair = polar_call(place, offsets, same, cross, chip, turned, partial)
    swapped = lax.ppermute(same, "core", SWAP)
    near = near_call(place, swapped, cross)
    bands = lax.all_to_all(pair.reshape(BANDS, ROWS, 128), PLANE, 0, 0, tiled=True)
    early = born_call(place, offsets, occupation, coupling, (own, mate, near), vertex)
    copies = plane_call(bands)
    bands = lax.all_to_all(copies, ROW, 0, 0, tiled=True)
    copies = row_call(bands)
    mine = lax.all_to_all(copies, PLANE, 0, 0, tiled=True).reshape(FLAT, 128)
    late = born_call(
        place, offsets, occupation, coupling, (own, mate, near, far), vertex
    )
    other = lax.ppermute(mine, "core", SWAP)
    held = start_call(place, offsets, mine, tables, own, mate)
    return final_call(place, offsets, other, near, far, early, late, *held)


def solution(mesh):
    fine = Mesh(mesh.devices.reshape(4, 2, 2, 2, 4), ("y", "xh", "core", "xl", "z"))
    blocks = P(ENERGY, LAYER, None, None, None)
    placed = (blocks, P(), P(), P(LAYER, None), P(), P())
    return jax.shard_map(
        per_device, mesh=fine, in_specs=placed, out_specs=blocks, check_vma=False
    )
```

```python
import jax
import jax.numpy as jnp
from jax import lax
from jax.experimental import pallas as pl
from jax.experimental.pallas import tpu as pltpu
from jax.sharding import Mesh
from jax.sharding import PartitionSpec as P


NB = 384
HALF = NB // 2
BANDS = 16
ROWS = 18 * HALF // BANDS
FLAT = BANDS * ROWS
F32 = jnp.float32
BF16 = jnp.bfloat16
SWAP = [(0, 1), (1, 0)]
PLANE = ("y", "z")
ROW = ("xh", "xl")
ENERGY = ("y", "xh", "core")
LAYER = ("xl", "z")
ANY = pl.BlockSpec(memory_space=pl.ANY)
SMEM = pl.BlockSpec(memory_space=pltpu.SMEM)
VMEM = pl.BlockSpec(memory_space=pltpu.VMEM)


def in_hbm(array):
    return pltpu.with_memory_space_constraint(array, pltpu.HBM)


def in_vmem(array):
    return pltpu.with_memory_space_constraint(array, pltpu.VMEM)


def first_index(offsets, value):
    return jnp.where(
        offsets[0] == value, 0, jnp.where(offsets[1] == value, 1, jnp.where(offsets[2] == value, 2, 3))
    )


def offset_roles(offsets):
    top = first_index(offsets, 4)
    bottom = first_index(offsets, -4)
    low = jnp.minimum(top, bottom)
    high = jnp.maximum(top, bottom)
    first = jnp.where(low != 0, 0, jnp.where(high != 1, 1, 2))
    last = jnp.where(high != 3, 3, jnp.where(low != 2, 2, 1))
    return top, bottom, first, last


def spans(offsets, first, last):
    return (jnp.int32(4), jnp.abs(offsets[first]), jnp.abs(offsets[last]))


def cut_body(place, base, sign, own, out, sem):
    copy = pltpu.make_async_copy(own.at[pl.ds(base + sign * place[0], 2)], out, sem)
    copy.start()
    copy.wait()


def cut_call(place, own, base, sign):
    return pl.pallas_call(
        lambda place, own, out, sem: cut_body(place, base, sign, own, out, sem),
        out_shape=jax.ShapeDtypeStruct((2, 2, NB, NB), BF16),
        in_specs=[SMEM, ANY],
        out_specs=VMEM,
        scratch_shapes=[pltpu.SemaphoreType.DMA],
        compiler_params=pltpu.CompilerParams(vmem_limit_bytes=4 << 20),
        cost_estimate=pl.CostEstimate(flops=0, bytes_accessed=2_400_000, transcendentals=0),
    )(place, in_hbm(own))


def edge_body(place, own, same, cross, whole, sems):
    core = place[0]

    @pl.when(core == 1)
    def _():
        copies = [
            pltpu.make_async_copy(own.at[pl.ds(2, 2), :, pl.ds(HALF, HALF), :], same, sems.at[0]),
            pltpu.make_async_copy(own.at[pl.ds(2, 2), :, pl.ds(0, HALF), :], cross, sems.at[1]),
        ]
        for copy in copies:
            copy.start()
        for copy in copies:
            copy.wait()

    @pl.when(core == 0)
    def _():
        copy = pltpu.make_async_copy(own.at[pl.ds(0, 2)], whole, sems.at[0])
        copy.start()
        copy.wait()
        for item in range(2):
            for part in range(2):
                value = whole[item, part].astype(F32).T.astype(BF16)
                same[item, part] = value[:HALF]
                cross[item, part] = value[HALF:]


def edge_call(place, own):
    half = jax.ShapeDtypeStruct((2, 2, HALF, NB), BF16)
    return pl.pallas_call(
        edge_body,
        out_shape=(half, half),
        in_specs=[SMEM, ANY],
        out_specs=(VMEM, VMEM),
        scratch_shapes=[pltpu.VMEM((2, 2, NB, NB), BF16), pltpu.SemaphoreType.DMA((2,))],
        compiler_params=pltpu.CompilerParams(vmem_limit_bytes=6 << 20),
        cost_estimate=pl.CostEstimate(flops=0, bytes_accessed=2_400_000, transcendentals=0),
        name="edge",
    )(place, in_hbm(own))


def prepare_body(place, offsets, own, mate, chip, turned, partial, sems):
    core = place[0]
    copies = [
        pltpu.make_async_copy(own, chip.at[pl.ds(4 * core, 4)], sems.at[0]),
        pltpu.make_async_copy(mate, chip.at[pl.ds(4 - 4 * core, 4)], sems.at[1]),
    ]
    for copy in copies:
        copy.start()
    for copy in copies:
        copy.wait()

    @pl.loop(2, 16)
    def _(step):
        turned[step // 2, step % 2] = chip[step // 2, step % 2].astype(F32).T

    _, _, first, last = offset_roles(offsets)
    for index, span in enumerate(spans(offsets, first, last)):

        @pl.loop(0, HALF // 32)
        def _(block):
            rows = pl.ds(pl.multiple_of(block * 32, 32), 32)
            there = pl.ds(pl.multiple_of(core * HALF + block * 32, 32), 32)

            def step(s, carry):
                real, imag = carry
                ar = chip[s, 0, there, :].astype(F32)
                ai = chip[s, 1, there, :].astype(F32)
                br = turned[s + span, 0, there, :]
                bi = turned[s + span, 1, there, :]
                return real + (ar * br - ai * bi), imag + (ar * bi + ai * br)

            zero = jnp.zeros((32, NB), F32)
            real, imag = lax.fori_loop(0, 8 - span, step, (zero, zero))
            partial[index, 0, rows, :] = real
            partial[index, 1, rows, :] = imag


def prepare_call(place, offsets, own, mate):
    return pl.pallas_call(
        prepare_body,
        out_shape=(
            jax.ShapeDtypeStruct((8, 2, NB, NB), BF16),
            jax.ShapeDtypeStruct((8, 2, NB, NB), F32),
            jax.ShapeDtypeStruct((3, 2, HALF, NB), F32),
        ),
        in_specs=[SMEM, SMEM, ANY, ANY],
        out_specs=(VMEM, VMEM, VMEM),
        scratch_shapes=[pltpu.SemaphoreType.DMA((2,))],
        compiler_params=pltpu.CompilerParams(vmem_limit_bytes=4 << 20),
        cost_estimate=pl.CostEstimate(flops=20_000_000, bytes_accessed=9_000_000, transcendentals=0),
        name="prepare",
    )(place, offsets, own, mate)


def polar_body(place, offsets, same, cross, chip, turned, partial, out, flat, sems):
    core = place[0]

    def run(edges):
        _, _, first, last = offset_roles(offsets)
        for index, span in enumerate(spans(offsets, first, last)):

            @pl.loop(0, HALF // 32)
            def _(block):
                rows = pl.ds(pl.multiple_of(block * 32, 32), 32)
                there = pl.ds(pl.multiple_of(core * HALF + block * 32, 32), 32)

                def multiply(carry, ar, ai, br, bi):
                    real, imag = carry
                    return real + (ar * br - ai * bi), imag + (ar * bi + ai * br)

                def before(j, carry):
                    ar = edges[0][1 - j, 0, rows, :].astype(F32)
                    ai = edges[0][1 - j, 1, rows, :].astype(F32)
                    if index > 0:
                        keep = jnp.where(span > 2 + j, 1.0, 0.0)
                        ar, ai = ar * keep, ai * keep
                    at = jnp.maximum(span - 1 - j, 1)
                    return multiply(carry, ar, ai, turned[at, 0, there, :], turned[at, 1, there, :])

                def after(j, carry):
                    at = jnp.minimum(8 - span + j, 7)
                    ar = chip[at, 0, there, :].astype(F32)
                    ai = chip[at, 1, there, :].astype(F32)
                    if index > 0 and j > 0:
                        keep = jnp.where(span > j, 1.0, 0.0)
                        ar, ai = ar * keep, ai * keep
                    return multiply(
                        carry,
                        ar,
                        ai,
                        edges[1][j, 0, rows, :].astype(F32),
                        edges[1][j, 1, rows, :].astype(F32),
                    )

                pair = (partial[index, 0, rows, :], partial[index, 1, rows, :])
                for j in range(2):
                    pair = before(j, pair)
                for j in range(2):
                    pair = after(j, pair)
                for part, value in enumerate(pair):
                    for panel in range(3):
                        start = ((index * 2 + part) * 3 + panel) * HALF
                        flat[pl.ds(pl.multiple_of(start + block * 32, 32), 32), :] = value[
                            :, panel * 128 : (panel + 1) * 128
                        ].astype(BF16)

            done = pl.ds(index * 6 * HALF, 6 * HALF)
            store = pltpu.make_async_copy(flat.at[done], out.at[done], sems.at[index])
            store.start()

    @pl.when(core == 0)
    def _():
        run((cross, same))

    @pl.when(core == 1)
    def _():
        run((same, cross))

    for index in range(3):
        done = pl.ds(index * 6 * HALF, 6 * HALF)
        pltpu.make_async_copy(flat.at[done], out.at[done], sems.at[index]).wait()


def polar_call(place, offsets, same, cross, chip, turned, partial):
    return pl.pallas_call(
        polar_body,
        out_shape=pltpu.HBM((FLAT, 128), BF16),
        in_specs=[SMEM, SMEM, VMEM, VMEM, VMEM, VMEM, VMEM],
        out_specs=ANY,
        scratch_shapes=[
            pltpu.VMEM((FLAT, 128), BF16),
            pltpu.SemaphoreType.DMA((3,)),
        ],
        compiler_params=pltpu.CompilerParams(vmem_limit_bytes=6 << 20),
        cost_estimate=pl.CostEstimate(flops=20_000_000, bytes_accessed=9_000_000, transcendentals=0),
        name="polar",
    )(place, offsets, in_vmem(same), in_vmem(cross), chip, turned, partial)


def near_body(place, swapped, cross, out, sems):
    core = place[0]
    copies = [
        pltpu.make_async_copy(cross, out.at[:, :, pl.ds(core * HALF, HALF), :], sems.at[0]),
        pltpu.make_async_copy(
            swapped, out.at[:, :, pl.ds(HALF - core * HALF, HALF), :], sems.at[1]
        ),
    ]
    for copy in copies:
        copy.start()
    for copy in copies:
        copy.wait()

    @pl.when(core == 1)
    def _():
        for item in range(2):
            for part in range(2):
                out[item, part] = out[item, part].astype(F32).T.astype(BF16)


def near_call(place, swapped, cross):
    return pl.pallas_call(
        near_body,
        out_shape=jax.ShapeDtypeStruct((2, 2, NB, NB), BF16),
        in_specs=[SMEM, ANY, ANY],
        out_specs=VMEM,
        scratch_shapes=[pltpu.SemaphoreType.DMA((2,))],
        compiler_params=pltpu.CompilerParams(vmem_limit_bytes=4 << 20),
        cost_estimate=pl.CostEstimate(flops=0, bytes_accessed=2_400_000, transcendentals=0),
        name="near_join",
    )(place, swapped, in_hbm(cross))


def born_body(early, *refs):
    refs = list(refs)
    place, offsets, occupation, coupling, own, mate, near = refs[:7]
    refs = refs[7:]
    far = None if early else refs.pop(0)
    vertex, out, chosen, lows, highs, mixed, wide, stack, side, total, rounded, sems = refs
    core = place[0]
    energy = 2 * (1 - core) if early else 2 * core

    def fetch(slot, target, sem):
        sources = [(own, 4, 4), (mate, 8 - 8 * core, 4), (near, 2 + 6 * core, 2)]
        if far is not None:
            sources.append((far, 10 * core, 2))
        for source, low, size in sources:

            @pl.when((slot >= low) & (slot < low + size))
            def _():
                pltpu.make_async_copy(source.at[slot - low], target, sem).start()

    for k in range(4):
        pltpu.make_async_copy(vertex.at[coupling[0, k]], chosen.at[k], sems.at[k, 4]).start()
        for item in range(2):
            at = energy + 4 + item
            fetch(at - offsets[k], lows.at[k, item], sems.at[k, 2 * item])
            fetch(at + offsets[k], highs.at[k, item], sems.at[k, 2 * item + 1])

    total[...] = jnp.zeros_like(total)

    @pl.loop(0, 4)
    def _(k):
        pltpu.make_async_copy(vertex.at[0], chosen.at[k], sems.at[k, 4]).wait()
        vr = chosen[k, 0]
        vi = chosen[k, 1]
        wide[:NB, :NB] = vr
        wide[:NB, NB:] = -vi
        wide[NB:, :NB] = vi
        wide[NB:, NB:] = vr
        side[:NB, :NB] = vr
        side[:NB, NB:] = vi
        side[NB:, :NB] = -vi
        side[NB:, NB:] = vr
        weight = occupation[k]
        for item in range(2):
            pltpu.make_async_copy(own.at[0], lows.at[k, item], sems.at[k, 2 * item]).wait()
            pltpu.make_async_copy(own.at[0], highs.at[k, item], sems.at[k, 2 * item + 1]).wait()
        for item in range(2):
            for part in range(2):
                low = lows[k, item, part].astype(F32)
                high = highs[k, item, part].astype(F32)
                value = weight * low + (weight + 1.0) * high
                mixed[part * NB : (part + 1) * NB, item * NB : (item + 1) * NB] = value.astype(BF16)
        for piece in range(2):
            begin = piece * 384
            part, row = begin // NB, begin % NB
            half = jnp.dot(
                wide[begin : begin + 384, :], mixed[...], preferred_element_type=F32
            ).astype(BF16)
            for item in range(2):
                stack[item * NB + row : item * NB + row + 384, part * NB : (part + 1) * NB] = half[
                    :, item * NB : (item + 1) * NB
                ]
        for piece in range(2):
            rows = slice(piece * 384, (piece + 1) * 384)
            term = lax.dot_general(
                stack[rows, :], side[...], (((1,), (1,)), ((), ())), preferred_element_type=F32
            )
            total[rows, :] += term

    if early:
        rounded[...] = total[...].astype(BF16)
        store = pltpu.make_async_copy(rounded, out, sems.at[0, 0])
        store.start()
        store.wait()
    else:
        out[...] = total[...].astype(BF16)


def born_call(place, offsets, occupation, coupling, arrays, vertex):
    early = len(arrays) == 3
    size = 2 * NB
    held = (*map(in_hbm, arrays[:2]), *arrays[2:])
    shape = (size, size)
    return pl.pallas_call(
        lambda *refs: born_body(early, *refs),
        out_shape=pltpu.HBM(shape, BF16) if early else jax.ShapeDtypeStruct(shape, BF16),
        in_specs=[SMEM] * 4 + [ANY] * (len(held) + 1),
        out_specs=ANY if early else VMEM,
        scratch_shapes=[
            pltpu.VMEM((4, 2, NB, NB), BF16),
            pltpu.VMEM((4, 2, 2, NB, NB), BF16),
            pltpu.VMEM((4, 2, 2, NB, NB), BF16),
            pltpu.VMEM((size, size), BF16),
            pltpu.VMEM((size, size), BF16),
            pltpu.VMEM((size, size), BF16),
            pltpu.VMEM((size, size), BF16),
            pltpu.VMEM((size, size), F32),
            pltpu.VMEM((size, size), BF16),
            pltpu.SemaphoreType.DMA((4, 5)),
        ],
        compiler_params=pltpu.CompilerParams(vmem_limit_bytes=22 << 20),
        cost_estimate=pl.CostEstimate(
            flops=16 * size**3, bytes_accessed=12_000_000, transcendentals=0
        ),
        name="born_early" if early else "born_late",
    )(place, offsets, occupation, coupling, *held, in_hbm(vertex))


def band_total(bands, rows):
    total = bands[0, rows, :].astype(F32)
    for i in range(1, bands.shape[0]):
        total += bands[i, rows, :].astype(F32)
    return total.astype(BF16)


def plane_body(bands, out):
    for begin in range(0, ROWS, 64):
        rows = slice(begin, min(begin + 64, ROWS))
        value = band_total(bands, rows)
        for i in range(out.shape[0]):
            out[i, rows, :] = value


def plane_call(bands):
    return pl.pallas_call(
        plane_body,
        out_shape=jax.ShapeDtypeStruct((4, ROWS, 128), BF16),
        in_specs=[VMEM],
        out_specs=VMEM,
        compiler_params=pltpu.CompilerParams(vmem_limit_bytes=4 << 20),
        cost_estimate=pl.CostEstimate(flops=500_000, bytes_accessed=1_200_000, transcendentals=0),
        name="plane_sum",
    )(bands)


def row_body(bands, out, value, sems):
    stores = []
    for piece, (begin, end) in enumerate(((0, 128), (128, ROWS))):
        rows = slice(begin, end)
        value[rows, :] = band_total(bands, rows)
        for i in range(BANDS):
            store = pltpu.make_async_copy(value.at[rows], out.at[i, rows], sems.at[piece, i])
            store.start()
            stores.append(store)
    for store in stores:
        store.wait()


def row_call(bands):
    return pl.pallas_call(
        row_body,
        out_shape=pltpu.HBM((BANDS, ROWS, 128), BF16),
        in_specs=[VMEM],
        out_specs=ANY,
        scratch_shapes=[pltpu.VMEM((ROWS, 128), BF16), pltpu.SemaphoreType.DMA((2, BANDS))],
        compiler_params=pltpu.CompilerParams(vmem_limit_bytes=4 << 20),
        cost_estimate=pl.CostEstimate(flops=500_000, bytes_accessed=1_200_000, transcendentals=0),
        name="row_sum",
    )(bands)


def unpack_half(source, joined):
    for index in range(3):
        for part in range(2):
            for panel in range(3):
                start = ((index * 2 + part) * 3 + panel) * HALF
                joined[index, :, part * NB + panel * 128 : part * NB + (panel + 1) * 128] = source[
                    start : start + HALF, :
                ]


def direct(index, role, half, joined, table, magnon):
    rows = pl.ds(pl.multiple_of(half * HALF, HALF), HALF)
    value = jnp.dot(joined[index], table[role], preferred_element_type=F32)
    magnon[index, rows, :] = value.astype(BF16).astype(F32)


def transposed(index, role, half, joined, table):
    value = None
    for part in range(2):
        turned = joined[index, :, part * NB : (part + 1) * NB].astype(F32).T.astype(BF16)
        these = pl.ds(pl.multiple_of(part * NB + half * HALF, HALF), HALF)
        term = jnp.dot(turned, table[role, these, :], preferred_element_type=F32)
        value = term if value is None else value + term
    return value


def tables_body(offsets, free, out, plain, table, sems):
    roles = offset_roles(offsets)
    loads = [
        pltpu.make_async_copy(free.at[k], plain.at[role], sems.at[role])
        for role, k in enumerate(roles)
    ]
    for load in loads:
        load.start()
    stores = []
    for role in range(4):
        loads[role].wait()
        fr = plain[role, 0]
        fi = plain[role, 1]
        table[role, :NB, :NB] = fr
        table[role, :NB, NB:] = fi
        table[role, NB:, :NB] = -fi
        table[role, NB:, NB:] = fr
        store = pltpu.make_async_copy(table.at[role], out.at[role], sems.at[4 + role])
        store.start()
        stores.append(store)
    for store in stores:
        store.wait()


def tables_call(offsets, free):
    size = 2 * NB
    return pl.pallas_call(
        tables_body,
        out_shape=pltpu.HBM((4, size, size), BF16),
        in_specs=[SMEM, ANY],
        out_specs=ANY,
        scratch_shapes=[
            pltpu.VMEM((4, 2, NB, NB), BF16),
            pltpu.VMEM((4, size, size), BF16),
            pltpu.SemaphoreType.DMA((8,)),
        ],
        compiler_params=pltpu.CompilerParams(vmem_limit_bytes=9 << 20),
        cost_estimate=pl.CostEstimate(flops=0, bytes_accessed=7_000_000, transcendentals=0),
        name="tables",
    )(offsets, in_hbm(free))


def start_body(
    place, offsets, mine, free, own, mate,
    slots, magnon, sums, table, joined, sems,
):
    core = place[0]
    roles = offset_roles(offsets)
    tables = [
        pltpu.make_async_copy(free.at[role], table.at[role], sems.at[role]) for role in range(4)
    ]
    loads = [
        pltpu.make_async_copy(own, slots.at[pl.ds(4, 4)], sems.at[4]),
        pltpu.make_async_copy(mate, slots.at[pl.ds(8 - 8 * core, 4)], sems.at[5]),
    ]
    for load in tables + loads:
        load.start()
    unpack_half(mine, joined)
    for role in range(4):
        tables[role].wait()
        if role == 0:
            direct(0, 0, core, joined, table, magnon)
        elif role == 1:
            sums[0] = transposed(0, 1, core, joined, table)
        else:

            @pl.when(offsets[roles[role]] > 0)
            def _():
                direct(role - 1, role, core, joined, table, magnon)

            @pl.when(offsets[roles[role]] < 0)
            def _():
                sums[role - 1] = transposed(role - 1, role, core, joined, table)

    for load in loads:
        load.wait()


def start_call(place, offsets, mine, free, own, mate):
    size = 2 * NB
    return pl.pallas_call(
        start_body,
        out_shape=(
            jax.ShapeDtypeStruct((12, 2, NB, NB), BF16),
            jax.ShapeDtypeStruct((3, NB, size), F32),
            jax.ShapeDtypeStruct((3, NB, size), F32),
            jax.ShapeDtypeStruct((4, size, size), BF16),
        ),
        in_specs=[SMEM, SMEM, VMEM] + [ANY] * 3,
        out_specs=(VMEM,) * 4,
        scratch_shapes=[
            pltpu.VMEM((3, HALF, size), BF16),
            pltpu.SemaphoreType.DMA((6,)),
        ],
        compiler_params=pltpu.CompilerParams(vmem_limit_bytes=10 << 20),
        cost_estimate=pl.CostEstimate(
            flops=1_000_000_000, bytes_accessed=10_000_000, transcendentals=0
        ),
        name="final_start",
    )(place, offsets, mine, *(in_hbm(x) for x in (free, own, mate)))


def final_body(
    place, offsets, other, near, far, early, late, slots_in, magnon_in, sums, table,
    out, slots, magnon, joined, result, sems,
):
    core = place[0]
    loads = [
        pltpu.make_async_copy(near, slots.at[pl.ds(2 + 6 * core, 2)], sems.at[5]),
        pltpu.make_async_copy(far, slots.at[pl.ds(10 * core, 2)], sems.at[6]),
    ]
    for load in loads:
        load.start()
    unpack_half(other, joined)
    roles = offset_roles(offsets)
    _, _, first, last = roles
    half = 1 - core
    direct(0, 0, half, joined, table, magnon)
    total = sums[0] + transposed(0, 1, half, joined, table)
    magnon[0] += total.astype(BF16).astype(F32)
    for role in (2, 3):

        @pl.when(offsets[roles[role]] > 0)
        def _():
            direct(role - 1, role, half, joined, table, magnon)

        @pl.when(offsets[roles[role]] < 0)
        def _():
            total = sums[role - 1] + transposed(role - 1, role, half, joined, table)
            magnon[role - 1] = total.astype(BF16).astype(F32)

    for load in loads:
        load.wait()
    reach = spans(offsets, first, last)
    stores = []
    for item, energy in enumerate((2 - 2 * core, 3 - 2 * core, 2 * core, 2 * core + 1)):
        born = early if item < 2 else late

        @pl.loop(0, NB // 32)
        def _(block):
            rows = pl.ds(pl.multiple_of(block * 32, 32), 32)
            begin = pl.ds(pl.multiple_of((item % 2) * NB + block * 32, 32), 32)
            real = born[begin, :NB].astype(F32)
            imag = born[begin, NB:].astype(F32)
            for index in range(3):
                down = energy + 4 - reach[index]
                up = energy + 4 + reach[index]
                sr = slots[down, 0, rows, :].astype(F32) + slots[up, 0, rows, :].astype(F32)
                si = slots[down, 1, rows, :].astype(F32) + slots[up, 1, rows, :].astype(F32)
                mr = magnon[index, rows, :NB]
                mi = magnon[index, rows, NB:]
                real += mr * sr - mi * si
                imag += mr * si + mi * sr
            result[item, 0, rows, :] = real.astype(BF16)
            result[item, 1, rows, :] = imag.astype(BF16)

        store = pltpu.make_async_copy(result.at[item], out.at[energy, 0], sems.at[item])
        store.start()
        stores.append(store)
    for store in stores:
        store.wait()


def final_call(place, offsets, other, near, far, early, late, slots, magnon, sums, table):
    size = 2 * NB
    return pl.pallas_call(
        final_body,
        out_shape=(
            jax.ShapeDtypeStruct((4, 1, 2, NB, NB), BF16),
            jax.ShapeDtypeStruct(slots.shape, BF16),
            jax.ShapeDtypeStruct(magnon.shape, F32),
        ),
        in_specs=[SMEM, SMEM, VMEM, ANY, ANY] + [VMEM] * 6,
        out_specs=(ANY, VMEM, VMEM),
        input_output_aliases={7: 1, 8: 2},
        scratch_shapes=[
            pltpu.VMEM((3, HALF, size), BF16),
            pltpu.VMEM((4, 2, NB, NB), BF16),
            pltpu.SemaphoreType.DMA((7,)),
        ],
        compiler_params=pltpu.CompilerParams(vmem_limit_bytes=12 << 20),
        cost_estimate=pl.CostEstimate(
            flops=1_000_000_000, bytes_accessed=18_000_000, transcendentals=0
        ),
        name="final",
    )(place, offsets, other, in_hbm(near), in_hbm(far), early, late, slots, magnon, sums, table)[0]


def per_device(green_blocks, offsets, occupation, coupling, vertex, magnon_free):
    count = lax.axis_size(ENERGY)
    core = lax.axis_index("core").astype(jnp.int32)
    place = core[None]
    own = green_blocks.reshape(4, 2, NB, NB)
    across = [(i, i + 1) for i in range(1, count - 1, 2)]
    across += [(target, source) for source, target in across]
    along = [(i, i + 2) for i in range(1, count - 2, 2)]
    along += [(i + 1, i - 1) for i in range(1, count - 2, 2)]
    to_same, to_cross = edge_call(place, own)
    cross = lax.ppermute(to_cross, ENERGY, across)
    same = lax.ppermute(to_same, ENERGY, along)
    mate = lax.ppermute(own, "core", SWAP)
    inner = cut_call(place, own, 2, -2)
    far = lax.ppermute(inner, ENERGY, across)
    tables = tables_call(offsets, magnon_free)
    chip, turned, partial = prepare_call(place, offsets, own, mate)
    pair = polar_call(place, offsets, same, cross, chip, turned, partial)
    swapped = lax.ppermute(same, "core", SWAP)
    near = near_call(place, swapped, cross)
    bands = lax.all_to_all(pair.reshape(BANDS, ROWS, 128), PLANE, 0, 0, tiled=True)
    early = born_call(place, offsets, occupation, coupling, (own, mate, near), vertex)
    copies = plane_call(bands)
    bands = lax.all_to_all(copies, ROW, 0, 0, tiled=True)
    copies = row_call(bands)
    mine = lax.all_to_all(copies, PLANE, 0, 0, tiled=True).reshape(FLAT, 128)
    late = born_call(
        place, offsets, occupation, coupling, (own, mate, near, far), vertex
    )
    other = lax.ppermute(mine, "core", SWAP)
    held = start_call(place, offsets, mine, tables, own, mate)
    return final_call(place, offsets, other, near, far, early, late, *held)


def solution(mesh):
    fine = Mesh(mesh.devices.reshape(4, 2, 2, 2, 4), ("y", "xh", "core", "xl", "z"))
    blocks = P(ENERGY, LAYER, None, None, None)
    placed = (blocks, P(), P(), P(LAYER, None), P(), P())
    return jax.shard_map(
        per_device, mesh=fine, in_specs=placed, out_specs=blocks, check_vma=False
    )
```
